32 devices in a mesh: dp: 8 (over y, x, core), mp: 4 (over z).
Axes of the slice: x: 2, y: 2, z: 4, core: 2. Of those that a mesh axis runs over, the one named last changes fastest.
Arguments:
- tokens: bfloat16 [32768, 1024], P('dp', 'mp'), may hold values from -6 to 6
- cotangent: bfloat16 [32768, 1024], P('dp', 'mp'), may hold values from -6 to 6
- norm_gain: float32 [1024], P('mp'), may hold values from 0.5 to 1.5
- ema_delta: float32 [1024, 16], P('mp'), may hold values from -4 to 2
- ema_alpha: float32 [1024, 16], P('mp'), may hold values from -1.5 to 2
- ema_beta: float32 [1024, 16], P('mp'), may hold values from -4 to 4
- ema_eta: float32 [1024, 16], P('mp'), may hold values from -1.5 to 1.5
- ema_omega: float32 [1024], P('mp'), may hold values from -4 to 4
- shared_proj: bfloat16 [1024, 128], replicated, may hold values from -0.1875 to 0.1875
- query_gain: float32 [128], replicated, may hold values from -8 to 8
- query_bias: float32 [128], replicated, may hold values from -4 to 4
- key_gain: float32 [128], replicated, may hold values from -8 to 8
- value_proj: bfloat16 [1024, 2048], P(None, 'mp'), may hold values from -0.1875 to 0.1875
- gate_proj: bfloat16 [1024, 2048], P(None, 'mp'), may hold values from -0.1875 to 0.1875
- mixer_proj: bfloat16 [1024, 1024], P(None, 'mp'), may hold values from -0.1875 to 0.1875
- update_proj: bfloat16 [1024, 1024], P(None, 'mp'), may hold values from -0.1875 to 0.1875
- output_proj: bfloat16 [2048, 1024], P('mp'), may hold values from -0.5 to 0.5
- ffn_gain: float32 [1024], P('mp'), may hold values from 0.5 to 1.5
- up_proj: bfloat16 [1024, 4096], P(None, 'mp'), may hold values from -0.1875 to 0.1875
- down_proj: bfloat16 [4096, 1024], P('mp'), may hold values from -0.09375 to 0.09375
Outputs:
- layer_out: bfloat16 [32768, 1024], P('dp', 'mp')
- token_grad: bfloat16 [32768, 1024], P('dp', 'mp')
- gain_grad: float32 [1024], P('mp')
- delta_grad: float32 [1024, 16], P('mp')
- alpha_grad: float32 [1024, 16], P('mp')
- beta_grad: float32 [1024, 16], P('mp')
- eta_grad: float32 [1024, 16], P('mp')
- omega_grad: float32 [1024], P('mp')
- shared_grad: float32 [1024, 128], replicated
- query_grad: float32 [128], replicated
- bias_grad: float32 [128], replicated
- key_grad: float32 [128], replicated
- value_grad: float32 [1024, 2048], P(None, 'mp')
- gate_grad: float32 [1024, 2048], P(None, 'mp')
- mixer_grad: float32 [1024, 1024], P(None, 'mp')
- update_grad: float32 [1024, 1024], P(None, 'mp')
- output_grad: float32 [2048, 1024], P('mp')
- ffn_grad: float32 [1024], P('mp')
- up_grad: float32 [1024, 4096], P(None, 'mp')
- down_grad: float32 [4096, 1024], P('mp')
The draws below stay inside these ranges and needn't reach their ends.
All inputs are finite; a program needn't handle non-finite values.
Results may differ from the reference program's by a relative error of at most 0.0307.
Values may be sent and summed in bfloat16 or wider, within the bound.
A program may use at most 384 MiB of HBM per device.

```python
import jax
import jax.numpy as jnp
from jax import lax

D = 1024
Z = 128
V = 2048
NDIM = 16
FF = 4096
GROUP = 128
LEN = 2048
TOKENS = 32768


def levels(key, extent, pieces, least, high):
    def one(position, shards_of):
        heights = jax.random.uniform(jax.random.fold_in(jax.random.fold_in(key, 6), position), (shards_of,), jnp.float32, least / len(pieces), high / len(pieces))
        return jnp.repeat(jnp.exp(heights), extent[position] // shards_of).reshape((-1,) + (1,) * (len(extent) - position - 1))

    level = one(*pieces[0])
    for cut in pieces[1:]:
        level = level * one(*cut)
    return level


def noise(key, extent, spread, most, pieces=(), dtype=jnp.bfloat16):
    values = spread * jax.random.normal(key, extent, jnp.float32)
    if pieces:
        values = values * levels(key, extent, pieces, -0.22, 0.18)
    return jnp.clip(values, -most, most).astype(dtype)


def setup_inputs(seed: int = 0) -> dict:
    key_list = jax.random.split(jax.random.key(seed), 21)
    return {
        "tokens": noise(key_list[0], (TOKENS, D), 1.0, 6.0, ((0, 8), (1, 4))),
        "cotangent": noise(key_list[1], (TOKENS, D), 1.0, 6.0, ((0, 8), (1, 4))),
        "norm_gain": jnp.clip(1.0 + 0.1 * jax.random.normal(key_list[2], (D,), jnp.float32), 0.5, 1.5),
        "ema_delta": jnp.clip(-4.0 + 6.0 * jax.random.uniform(key_list[3], (D, NDIM), jnp.float32) ** levels(key_list[3], (D, NDIM), ((0, 4),), -0.2, 0.2), -4.0, 2.0),
        "ema_alpha": jnp.clip(-1.5 + 3.5 * jax.random.uniform(key_list[4], (D, NDIM), jnp.float32) ** levels(key_list[4], (D, NDIM), ((0, 4),), -0.2, 0.2), -1.5, 2.0),
        "ema_beta": noise(key_list[5], (D, NDIM), 1.0, 4.0, ((0, 4),), jnp.float32),
        "ema_eta": noise(key_list[6], (D, NDIM), NDIM ** -0.5, 1.5, ((0, 4),), jnp.float32),
        "ema_omega": noise(key_list[7], (D,), 1.0, 4.0, ((0, 4),), jnp.float32),
        "shared_proj": noise(key_list[8], (D, Z), D ** -0.5, 0.1875),
        "query_gain": noise(key_list[9], (Z,), 2.0, 8.0, (), jnp.float32),
        "query_bias": noise(key_list[10], (Z,), 1.0, 4.0, (), jnp.float32),
        "key_gain": noise(key_list[11], (Z,), 2.0, 8.0, (), jnp.float32),
        "value_proj": noise(key_list[12], (D, V), D ** -0.5, 0.1875, ((1, 4),)),
        "gate_proj": noise(key_list[13], (D, V), D ** -0.5, 0.1875, ((1, 4),)),
        "mixer_proj": noise(key_list[14], (D, D), D ** -0.5, 0.1875, ((1, 4),)),
        "update_proj": noise(key_list[15], (D, D), D ** -0.5, 0.1875, ((1, 4),)),
        "output_proj": noise(key_list[16], (V, D), (V // 16) ** -0.5, 0.5, ((0, 4),)),
        "ffn_gain": jnp.clip(1.0 + 0.1 * jax.random.normal(key_list[17], (D,), jnp.float32), 0.5, 1.5),
        "up_proj": noise(key_list[18], (D, FF), D ** -0.5, 0.1875, ((1, 4),)),
        "down_proj": noise(key_list[19], (FF, D), FF ** -0.5, 0.09375, ((0, 4),)),
    }


@jax.custom_vjp
def reduced_precision(v):
    return lax.optimization_barrier(v.astype(jnp.bfloat16)).astype(jnp.float32)

@jax.custom_vjp
def low_back(v):
    return v

def low_keep(v):
    return (reduced_precision(v), None)

def low_pass(kept, grad):
    return (grad,)

def back_keep(v):
    return (v, None)

def back_low(kept, grad):
    return (reduced_precision(grad),)
reduced_precision.defvjp(low_keep, low_pass)
low_back.defvjp(back_keep, back_low)
EPS = 1e-05

def product(left, right):
    return jnp.dot(left, right, precision=lax.Precision.HIGHEST, preferred_element_type=jnp.float32)

def layer_norm(values, gain):
    mean_row = lax.optimization_barrier(jnp.mean(values, axis=-1, keepdims=True))
    power = lax.optimization_barrier(jnp.mean(values * values, axis=-1, keepdims=True))
    return (values - mean_row) * lax.rsqrt(power - mean_row * mean_row + EPS) * gain

def ema_scan(signal, delta, alpha, beta, eta):
    rate = jax.nn.sigmoid(delta)
    keep = 1.0 - rate * jax.nn.sigmoid(alpha)
    push = rate * beta

    def advance(state, row_now):
        state = keep * state + push * row_now[:, None]
        return (state, lax.optimization_barrier(jnp.sum(eta * state, axis=1)))
    _, result = lax.scan(advance, jnp.zeros(delta.shape, jnp.float32), signal)
    return result

def segment(seg_rows, params):
    norm_gain, ema_delta, ema_alpha, ema_beta, ema_eta, ema_omega, shared_proj, query_gain, query_bias, key_gain, value_proj, gate_proj, mixer_proj, update_proj, output_proj, ffn_gain, up_proj, down_proj = params
    normed = reduced_precision(layer_norm(seg_rows, norm_gain))
    mix_pre = ema_scan(normed, ema_delta, ema_alpha, ema_beta, ema_eta) + ema_omega * normed
    mixed = reduced_precision(jax.nn.silu(mix_pre))
    shared = jax.nn.silu(low_back(product(mixed, shared_proj)))
    query = reduced_precision(shared * query_gain + query_bias)
    keys = reduced_precision(shared * key_gain)
    values = reduced_precision(jax.nn.silu(low_back(product(normed, value_proj))))
    gate = jax.nn.silu(low_back(product(mixed, gate_proj)))
    blocks = LEN // GROUP
    query_blocks = query.reshape(blocks, GROUP, Z)
    key_blocks = keys.reshape(blocks, GROUP, Z)
    value_block_rows = values.reshape(blocks, GROUP, V)
    raw = jnp.einsum('nqz,nkz->nqk', query_blocks, key_blocks, precision=lax.Precision.HIGHEST)
    scores = low_back(raw * Z ** (-0.5))
    place = jnp.arange(GROUP)
    causal = place[:, None] >= place[None, :]
    probabilities = jax.nn.softmax(jnp.where(causal[None], scores, -1e+30), axis=-1)
    attention_result = jnp.einsum('dzc,dcs->dzs', reduced_precision(probabilities), value_block_rows, precision=lax.Precision.HIGHEST)
    attention_result = low_back(attention_result.reshape(LEN, V))
    hidden = reduced_precision(gate * attention_result)
    update = jax.nn.sigmoid(low_back(product(mixed, update_proj)))
    act_value = jax.nn.silu(low_back(product(mixed, mixer_proj) + product(hidden, output_proj)))
    middle = update * act_value + (1.0 - update) * seg_rows
    ffn_in = reduced_precision(layer_norm(middle, ffn_gain))
    upper = reduced_precision(jax.nn.silu(low_back(product(ffn_in, up_proj))))
    return middle + product(upper, down_proj)

def reference(tokens, cotangent, norm_gain, ema_delta, ema_alpha, ema_beta, ema_eta, ema_omega, shared_proj, query_gain, query_bias, key_gain, value_proj, gate_proj, mixer_proj, update_proj, output_proj, ffn_gain, up_proj, down_proj):
    params = tuple((item.astype(jnp.float32) for item in (norm_gain, ema_delta, ema_alpha, ema_beta, ema_eta, ema_omega, shared_proj, query_gain, query_bias, key_gain, value_proj, gate_proj, mixer_proj, update_proj, output_proj, ffn_gain, up_proj, down_proj)))
    segments = tokens.shape[0] // LEN
    inputs = tokens.astype(jnp.float32).reshape(segments, LEN, D)
    grads_in = cotangent.astype(jnp.float32).reshape(segments, LEN, D)

    def per_segment(totals, segment_pair):
        seg_rows, grad_rows = segment_pair
        result, pull = jax.vjp(segment, seg_rows, params)
        row_grad, param_grads = pull(grad_rows)
        return (jax.tree.map(jnp.add, totals, param_grads), (result, row_grad))
    totals, (results, row_grads) = lax.scan(per_segment, jax.tree.map(jnp.zeros_like, params), (inputs, grads_in))
    return (results.reshape(-1, D).astype(jnp.bfloat16), row_grads.reshape(-1, D).astype(jnp.bfloat16), totals[0], totals[1], totals[2], totals[3], totals[4], totals[5], totals[6], totals[7], totals[8], totals[9], totals[10], totals[11], totals[12], totals[13], totals[14], totals[15], totals[16], totals[17])
```

```python
import functools

import jax
import jax.numpy as jnp
from jax import lax
from jax.experimental import pallas as pl
from jax.experimental.pallas import tpu as pltpu
from jax.sharding import PartitionSpec as P

D = 1024
GROUP = 128
LEN = 2048
NDIM = 16
LANES = 128
SUB = D // LANES
EPS = 1e-05
TB = 128


def matmul(left, right):
    return jnp.dot(left, right, preferred_element_type=jnp.float32)


def matmul_tn(left, right):
    return lax.dot_general(
        left, right, (((0,), (0,)), ((), ())), preferred_element_type=jnp.float32
    )


def matmul_nt(left, right):
    return lax.dot_general(
        left, right, (((1,), (1,)), ((), ())), preferred_element_type=jnp.float32
    )


def silu_slope(values):
    logistic = jax.nn.sigmoid(values)
    return logistic * (1.0 + values * (1.0 - logistic))


def to_rows(scratch, value):
    for part in range(SUB):
        scratch[pl.ds(part, TB, stride=SUB), :] = value[:, part * LANES : (part + 1) * LANES]


def from_rows(scratch):
    return jnp.concatenate(
        [scratch[pl.ds(part, TB, stride=SUB), :] for part in range(SUB)], axis=1
    )


def row(scratch, index):
    return scratch[pl.ds(pl.multiple_of(index * SUB, SUB), SUB), :]


def norm_ends_kernel(x_ref, gain_ref, keep_ref, xn_ref, ends_ref, rows):
    x = x_ref[...].astype(jnp.float32)
    mean = jnp.mean(x, axis=1, keepdims=True)
    power = jnp.mean(x * x, axis=1, keepdims=True)
    scale = lax.rsqrt(power - mean * mean + EPS)
    xn = ((x - mean) * scale * gain_ref[...]).astype(jnp.bfloat16)
    xn_ref[...] = xn
    to_rows(rows, xn.astype(jnp.float32))

    @pl.when(pl.program_id(0) == 0)
    def _():
        ends_ref[...] = jnp.zeros_like(ends_ref)

    keep = [keep_ref[j] for j in range(NDIM)]

    def step(t, carry):
        state, slope = carry
        now = row(rows, t)
        slope = tuple(keep[j] * slope[j] + state[j] for j in range(NDIM))
        state = tuple(keep[j] * state[j] + now for j in range(NDIM))
        return (state, slope)

    state = tuple(ends_ref[j] for j in range(NDIM))
    slope = tuple(ends_ref[NDIM + j] for j in range(NDIM))
    state, slope = lax.fori_loop(0, TB, step, (state, slope), unroll=4)
    for j in range(NDIM):
        ends_ref[j] = state[j]
        ends_ref[NDIM + j] = slope[j]


def ema_kernel(xn_ref, keep_ref, weight_ref, omega_ref, start_ref, mix_ref, xp_ref, rows, outs, state_ref):
    xn = xn_ref[...].astype(jnp.float32)
    to_rows(rows, xn)

    @pl.when(pl.program_id(0) == 0)
    def _():
        for j in range(NDIM):
            state_ref[j] = start_ref[j]

    keep = [keep_ref[j] for j in range(NDIM)]

    def step(t, state):
        now = row(rows, t)
        state = tuple(keep[j] * state[j] + now for j in range(NDIM))
        terms = [weight_ref[j] * state[j] for j in range(NDIM)]
        while len(terms) > 1:
            terms = [a + b for a, b in zip(terms[::2], terms[1::2])]
        outs[pl.ds(pl.multiple_of(t * SUB, SUB), SUB), :] = terms[0]
        return state

    state = lax.fori_loop(0, TB, step, tuple(state_ref[j] for j in range(NDIM)), unroll=4)
    for j in range(NDIM):
        state_ref[j] = state[j]
    mix = from_rows(outs) + omega_ref[...] * xn
    mix_ref[...] = mix
    xp_ref[...] = (mix * jax.nn.sigmoid(mix)).astype(jnp.bfloat16)


def adjoint_start_kernel(grad_ref, keep_ref, start_ref, rows):
    to_rows(rows, grad_ref[...])

    @pl.when(pl.program_id(0) == 0)
    def _():
        start_ref[...] = jnp.zeros_like(start_ref)

    keep = [keep_ref[j] for j in range(NDIM)]

    def step(t, state):
        now = row(rows, TB - 1 - t)
        return tuple(keep[j] * state[j] + now for j in range(NDIM))

    state = lax.fori_loop(0, TB, step, tuple(start_ref[j] for j in range(NDIM)), unroll=4)
    for j in range(NDIM):
        start_ref[j] = state[j]


def ema_params_kernel(grad_ref, xn_ref, keep_ref, start_ref, sums_ref, omega_ref, grads, rows, state_ref):
    xn = xn_ref[...].astype(jnp.float32)
    to_rows(rows, xn)
    grad = grad_ref[...]
    to_rows(grads, grad)

    @pl.when(pl.program_id(0) == 0)
    def _():
        sums_ref[...] = jnp.zeros_like(sums_ref)
        omega_ref[...] = jnp.zeros_like(omega_ref)
        state_ref[...] = start_ref[...]

    omega_ref[...] += jnp.sum(grad * xn, axis=0, keepdims=True)
    half = NDIM // 2
    for first in (0, half):
        dims = range(first, first + half)
        keep = [keep_ref[j] for j in dims]

        def step(t, carry):
            state, slope, weight_sum, keep_sum = carry
            now = row(rows, t)
            grad_now = row(grads, t)
            slope = tuple(keep[j] * slope[j] + state[j] for j in range(half))
            state = tuple(keep[j] * state[j] + now for j in range(half))
            weight_sum = tuple(weight_sum[j] + grad_now * state[j] for j in range(half))
            keep_sum = tuple(keep_sum[j] + grad_now * slope[j] for j in range(half))
            return (state, slope, weight_sum, keep_sum)

        carry = (
            tuple(state_ref[j] for j in dims),
            tuple(state_ref[NDIM + j] for j in dims),
            tuple(sums_ref[j] for j in dims),
            tuple(sums_ref[NDIM + j] for j in dims),
        )
        state, slope, weight_sum, keep_sum = lax.fori_loop(0, TB, step, carry, unroll=4)
        for place, j in enumerate(dims):
            state_ref[j] = state[place]
            state_ref[NDIM + j] = slope[place]
            sums_ref[j] = weight_sum[place]
            sums_ref[NDIM + j] = keep_sum[place]


def token_grad_kernel(
    grad_ref, x_ref, normed_ref, direct_ref, gain_ref, omega_ref, keep_ref, weight_ref, start_ref,
    out_ref, gain_sum_ref, rows, outs, state_ref,
):
    grad = grad_ref[...]
    to_rows(rows, grad)

    @pl.when(pl.program_id(0) == 0)
    def _():
        gain_sum_ref[...] = jnp.zeros_like(gain_sum_ref)
        for j in range(NDIM):
            state_ref[j] = start_ref[j]

    keep = [keep_ref[j] for j in range(NDIM)]

    def step(t, state):
        place = TB - 1 - t
        now = row(rows, place)
        state = tuple(keep[j] * state[j] + now for j in range(NDIM))
        terms = [weight_ref[j] * state[j] for j in range(NDIM)]
        while len(terms) > 1:
            terms = [a + b for a, b in zip(terms[::2], terms[1::2])]
        outs[pl.ds(pl.multiple_of(place * SUB, SUB), SUB), :] = terms[0]
        return state

    state = lax.fori_loop(0, TB, step, tuple(state_ref[j] for j in range(NDIM)), unroll=4)
    for j in range(NDIM):
        state_ref[j] = state[j]
    d_xn = from_rows(outs) + grad * omega_ref[...] + normed_ref[...].astype(jnp.float32)
    x = x_ref[...].astype(jnp.float32)
    mean = jnp.mean(x, axis=1, keepdims=True)
    power = jnp.mean(x * x, axis=1, keepdims=True)
    scale = lax.rsqrt(power - mean * mean + EPS)
    normed = (x - mean) * scale
    gain_sum_ref[...] += jnp.sum(d_xn * normed, axis=0, keepdims=True)
    scaled = d_xn * gain_ref[...]
    first = jnp.mean(scaled, axis=1, keepdims=True)
    second = jnp.mean(scaled * normed, axis=1, keepdims=True)
    back = scale * (scaled - first - normed * second)
    out_ref[...] = (direct_ref[...].astype(jnp.float32) + back).astype(jnp.bfloat16)


def sds(shape, dtype=jnp.float32):
    return jax.ShapeDtypeStruct(shape, dtype)


def block(reverse=None):
    if reverse is None:
        return pl.BlockSpec((TB, D), lambda i: (i, 0))
    return pl.BlockSpec((TB, D), lambda i: (reverse - 1 - i, 0))


def whole(*shape):
    return pl.BlockSpec(shape, lambda i: (0,) * len(shape))


STATE = (NDIM, SUB, LANES)
STATES = (2 * NDIM, SUB, LANES)
ROWS = pltpu.VMEM((TB * SUB, LANES), jnp.float32)
PARAMS = pltpu.CompilerParams(vmem_limit_bytes=32 << 20)


def norm_ends(x, gain, keep):
    count = x.shape[0]
    return pl.pallas_call(
        norm_ends_kernel,
        grid=(count // TB,),
        in_specs=[block(), whole(1, D), whole(*STATE)],
        out_specs=[block(), whole(*STATES)],
        out_shape=[sds((count, D), jnp.bfloat16), sds(STATES)],
        scratch_shapes=[ROWS],
        compiler_params=PARAMS,
        cost_estimate=pl.CostEstimate(flops=count * D * 64, transcendentals=0, bytes_accessed=count * D * 4),
        name="norm_ends",
    )(x, gain, keep)


def ema(xn, keep, weight, omega, start):
    count = xn.shape[0]
    return pl.pallas_call(
        ema_kernel,
        grid=(count // TB,),
        in_specs=[block(), whole(*STATE), whole(*STATE), whole(1, D), whole(*STATES)],
        out_specs=[block(), block()],
        out_shape=[sds((count, D)), sds((count, D), jnp.bfloat16)],
        scratch_shapes=[ROWS, ROWS, pltpu.VMEM(STATE, jnp.float32)],
        compiler_params=PARAMS,
        cost_estimate=pl.CostEstimate(flops=count * D * 64, transcendentals=0, bytes_accessed=count * D * 8),
        name="ema",
    )(xn, keep, weight, omega, start)


def adjoint_start(grad, keep):
    count = grad.shape[0]
    return pl.pallas_call(
        adjoint_start_kernel,
        grid=(count // TB,),
        in_specs=[block(count // TB), whole(*STATE)],
        out_specs=whole(*STATE),
        out_shape=sds(STATE),
        scratch_shapes=[ROWS],
        compiler_params=PARAMS,
        cost_estimate=pl.CostEstimate(flops=count * D * 32, transcendentals=0, bytes_accessed=count * D * 4),
        name="adjoint_start",
    )(grad, keep)


def ema_params(grad, xn, keep, start):
    count = grad.shape[0]
    return pl.pallas_call(
        ema_params_kernel,
        grid=(count // TB,),
        in_specs=[block(), block(), whole(*STATE), whole(*STATES)],
        out_specs=[whole(*STATES), whole(1, D)],
        out_shape=[sds(STATES), sds((1, D))],
        scratch_shapes=[ROWS, ROWS, pltpu.VMEM(STATES, jnp.float32)],
        compiler_params=PARAMS,
        cost_estimate=pl.CostEstimate(flops=count * D * 128, transcendentals=0, bytes_accessed=count * D * 6),
        name="ema_params",
    )(grad, xn, keep, start)


def token_grads(grad, x, normed_part, direct, gain, omega, keep, weight, start):
    count = grad.shape[0]
    back = count // TB
    return pl.pallas_call(
        token_grad_kernel,
        grid=(back,),
        in_specs=[
            block(back), block(back), block(back), block(back),
            whole(1, D), whole(1, D), whole(*STATE), whole(*STATE), whole(*STATE),
        ],
        out_specs=[block(back), whole(1, D)],
        out_shape=[sds((count, D), jnp.bfloat16), sds((1, D))],
        scratch_shapes=[ROWS, ROWS, pltpu.VMEM(STATE, jnp.float32)],
        compiler_params=PARAMS,
        cost_estimate=pl.CostEstimate(flops=count * D * 64, transcendentals=0, bytes_accessed=count * D * 14),
        name="token_grads",
    )(grad, x, normed_part, direct, gain, omega, keep, weight, start)


def group_scores(query, keys):
    blocks = query.shape[0] // GROUP
    query_blocks = query.reshape(blocks, GROUP, query.shape[1])
    key_blocks = keys.reshape(blocks, GROUP, keys.shape[1])
    raw = jnp.einsum("nqz,nkz->nqk", query_blocks, key_blocks, preferred_element_type=jnp.float32)
    raw = raw * query.shape[1] ** (-0.5)
    place = jnp.arange(GROUP)
    return jnp.where((place[:, None] >= place[None, :])[None], raw, -1e30)


def gather_columns(shard, dp, index):
    share = shard.shape[0] // dp
    part = lax.dynamic_slice_in_dim(shard, index * share, share, 0)
    part = lax.all_gather(part, "mp", axis=1, tiled=True)
    return lax.all_gather(part, "dp", axis=0, tiled=True)


def gather_rows(shard, dp, index):
    share = shard.shape[0] // dp
    part = lax.dynamic_slice_in_dim(shard, index * share, share, 0)
    return lax.all_gather(part, ("mp", "dp"), axis=0, tiled=True)


def reduce_columns(grad):
    part = lax.psum_scatter(grad.astype(jnp.bfloat16), "dp", scatter_dimension=0, tiled=True)
    part = lax.psum_scatter(part, "mp", scatter_dimension=1, tiled=True)
    return lax.all_gather(part, "dp", axis=0, tiled=True).astype(jnp.float32)


def reduce_rows(grad, dp, mp):
    share = grad.shape[0] // (dp * mp)
    blocks = grad.astype(jnp.bfloat16).reshape(mp, dp, share, grad.shape[1])
    part = lax.psum_scatter(blocks, "dp", scatter_dimension=1, tiled=False)
    part = lax.psum_scatter(part, "mp", scatter_dimension=0, tiled=False)
    return lax.all_gather(part, "dp", axis=0, tiled=True).astype(jnp.float32)


def local(
    dp,
    mp,
    tokens,
    cotangent,
    norm_gain,
    ema_delta,
    ema_alpha,
    ema_beta,
    ema_eta,
    ema_omega,
    shared_proj,
    query_gain,
    query_bias,
    key_gain,
    value_proj,
    gate_proj,
    mixer_proj,
    update_proj,
    output_proj,
    ffn_gain,
    up_proj,
    down_proj,
):
    width = tokens.shape[1]
    index = lax.axis_index("dp")
    part = lax.axis_index("mp")
    count = tokens.shape[0] // mp
    span = LEN // count
    head_scale = query_gain.shape[0] ** (-0.5)

    x_low = lax.all_to_all(tokens, "mp", 0, 1, tiled=True)
    small = jnp.concatenate(
        [
            ema_delta, ema_alpha, ema_beta, ema_eta,
            norm_gain[:, None], ema_omega[:, None], ffn_gain[:, None],
        ],
        axis=1,
    )
    small = lax.all_gather(small, "mp", axis=0, tiled=True)
    small = small.T
    delta, alpha, beta, eta = (small[NDIM * i : NDIM * (i + 1)] for i in range(4))
    gain = small[4 * NDIM : 4 * NDIM + 1]
    omega = small[4 * NDIM + 1 : 4 * NDIM + 2]
    gain_two = small[4 * NDIM + 2 : 4 * NDIM + 3]
    rate = jax.nn.sigmoid(delta)
    damp = jax.nn.sigmoid(alpha)
    keep = (1.0 - rate * damp).reshape(STATE)
    weight = (rate * beta * eta).reshape(STATE)

    value_all = gather_columns(value_proj, dp, index)
    gate_all = gather_columns(gate_proj, dp, index)
    update_all = gather_columns(update_proj, dp, index)
    mixer_all = gather_columns(mixer_proj, dp, index)
    output_all = gather_rows(output_proj, dp, index)
    up_all = gather_columns(up_proj, dp, index)
    down_all = gather_rows(down_proj, dp, index)
    grad_out = lax.all_to_all(cotangent, "mp", 0, 1, tiled=True)

    xn, ends = norm_ends(x_low, gain, keep)
    forward = [(i, i + 1) for i in range(mp - 1) if (i + 1) % span]
    backward = [(j, i) for i, j in forward]
    starts = lax.ppermute(ends, "mp", forward)
    value_pre = matmul(xn, value_all)
    values = jax.nn.silu(value_pre).astype(jnp.bfloat16)
    mix_pre, xp = ema(xn, keep, weight, omega, starts)

    shared_pre = matmul(xp, shared_proj)
    shared = jax.nn.silu(shared_pre)
    query = (shared * query_gain + query_bias).astype(jnp.bfloat16)
    keys = (shared * key_gain).astype(jnp.bfloat16)
    gate_pre = matmul(xp, gate_all)
    gate = jax.nn.silu(gate_pre)
    scores = group_scores(query, keys)
    peak = jnp.max(scores, axis=-1, keepdims=True)
    weights = jnp.exp(scores - peak)
    probs = weights / jnp.sum(weights, axis=-1, keepdims=True)
    probs_low = probs.astype(jnp.bfloat16)
    blocks = probs.shape[0]
    value_blocks = values.reshape(blocks, GROUP, values.shape[1])
    attended = jnp.einsum(
        "dzc,dcs->dzs", probs_low, value_blocks, preferred_element_type=jnp.float32
    ).reshape(count, values.shape[1])
    hidden = (gate * attended).astype(jnp.bfloat16)
    inputs = x_low.astype(jnp.float32)
    update = jax.nn.sigmoid(matmul(xp, update_all))
    act_pre = matmul(xp, mixer_all) + matmul(hidden, output_all)
    act_value = jax.nn.silu(act_pre)
    middle = update * act_value + (1.0 - update) * inputs
    mean = jnp.mean(middle, axis=1, keepdims=True)
    power = jnp.mean(middle * middle, axis=1, keepdims=True)
    scale_two = lax.rsqrt(power - mean * mean + EPS)
    normed_two = (middle - mean) * scale_two
    ffn_in = (normed_two * gain_two).astype(jnp.bfloat16)
    up_pre = matmul(ffn_in, up_all)
    upper = jax.nn.silu(up_pre).astype(jnp.bfloat16)
    layer_rows = (middle + matmul(upper, down_all)).astype(jnp.bfloat16)
    layer_out = lax.all_to_all(layer_rows, "mp", 1, 0, tiled=True)

    down_grad = reduce_rows(matmul_tn(upper, grad_out), dp, mp)
    d_up_pre = (matmul_nt(grad_out, down_all) * silu_slope(up_pre)).astype(jnp.bfloat16)
    up_grad = reduce_columns(matmul_tn(ffn_in, d_up_pre))
    d_ffn_in = matmul_nt(d_up_pre, up_all)
    ffn_part = jnp.sum(d_ffn_in * normed_two, axis=0)
    scaled = d_ffn_in * gain_two
    first = jnp.mean(scaled, axis=1, keepdims=True)
    second = jnp.mean(scaled * normed_two, axis=1, keepdims=True)
    d_middle = grad_out.astype(jnp.float32) + scale_two * (scaled - first - normed_two * second)

    d_update_pre = (d_middle * (act_value - inputs) * update * (1.0 - update)).astype(jnp.bfloat16)
    d_act_pre = (d_middle * update * silu_slope(act_pre)).astype(jnp.bfloat16)
    d_inputs = d_middle * (1.0 - update)
    output_grad = reduce_rows(matmul_tn(hidden, d_act_pre), dp, mp)
    mixer_grad = reduce_columns(matmul_tn(xp, d_act_pre))
    update_grad = reduce_columns(matmul_tn(xp, d_update_pre))
    d_hidden = matmul_nt(d_act_pre, output_all)
    d_gate_pre = (d_hidden * attended * silu_slope(gate_pre)).astype(jnp.bfloat16)
    d_attended = (d_hidden * gate).astype(jnp.bfloat16).reshape(blocks, GROUP, -1)
    gate_grad = reduce_columns(matmul_tn(xp, d_gate_pre))
    d_probs = jnp.einsum(
        "gas,gcs->gac", d_attended, value_blocks, preferred_element_type=jnp.float32
    )
    d_value = jnp.einsum(
        "uhi,uhs->uis", probs_low, d_attended, preferred_element_type=jnp.float32
    ).reshape(count, values.shape[1])
    d_value_pre = (d_value * silu_slope(value_pre)).astype(jnp.bfloat16)
    value_grad = reduce_columns(matmul_tn(xn, d_value_pre))
    d_scores = probs * (d_probs - jnp.sum(probs * d_probs, axis=-1, keepdims=True))
    d_scores_low = d_scores.astype(jnp.bfloat16)
    query_blocks = query.reshape(blocks, GROUP, -1)
    key_blocks = keys.reshape(blocks, GROUP, -1)
    d_query = (
        jnp.einsum(
            "nqk,nkz->nqz", d_scores_low, key_blocks, preferred_element_type=jnp.float32
        ).reshape(count, -1)
        * head_scale
    )
    d_keys = (
        jnp.einsum(
            "nqk,nqz->nkz", d_scores_low, query_blocks, preferred_element_type=jnp.float32
        ).reshape(count, -1)
        * head_scale
    )
    query_part = jnp.sum(d_query * shared, axis=0)
    bias_part = jnp.sum(d_query, axis=0)
    key_part = jnp.sum(d_keys * shared, axis=0)
    d_shared_pre = ((d_query * query_gain + d_keys * key_gain) * silu_slope(shared_pre)).astype(
        jnp.bfloat16
    )
    shared_part = matmul_tn(xp, d_shared_pre)
    d_mixed = matmul_nt(d_gate_pre, gate_all) + matmul_nt(d_update_pre, update_all)
    d_mixed = d_mixed + matmul_nt(d_act_pre, mixer_all) + matmul_nt(d_shared_pre, shared_proj)
    d_mix_pre = d_mixed * silu_slope(mix_pre)
    normed_part = matmul_nt(d_value_pre, value_all)

    ahead = lax.ppermute(adjoint_start(d_mix_pre, keep), "mp", backward)
    sums, omega_part = ema_params(d_mix_pre, xn, keep, starts)
    token_rows, gain_part = token_grads(
        d_mix_pre, x_low, normed_part, d_inputs, gain, omega, keep, weight, ahead
    )
    token_grad = lax.all_to_all(token_rows, "mp", 1, 0, tiled=True)

    feature = jnp.concatenate(
        [sums.reshape(2 * NDIM, D), omega_part, gain_part, ffn_part[None]], axis=0
    )
    feature, shared_grad, query_grad, bias_grad, key_grad = lax.psum(
        (feature, shared_part, query_part, bias_part, key_part), ("dp", "mp")
    )
    weight_sum = feature[:NDIM]
    keep_sum = feature[NDIM : 2 * NDIM] * weight.reshape(NDIM, D)
    d_rate = weight_sum * beta * eta - keep_sum * damp
    packed = jnp.concatenate(
        [
            d_rate * rate * (1.0 - rate),
            -keep_sum * rate * damp * (1.0 - damp),
            weight_sum * rate * eta,
            weight_sum * rate * beta,
            feature[2 * NDIM :],
        ],
        axis=0,
    )
    mine = lax.dynamic_slice_in_dim(packed, part * width, width, 1).T
    delta_grad, alpha_grad, beta_grad, eta_grad = (
        mine[:, NDIM * i : NDIM * (i + 1)] for i in range(4)
    )
    omega_grad = mine[:, 4 * NDIM]
    gain_grad = mine[:, 4 * NDIM + 1]
    ffn_grad = mine[:, 4 * NDIM + 2]
    return (
        layer_out, token_grad, gain_grad, delta_grad, alpha_grad, beta_grad, eta_grad, omega_grad,
        shared_grad, query_grad, bias_grad, key_grad, value_grad, gate_grad, mixer_grad,
        update_grad, output_grad, ffn_grad, up_grad, down_grad,
    )


def solution(mesh):
    dp, mp = mesh.shape["dp"], mesh.shape["mp"]
    params = (
        P("mp"), P("mp", None), P("mp", None), P("mp", None), P("mp", None), P("mp"),
        P(), P(), P(), P(),
        P(None, "mp"), P(None, "mp"), P(None, "mp"), P(None, "mp"), P("mp", None),
        P("mp"), P(None, "mp"), P("mp", None),
    )
    specs = (P("dp", "mp"), P("dp", "mp")) + params
    return jax.shard_map(
        functools.partial(local, dp, mp), mesh=mesh, in_specs=specs, out_specs=specs, check_vma=False
    )
```

```python
import functools

import jax
import jax.numpy as jnp
from jax import lax
from jax.experimental import pallas as pl
from jax.experimental.pallas import tpu as pltpu
from jax.sharding import PartitionSpec as P

D = 1024
GROUP = 128
LEN = 2048
NDIM = 16
LANES = 128
SUB = D // LANES
EPS = 1e-05
TB = 128


def matmul(left, right):
    return jnp.dot(left, right, preferred_element_type=jnp.float32)


def matmul_tn(left, right):
    return lax.dot_general(
        left, right, (((0,), (0,)), ((), ())), preferred_element_type=jnp.float32
    )


def matmul_nt(left, right):
    return lax.dot_general(
        left, right, (((1,), (1,)), ((), ())), preferred_element_type=jnp.float32
    )


def silu_slope(values):
    logistic = jax.nn.sigmoid(values)
    return logistic * (1.0 + values * (1.0 - logistic))


def to_rows(scratch, value):
    for part in range(SUB):
        scratch[pl.ds(part, TB, stride=SUB), :] = value[:, part * LANES : (part + 1) * LANES]


def from_rows(scratch):
    return jnp.concatenate(
        [scratch[pl.ds(part, TB, stride=SUB), :] for part in range(SUB)], axis=1
    )


def row(scratch, index):
    return scratch[pl.ds(pl.multiple_of(index * SUB, SUB), SUB), :]


def norm_ends_kernel(x_ref, gain_ref, keep_ref, xn_ref, ends_ref, rows):
    x = x_ref[...].astype(jnp.float32)
    mean = jnp.mean(x, axis=1, keepdims=True)
    power = jnp.mean(x * x, axis=1, keepdims=True)
    scale = lax.rsqrt(power - mean * mean + EPS)
    xn = ((x - mean) * scale * gain_ref[...]).astype(jnp.bfloat16)
    xn_ref[...] = xn
    to_rows(rows, xn.astype(jnp.float32))

    @pl.when(pl.program_id(0) == 0)
    def _():
        ends_ref[...] = jnp.zeros_like(ends_ref)

    keep = [keep_ref[j] for j in range(NDIM)]

    def step(t, carry):
        state, slope = carry
        now = row(rows, t)
        slope = tuple(keep[j] * slope[j] + state[j] for j in range(NDIM))
        state = tuple(keep[j] * state[j] + now for j in range(NDIM))
        return (state, slope)

    state = tuple(ends_ref[j] for j in range(NDIM))
    slope = tuple(ends_ref[NDIM + j] for j in range(NDIM))
    state, slope = lax.fori_loop(0, TB, step, (state, slope), unroll=4)
    for j in range(NDIM):
        ends_ref[j] = state[j]
        ends_ref[NDIM + j] = slope[j]


def ema_kernel(xn_ref, keep_ref, weight_ref, omega_ref, start_ref, mix_ref, xp_ref, rows, outs, state_ref):
    xn = xn_ref[...].astype(jnp.float32)
    to_rows(rows, xn)

    @pl.when(pl.program_id(0) == 0)
    def _():
        for j in range(NDIM):
            state_ref[j] = start_ref[j]

    keep = [keep_ref[j] for j in range(NDIM)]

    def step(t, state):
        now = row(rows, t)
        state = tuple(keep[j] * state[j] + now for j in range(NDIM))
        terms = [weight_ref[j] * state[j] for j in range(NDIM)]
        while len(terms) > 1:
            terms = [a + b for a, b in zip(terms[::2], terms[1::2])]
        outs[pl.ds(pl.multiple_of(t * SUB, SUB), SUB), :] = terms[0]
        return state

    state = lax.fori_loop(0, TB, step, tuple(state_ref[j] for j in range(NDIM)), unroll=4)
    for j in range(NDIM):
        state_ref[j] = state[j]
    mix = from_rows(outs) + omega_ref[...] * xn
    mix_ref[...] = mix
    xp_ref[...] = (mix * jax.nn.sigmoid(mix)).astype(jnp.bfloat16)


def adjoint_start_kernel(grad_ref, keep_ref, start_ref, rows):
    to_rows(rows, grad_ref[...])

    @pl.when(pl.program_id(0) == 0)
    def _():
        start_ref[...] = jnp.zeros_like(start_ref)

    keep = [keep_ref[j] for j in range(NDIM)]

    def step(t, state):
        now = row(rows, TB - 1 - t)
        return tuple(keep[j] * state[j] + now for j in range(NDIM))

    state = lax.fori_loop(0, TB, step, tuple(start_ref[j] for j in range(NDIM)), unroll=4)
    for j in range(NDIM):
        start_ref[j] = state[j]


def ema_params_kernel(grad_ref, xn_ref, keep_ref, start_ref, sums_ref, omega_ref, grads, rows, state_ref):
    xn = xn_ref[...].astype(jnp.float32)
    to_rows(rows, xn)
    grad = grad_ref[...]
    to_rows(grads, grad)

    @pl.when(pl.program_id(0) == 0)
    def _():
        sums_ref[...] = jnp.zeros_like(sums_ref)
        omega_ref[...] = jnp.zeros_like(omega_ref)
        state_ref[...] = start_ref[...]

    omega_ref[...] += jnp.sum(grad * xn, axis=0, keepdims=True)
    half = NDIM // 2
    for first in (0, half):
        dims = range(first, first + half)
        keep = [keep_ref[j] for j in dims]

        def step(t, carry):
            state, slope, weight_sum, keep_sum = carry
            now = row(rows, t)
            grad_now = row(grads, t)
            slope = tuple(keep[j] * slope[j] + state[j] for j in range(half))
            state = tuple(keep[j] * state[j] + now for j in range(half))
            weight_sum = tuple(weight_sum[j] + grad_now * state[j] for j in range(half))
            keep_sum = tuple(keep_sum[j] + grad_now * slope[j] for j in range(half))
            return (state, slope, weight_sum, keep_sum)

        carry = (
            tuple(state_ref[j] for j in dims),
            tuple(state_ref[NDIM + j] for j in dims),
            tuple(sums_ref[j] for j in dims),
            tuple(sums_ref[NDIM + j] for j in dims),
        )
        state, slope, weight_sum, keep_sum = lax.fori_loop(0, TB, step, carry, unroll=4)
        for place, j in enumerate(dims):
            state_ref[j] = state[place]
            state_ref[NDIM + j] = slope[place]
            sums_ref[j] = weight_sum[place]
            sums_ref[NDIM + j] = keep_sum[place]


def token_grad_kernel(
    grad_ref, x_ref, normed_ref, direct_ref, gain_ref, omega_ref, keep_ref, weight_ref, start_ref,
    out_ref, gain_sum_ref, rows, outs, state_ref,
):
    grad = grad_ref[...]
    to_rows(rows, grad)

    @pl.when(pl.program_id(0) == 0)
    def _():
        gain_sum_ref[...] = jnp.zeros_like(gain_sum_ref)
        for j in range(NDIM):
            state_ref[j] = start_ref[j]

    keep = [keep_ref[j] for j in range(NDIM)]

    def step(t, state):
        place = TB - 1 - t
        now = row(rows, place)
        state = tuple(keep[j] * state[j] + now for j in range(NDIM))
        terms = [weight_ref[j] * state[j] for j in range(NDIM)]
        while len(terms) > 1:
            terms = [a + b for a, b in zip(terms[::2], terms[1::2])]
        outs[pl.ds(pl.multiple_of(place * SUB, SUB), SUB), :] = terms[0]
        return state

    state = lax.fori_loop(0, TB, step, tuple(state_ref[j] for j in range(NDIM)), unroll=4)
    for j in range(NDIM):
        state_ref[j] = state[j]
    d_xn = from_rows(outs) + grad * omega_ref[...] + normed_ref[...].astype(jnp.float32)
    x = x_ref[...].astype(jnp.float32)
    mean = jnp.mean(x, axis=1, keepdims=True)
    power = jnp.mean(x * x, axis=1, keepdims=True)
    scale = lax.rsqrt(power - mean * mean + EPS)
    normed = (x - mean) * scale
    gain_sum_ref[...] += jnp.sum(d_xn * normed, axis=0, keepdims=True)
    scaled = d_xn * gain_ref[...]
    first = jnp.mean(scaled, axis=1, keepdims=True)
    second = jnp.mean(scaled * normed, axis=1, keepdims=True)
    back = scale * (scaled - first - normed * second)
    out_ref[...] = (direct_ref[...].astype(jnp.float32) + back).astype(jnp.bfloat16)


def sds(shape, dtype=jnp.float32):
    return jax.ShapeDtypeStruct(shape, dtype)


def block(reverse=None):
    if reverse is None:
        return pl.BlockSpec((TB, D), lambda i: (i, 0))
    return pl.BlockSpec((TB, D), lambda i: (reverse - 1 - i, 0))


def whole(*shape):
    return pl.BlockSpec(shape, lambda i: (0,) * len(shape))


STATE = (NDIM, SUB, LANES)
STATES = (2 * NDIM, SUB, LANES)
ROWS = pltpu.VMEM((TB * SUB, LANES), jnp.float32)
PARAMS = pltpu.CompilerParams(vmem_limit_bytes=32 << 20)


def norm_ends(x, gain, keep):
    count = x.shape[0]
    return pl.pallas_call(
        norm_ends_kernel,
        grid=(count // TB,),
        in_specs=[block(), whole(1, D), whole(*STATE)],
        out_specs=[block(), whole(*STATES)],
        out_shape=[sds((count, D), jnp.bfloat16), sds(STATES)],
        scratch_shapes=[ROWS],
        compiler_params=PARAMS,
        cost_estimate=pl.CostEstimate(flops=count * D * 64, transcendentals=0, bytes_accessed=count * D * 4),
        name="norm_ends",
    )(x, gain, keep)


def ema(xn, keep, weight, omega, start):
    count = xn.shape[0]
    return pl.pallas_call(
        ema_kernel,
        grid=(count // TB,),
        in_specs=[block(), whole(*STATE), whole(*STATE), whole(1, D), whole(*STATES)],
        out_specs=[block(), block()],
        out_shape=[sds((count, D)), sds((count, D), jnp.bfloat16)],
        scratch_shapes=[ROWS, ROWS, pltpu.VMEM(STATE, jnp.float32)],
        compiler_params=PARAMS,
        cost_estimate=pl.CostEstimate(flops=count * D * 64, transcendentals=0, bytes_accessed=count * D * 8),
        name="ema",
    )(xn, keep, weight, omega, start)


def adjoint_start(grad, keep):
    count = grad.shape[0]
    return pl.pallas_call(
        adjoint_start_kernel,
        grid=(count // TB,),
        in_specs=[block(count // TB), whole(*STATE)],
        out_specs=whole(*STATE),
        out_shape=sds(STATE),
        scratch_shapes=[ROWS],
        compiler_params=PARAMS,
        cost_estimate=pl.CostEstimate(flops=count * D * 32, transcendentals=0, bytes_accessed=count * D * 4),
        name="adjoint_start",
    )(grad, keep)


def ema_params(grad, xn, keep, start):
    count = grad.shape[0]
    return pl.pallas_call(
        ema_params_kernel,
        grid=(count // TB,),
        in_specs=[block(), block(), whole(*STATE), whole(*STATES)],
        out_specs=[whole(*STATES), whole(1, D)],
        out_shape=[sds(STATES), sds((1, D))],
        scratch_shapes=[ROWS, ROWS, pltpu.VMEM(STATES, jnp.float32)],
        compiler_params=PARAMS,
        cost_estimate=pl.CostEstimate(flops=count * D * 128, transcendentals=0, bytes_accessed=count * D * 6),
        name="ema_params",
    )(grad, xn, keep, start)


def token_grads(grad, x, normed_part, direct, gain, omega, keep, weight, start):
    count = grad.shape[0]
    back = count // TB
    return pl.pallas_call(
        token_grad_kernel,
        grid=(back,),
        in_specs=[
            block(back), block(back), block(back), block(back),
            whole(1, D), whole(1, D), whole(*STATE), whole(*STATE), whole(*STATE),
        ],
        out_specs=[block(back), whole(1, D)],
        out_shape=[sds((count, D), jnp.bfloat16), sds((1, D))],
        scratch_shapes=[ROWS, ROWS, pltpu.VMEM(STATE, jnp.float32)],
        compiler_params=PARAMS,
        cost_estimate=pl.CostEstimate(flops=count * D * 64, transcendentals=0, bytes_accessed=count * D * 14),
        name="token_grads",
    )(grad, x, normed_part, direct, gain, omega, keep, weight, start)


MESH = pl.DeviceIdType.MESH


def rank_of(index, order):
    total = 0
    for place, bit in enumerate(order):
        total = total + lax.rem(lax.div(index, 1 << bit), 2) * (1 << place)
    return total


def flip(index, bit):
    low = lax.rem(lax.div(index, 1 << bit), 2)
    return index + (1 - 2 * low) * (1 << bit)


def orders_of(dp):
    bits = dp.bit_length() - 1
    inner = list(range(1, bits))
    return (inner + [0], inner[::-1] + [0])


def gather_kernel(dp, mp, packs, swaps, small_ref, *refs):
    pack_refs, refs = refs[:packs], refs[packs:]
    swap_refs, refs = refs[:swaps], refs[swaps:]
    small_out, refs = refs[0], refs[1:]
    full_refs, refs = refs[:packs], refs[packs:]
    row_refs, refs = refs[:swaps], refs[swaps:]
    send_sem, recv_sem, pass_sem, swap_send, swap_recv, small_send, small_recv, own_sem = refs
    me = lax.axis_index("dp")
    part = lax.axis_index("mp")
    bits = dp.bit_length() - 1
    orders = orders_of(dp)

    barrier = pltpu.get_barrier_semaphore()
    for step in range(1, mp):
        pl.semaphore_signal(
            barrier, inc=1, device_id={"mp": lax.rem(part + step, mp)}, device_id_type=MESH
        )
    for bit in range(bits):
        pl.semaphore_signal(barrier, inc=1, device_id={"dp": flip(me, bit)}, device_id_type=MESH)
    pl.semaphore_wait(barrier, mp - 1 + bits)

    local = []
    sends = []

    def own(src, dst, place):
        copy = pltpu.make_async_copy(src, dst, own_sem.at[place])
        copy.start()
        local.append(copy)

    small_rows = small_ref.shape[0]
    own(small_ref, small_out.at[part], 0)
    for step in range(1, mp):
        to = lax.rem(part + step, mp)
        copy = pltpu.make_async_remote_copy(
            src_ref=small_ref, dst_ref=small_out.at[part],
            send_sem=small_send.at[step], recv_sem=small_recv.at[part],
            device_id={"mp": to}, device_id_type=MESH,
        )
        copy.start()
        sends.append(copy)
    def region(ref, half, held):
        total, width = ref.shape[0], ref.shape[1] // 2
        share = total // dp
        rank = rank_of(me, orders[half])
        first = lax.div(rank, 1 << held) * (share << held)
        return ref.at[
            pl.ds(pl.multiple_of(first, share), share << held), half * width : (half + 1) * width
        ]

    def send_on(place, source, up, src, sem):
        dst = full_refs[place].at[source]
        to = part + 1 if up else part - 1
        copies = []
        for half in range(2):
            copies.append(
                pltpu.make_async_remote_copy(
                    src_ref=region(src, half, 0), dst_ref=region(dst, half, 0),
                    send_sem=send_sem.at[place, 0, sem, half],
                    recv_sem=recv_sem.at[place, 0, source, half],
                    device_id={"mp": to}, device_id_type=MESH,
                )
            )
        there = part < mp - 1 if up else part > 0

        @pl.when(there)
        def _():
            for copy in copies:
                copy.start()

        guarded.append((there, copies))

    guarded = []
    for place in range(packs):
        src, dst = pack_refs[place], full_refs[place]
        send_on(place, part, True, src, 0)
        send_on(place, part, False, src, mp)
    for place in range(packs):
        own(pack_refs[place], full_refs[place].at[part], 1 + swaps + place)

    for place in range(swaps):
        src, dst = swap_refs[place], row_refs[place]
        count, width = dst.shape[0], src.shape[1]
        columns = pl.ds(pl.multiple_of(part * width, width), width)

        def rows(index):
            return pl.ds(pl.multiple_of(index * count, count), count)

        own(src.at[rows(part), :], dst.at[:, columns], 1 + place)
        for step in range(1, mp):
            to = lax.rem(part + step, mp)
            copy = pltpu.make_async_remote_copy(
                src_ref=src.at[rows(to), :], dst_ref=dst.at[:, columns],
                send_sem=swap_send.at[place, step], recv_sem=swap_recv.at[place, part],
                device_id={"mp": to}, device_id_type=MESH,
            )
            copy.start()
            sends.append(copy)

    def arrived(ref, sem):
        pltpu.make_async_copy(ref, ref, sem).wait()

    def source_of(step):
        near = [lax.rem(part + 1, 2) + part - lax.rem(part, 2)]
        low = lax.div(part, mp // 2) == 0
        far = [
            jnp.where(low, mp // 2 + place, mp // 2 - 1 - place) for place in range(mp // 2)
        ]
        return (near + far)[step - 1]

    def advance(place, step, stage):
        source = source_of(step)
        dst = full_refs[place].at[source]
        for half in range(2):
            if stage == 0:
                came = region(dst, half, 0)
            else:
                total, width = dst.shape[0], dst.shape[1] // 2
                share = total // dp
                bit = orders[half][stage - 1]
                rank = rank_of(flip(me, bit), orders[half])
                first = lax.div(rank, 1 << (stage - 1)) * (share << (stage - 1))
                came = dst.at[
                    pl.ds(pl.multiple_of(first, share), share << (stage - 1)),
                    half * width : (half + 1) * width,
                ]
            arrived(came, recv_sem.at[place, stage, source, half])
        if stage == 0:
            forward(place, source, dst)
        for half in range(2):
            if stage < bits:
                bit = orders[half][stage]
                held = region(dst, half, stage)
                copy = pltpu.make_async_remote_copy(
                    src_ref=held, dst_ref=held,
                    send_sem=send_sem.at[place, stage + 1, step, half],
                    recv_sem=recv_sem.at[place, stage + 1, source, half],
                    device_id={"dp": flip(me, bit)}, device_id_type=MESH,
                )
                copy.start()
                sends.append(copy)

    def forward(place, source, dst):
        below = source < part
        there = jnp.logical_or(
            jnp.logical_and(below, part < mp - 1), jnp.logical_and(source > part, part > 0)
        )
        to = jnp.where(below, part + 1, part - 1)
        copies = [
            pltpu.make_async_remote_copy(
                src_ref=region(dst, half, 0), dst_ref=region(dst, half, 0),
                send_sem=pass_sem.at[place, source, half],
                recv_sem=recv_sem.at[place, 0, source, half],
                device_id={"mp": to}, device_id_type=MESH,
            )
            for half in range(2)
        ]

        @pl.when(there)
        def _():
            for copy in copies:
                copy.start()

        guarded.append((there, copies))

    jobs = [(place, step) for place in range(packs) for step in range(1, mp)]
    for wave in range(len(jobs) + bits):
        for stage in range(bits, -1, -1):
            number = wave - stage
            if 0 <= number < len(jobs):
                advance(jobs[number][0], jobs[number][1], stage)
    for place in range(swaps):
        width = swap_refs[place].shape[1]
        for step in range(1, mp):
            source = lax.rem(part + step, mp)
            columns = pl.ds(pl.multiple_of(source * width, width), width)
            arrived(row_refs[place].at[:, columns], swap_recv.at[place, source])
    for step in range(1, mp):
        source = lax.rem(part + step, mp)
        arrived(small_out.at[source], small_recv.at[source])
    for copy in sends:
        copy.wait_send()
    for there, copies in guarded:

        @pl.when(there)
        def _(copies=copies):
            for copy in copies:
                copy.wait_send()

    for copy in local:
        copy.wait()


def gather(dp, mp, small, packs, swaps):
    hbm = pl.BlockSpec(memory_space=pl.ANY)
    bits = dp.bit_length() - 1
    outs = [sds((mp,) + small.shape, small.dtype)]
    outs += [sds((mp,) + item.shape, item.dtype) for item in packs]
    outs += [sds((item.shape[0] // mp, item.shape[1] * mp), item.dtype) for item in swaps]
    dma = pltpu.SemaphoreType.DMA
    results = pl.pallas_call(
        functools.partial(gather_kernel, dp, mp, len(packs), len(swaps)),
        in_specs=[hbm] * (1 + len(packs) + len(swaps)),
        out_specs=[hbm] * len(outs),
        out_shape=outs,
        scratch_shapes=[
            dma((len(packs), bits + 1, mp + 1, 2)),
            dma((len(packs), bits + 1, mp, 2)),
            dma((len(packs), mp, 2)),
            dma((len(swaps), mp)),
            dma((len(swaps), mp)),
            dma((mp,)),
            dma((mp,)),
            dma((1 + len(swaps) + len(packs),)),
        ],
        compiler_params=pltpu.CompilerParams(
            collective_id=0, has_side_effects=True, vmem_limit_bytes=4 << 20
        ),
        name="gather",
    )(small, *packs, *swaps)
    return results[0], results[1 : 1 + len(packs)], results[1 + len(packs) :]


def group_scores(query, keys):
    blocks = query.shape[0] // GROUP
    query_blocks = query.reshape(blocks, GROUP, query.shape[1])
    key_blocks = keys.reshape(blocks, GROUP, keys.shape[1])
    raw = jnp.einsum("nqz,nkz->nqk", query_blocks, key_blocks, preferred_element_type=jnp.float32)
    raw = raw * query.shape[1] ** (-0.5)
    place = jnp.arange(GROUP)
    return jnp.where((place[:, None] >= place[None, :])[None], raw, -1e30)


def reduce_columns(grad):
    part = lax.psum_scatter(grad.astype(jnp.bfloat16), "dp", scatter_dimension=0, tiled=True)
    part = lax.psum_scatter(part, "mp", scatter_dimension=1, tiled=True)
    return lax.all_gather(part, "dp", axis=0, tiled=True).astype(jnp.float32)


def reduce_rows(grad, dp, mp):
    share = grad.shape[0] // (dp * mp)
    blocks = grad.astype(jnp.bfloat16).reshape(mp, dp, share, grad.shape[1])
    part = lax.psum_scatter(blocks, "dp", scatter_dimension=1, tiled=False)
    part = lax.psum_scatter(part, "mp", scatter_dimension=0, tiled=False)
    return lax.all_gather(part, "dp", axis=0, tiled=True).astype(jnp.float32)


def local(
    dp,
    mp,
    tokens,
    cotangent,
    norm_gain,
    ema_delta,
    ema_alpha,
    ema_beta,
    ema_eta,
    ema_omega,
    shared_proj,
    query_gain,
    query_bias,
    key_gain,
    value_proj,
    gate_proj,
    mixer_proj,
    update_proj,
    output_proj,
    ffn_gain,
    up_proj,
    down_proj,
):
    width = tokens.shape[1]
    part = lax.axis_index("mp")
    count = tokens.shape[0] // mp
    span = LEN // count
    head_scale = query_gain.shape[0] ** (-0.5)

    small = jnp.concatenate(
        [
            ema_delta, ema_alpha, ema_beta, ema_eta,
            norm_gain[:, None], ema_omega[:, None], ffn_gain[:, None],
        ],
        axis=1,
    ).T
    small = jnp.pad(small, ((0, -small.shape[0] % 8), (0, 0)))
    pack_one = jnp.concatenate([value_proj, gate_proj, mixer_proj, update_proj], axis=1)
    pack_two = jnp.concatenate([up_proj, down_proj], axis=1)
    small, (one, outs, two), (x_low, grad_out) = gather(
        dp, mp, small, (pack_one, output_proj, pack_two), (tokens, cotangent)
    )
    small = small.transpose(1, 0, 2).reshape(small.shape[1], D)
    wide, narrow = value_proj.shape[1], mixer_proj.shape[1]

    def columns(first, size, pack):
        block = lax.slice_in_dim(pack, first, first + size, axis=2)
        return block.transpose(1, 0, 2).reshape(block.shape[1], mp * size)

    value_all = columns(0, wide, one)
    gate_all = columns(wide, wide, one)
    mixer_all = columns(2 * wide, narrow, one)
    update_all = columns(2 * wide + narrow, narrow, one)
    output_all = outs.reshape(-1, D)
    up_all = columns(0, up_proj.shape[1], two)
    down_all = lax.slice_in_dim(two, up_proj.shape[1], two.shape[2], axis=2).reshape(-1, D)
    delta, alpha, beta, eta = (small[NDIM * i : NDIM * (i + 1)] for i in range(4))
    gain = small[4 * NDIM : 4 * NDIM + 1]
    omega = small[4 * NDIM + 1 : 4 * NDIM + 2]
    gain_two = small[4 * NDIM + 2 : 4 * NDIM + 3]
    rate = jax.nn.sigmoid(delta)
    damp = jax.nn.sigmoid(alpha)
    keep = (1.0 - rate * damp).reshape(STATE)
    weight = (rate * beta * eta).reshape(STATE)

    xn, ends = norm_ends(x_low, gain, keep)
    forward = [(i, i + 1) for i in range(mp - 1) if (i + 1) % span]
    backward = [(j, i) for i, j in forward]
    starts = lax.ppermute(ends, "mp", forward)
    value_pre = matmul(xn, value_all)
    values = jax.nn.silu(value_pre).astype(jnp.bfloat16)
    mix_pre, xp = ema(xn, keep, weight, omega, starts)

    shared_pre = matmul(xp, shared_proj)
    shared = jax.nn.silu(shared_pre)
    query = (shared * query_gain + query_bias).astype(jnp.bfloat16)
    keys = (shared * key_gain).astype(jnp.bfloat16)
    gate_pre = matmul(xp, gate_all)
    gate = jax.nn.silu(gate_pre)
    scores = group_scores(query, keys)
    peak = jnp.max(scores, axis=-1, keepdims=True)
    weights = jnp.exp(scores - peak)
    probs = weights / jnp.sum(weights, axis=-1, keepdims=True)
    probs_low = probs.astype(jnp.bfloat16)
    blocks = probs.shape[0]
    value_blocks = values.reshape(blocks, GROUP, values.shape[1])
    attended = jnp.einsum(
        "dzc,dcs->dzs", probs_low, value_blocks, preferred_element_type=jnp.float32
    ).reshape(count, values.shape[1])
    hidden = (gate * attended).astype(jnp.bfloat16)
    inputs = x_low.astype(jnp.float32)
    update = jax.nn.sigmoid(matmul(xp, update_all))
    act_pre = matmul(xp, mixer_all) + matmul(hidden, output_all)
    act_value = jax.nn.silu(act_pre)
    middle = update * act_value + (1.0 - update) * inputs
    mean = jnp.mean(middle, axis=1, keepdims=True)
    power = jnp.mean(middle * middle, axis=1, keepdims=True)
    scale_two = lax.rsqrt(power - mean * mean + EPS)
    normed_two = (middle - mean) * scale_two
    ffn_in = (normed_two * gain_two).astype(jnp.bfloat16)
    up_pre = matmul(ffn_in, up_all)
    upper = jax.nn.silu(up_pre).astype(jnp.bfloat16)
    layer_rows = (middle + matmul(upper, down_all)).astype(jnp.bfloat16)
    layer_out = lax.all_to_all(layer_rows, "mp", 1, 0, tiled=True)

    down_grad = reduce_rows(matmul_tn(upper, grad_out), dp, mp)
    d_up_pre = (matmul_nt(grad_out, down_all) * silu_slope(up_pre)).astype(jnp.bfloat16)
    up_grad = reduce_columns(matmul_tn(ffn_in, d_up_pre))
    d_ffn_in = matmul_nt(d_up_pre, up_all)
    ffn_part = jnp.sum(d_ffn_in * normed_two, axis=0)
    scaled = d_ffn_in * gain_two
    first = jnp.mean(scaled, axis=1, keepdims=True)
    second = jnp.mean(scaled * normed_two, axis=1, keepdims=True)
    d_middle = grad_out.astype(jnp.float32) + scale_two * (scaled - first - normed_two * second)

    d_update_pre = (d_middle * (act_value - inputs) * update * (1.0 - update)).astype(jnp.bfloat16)
    d_act_pre = (d_middle * update * silu_slope(act_pre)).astype(jnp.bfloat16)
    d_inputs = d_middle * (1.0 - update)
    output_grad = reduce_rows(matmul_tn(hidden, d_act_pre), dp, mp)
    mixer_grad = reduce_columns(matmul_tn(xp, d_act_pre))
    update_grad = reduce_columns(matmul_tn(xp, d_update_pre))
    d_hidden = matmul_nt(d_act_pre, output_all)
    d_gate_pre = (d_hidden * attended * silu_slope(gate_pre)).astype(jnp.bfloat16)
    d_attended = (d_hidden * gate).astype(jnp.bfloat16).reshape(blocks, GROUP, -1)
    gate_grad = reduce_columns(matmul_tn(xp, d_gate_pre))
    d_probs = jnp.einsum(
        "gas,gcs->gac", d_attended, value_blocks, preferred_element_type=jnp.float32
    )
    d_value = jnp.einsum(
        "uhi,uhs->uis", probs_low, d_attended, preferred_element_type=jnp.float32
    ).reshape(count, values.shape[1])
    d_value_pre = (d_value * silu_slope(value_pre)).astype(jnp.bfloat16)
    value_grad = reduce_columns(matmul_tn(xn, d_value_pre))
    d_scores = probs * (d_probs - jnp.sum(probs * d_probs, axis=-1, keepdims=True))
    d_scores_low = d_scores.astype(jnp.bfloat16)
    query_blocks = query.reshape(blocks, GROUP, -1)
    key_blocks = keys.reshape(blocks, GROUP, -1)
    d_query = (
        jnp.einsum(
            "nqk,nkz->nqz", d_scores_low, key_blocks, preferred_element_type=jnp.float32
        ).reshape(count, -1)
        * head_scale
    )
    d_keys = (
        jnp.einsum(
            "nqk,nqz->nkz", d_scores_low, query_blocks, preferred_element_type=jnp.float32
        ).reshape(count, -1)
        * head_scale
    )
    query_part = jnp.sum(d_query * shared, axis=0)
    bias_part = jnp.sum(d_query, axis=0)
    key_part = jnp.sum(d_keys * shared, axis=0)
    d_shared_pre = ((d_query * query_gain + d_keys * key_gain) * silu_slope(shared_pre)).astype(
        jnp.bfloat16
    )
    shared_part = matmul_tn(xp, d_shared_pre)
    d_mixed = matmul_nt(d_gate_pre, gate_all) + matmul_nt(d_update_pre, update_all)
    d_mixed = d_mixed + matmul_nt(d_act_pre, mixer_all) + matmul_nt(d_shared_pre, shared_proj)
    d_mix_pre = d_mixed * silu_slope(mix_pre)
    normed_part = matmul_nt(d_value_pre, value_all)

    ahead = lax.ppermute(adjoint_start(d_mix_pre, keep), "mp", backward)
    sums, omega_part = ema_params(d_mix_pre, xn, keep, starts)
    token_rows, gain_part = token_grads(
        d_mix_pre, x_low, normed_part, d_inputs, gain, omega, keep, weight, ahead
    )
    token_grad = lax.all_to_all(token_rows, "mp", 1, 0, tiled=True)

    feature = jnp.concatenate(
        [sums.reshape(2 * NDIM, D), omega_part, gain_part, ffn_part[None]], axis=0
    )
    feature, shared_grad, query_grad, bias_grad, key_grad = lax.psum(
        (feature, shared_part, query_part, bias_part, key_part), ("dp", "mp")
    )
    weight_sum = feature[:NDIM]
    keep_sum = feature[NDIM : 2 * NDIM] * weight.reshape(NDIM, D)
    d_rate = weight_sum * beta * eta - keep_sum * damp
    packed = jnp.concatenate(
        [
            d_rate * rate * (1.0 - rate),
            -keep_sum * rate * damp * (1.0 - damp),
            weight_sum * rate * eta,
            weight_sum * rate * beta,
            feature[2 * NDIM :],
        ],
        axis=0,
    )
    mine = lax.dynamic_slice_in_dim(packed, part * width, width, 1).T
    delta_grad, alpha_grad, beta_grad, eta_grad = (
        mine[:, NDIM * i : NDIM * (i + 1)] for i in range(4)
    )
    omega_grad = mine[:, 4 * NDIM]
    gain_grad = mine[:, 4 * NDIM + 1]
    ffn_grad = mine[:, 4 * NDIM + 2]
    return (
        layer_out, token_grad, gain_grad, delta_grad, alpha_grad, beta_grad, eta_grad, omega_grad,
        shared_grad, query_grad, bias_grad, key_grad, value_grad, gate_grad, mixer_grad,
        update_grad, output_grad, ffn_grad, up_grad, down_grad,
    )


def solution(mesh):
    dp, mp = mesh.shape["dp"], mesh.shape["mp"]
    params = (
        P("mp"), P("mp", None), P("mp", None), P("mp", None), P("mp", None), P("mp"),
        P(), P(), P(), P(),
        P(None, "mp"), P(None, "mp"), P(None, "mp"), P(None, "mp"), P("mp", None),
        P("mp"), P(None, "mp"), P("mp", None),
    )
    specs = (P("dp", "mp"), P("dp", "mp")) + params
    return jax.shard_map(
        functools.partial(local, dp, mp), mesh=mesh, in_specs=specs, out_specs=specs, check_vma=False
    )
```

```python
import functools

import jax
import jax.numpy as jnp
from jax import lax
from jax.experimental import pallas as pl
from jax.experimental.pallas import tpu as pltpu
from jax.sharding import PartitionSpec as P

D = 1024
GROUP = 128
LEN = 2048
NDIM = 16
LANES = 128
SUB = D // LANES
EPS = 1e-05
TB = 128


def matmul(left, right):
    return jnp.dot(left, right, preferred_element_type=jnp.float32)


def matmul_tn(left, right):
    return lax.dot_general(
        left, right, (((0,), (0,)), ((), ())), preferred_element_type=jnp.float32
    )


def matmul_nt(left, right):
    return lax.dot_general(
        left, right, (((1,), (1,)), ((), ())), preferred_element_type=jnp.float32
    )


def to_rows(scratch, value):
    for part in range(SUB):
        scratch[pl.ds(part, TB, stride=SUB), :] = value[:, part * LANES : (part + 1) * LANES]


def from_rows(scratch):
    return jnp.concatenate(
        [scratch[pl.ds(part, TB, stride=SUB), :] for part in range(SUB)], axis=1
    )


def row(scratch, index):
    return scratch[pl.ds(pl.multiple_of(index * SUB, SUB), SUB), :]


def sds(shape, dtype=jnp.float32):
    return jax.ShapeDtypeStruct(shape, dtype)


def block(reverse=None):
    if reverse is None:
        return pl.BlockSpec((TB, D), lambda i: (i, 0))
    return pl.BlockSpec((TB, D), lambda i: (reverse - 1 - i, 0))


def whole(*shape):
    return pl.BlockSpec(shape, lambda i: (0,) * len(shape))


STATE = (NDIM, SUB, LANES)
STATES = (2 * NDIM, SUB, LANES)
ROWS = pltpu.VMEM((TB * SUB, LANES), jnp.float32)
PARAMS = pltpu.CompilerParams(vmem_limit_bytes=32 << 20)


ROWS_C = 256


def sigmoid(value):
    return 0.5 + 0.5 * jnp.tanh(0.5 * value)


def causal_probs(query, keys, head_scale):
    scores = matmul_nt(query, keys) * head_scale
    down = lax.broadcasted_iota(jnp.int32, scores.shape, 0)
    across = lax.broadcasted_iota(jnp.int32, scores.shape, 1)
    scores = jnp.where(down >= across, scores, -1e30)
    weights = jnp.exp(scores - jnp.max(scores, axis=1, keepdims=True))
    return weights / jnp.sum(weights, axis=1, keepdims=True)


def mixer_forward_kernel(
    xn_ref, xp_ref, x_ref, one_ref, shared_ref, qgain_ref, qbias_ref, kgain_ref,
    vpre_ref, gpre_ref, att_ref, hid_ref, act_ref, upd_ref, mid_ref, spre_ref,
):
    mp = one_ref.shape[0]
    narrow = D // mp
    wide = vpre_ref.shape[1] // mp
    base = 2 * (wide + narrow)
    groups = ROWS_C // GROUP
    xn, xp = xn_ref[...], xp_ref[...]
    shared_pre = matmul(xp, shared_ref[...])
    spre_ref[...] = shared_pre
    shared = shared_pre * sigmoid(shared_pre)
    query = (shared * qgain_ref[...] + qbias_ref[...]).astype(jnp.bfloat16)
    keys = (shared * kgain_ref[...]).astype(jnp.bfloat16)
    head_scale = shared.shape[1] ** (-0.5)
    probs = [
        causal_probs(
            query[g * GROUP : (g + 1) * GROUP], keys[g * GROUP : (g + 1) * GROUP], head_scale
        ).astype(jnp.bfloat16)
        for g in range(groups)
    ]
    attn_out = None
    for m in range(mp):
        span = slice(m * wide, (m + 1) * wide)
        value_pre = matmul(xn, one_ref[m, :, 0:wide])
        values = (value_pre * sigmoid(value_pre)).astype(jnp.bfloat16)
        vpre_ref[:, span] = value_pre.astype(jnp.bfloat16)
        gate_pre = matmul(xp, one_ref[m, :, wide : 2 * wide])
        gate = gate_pre * sigmoid(gate_pre)
        gpre_ref[:, span] = gate_pre.astype(jnp.bfloat16)
        attended = jnp.concatenate(
            [matmul(probs[g], values[g * GROUP : (g + 1) * GROUP]) for g in range(groups)], axis=0
        )
        att_ref[:, span] = attended.astype(jnp.bfloat16)
        hidden = (gate * attended).astype(jnp.bfloat16)
        hid_ref[:, span] = hidden
        term = jnp.concatenate(
            [matmul(hidden, one_ref[m, 0:wide, base:]), matmul(hidden, one_ref[m, wide:, base:])], axis=1
        )
        attn_out = term if attn_out is None else attn_out + term
    for m in range(mp):
        span = slice(m * narrow, (m + 1) * narrow)
        act = matmul(xp, one_ref[m, :, 2 * wide : 2 * wide + narrow]) + attn_out[:, span]
        upd = matmul(xp, one_ref[m, :, 2 * wide + narrow : base])
        update = sigmoid(upd)
        act_ref[:, span] = act.astype(jnp.bfloat16)
        upd_ref[:, span] = upd.astype(jnp.bfloat16)
        x = x_ref[:, span].astype(jnp.float32)
        mid_ref[:, span] = x + update * (act * sigmoid(act) - x)


def ffn_kernel(
    mid_ref, grad_ref, x_ref, act_ref, upd_ref, two_ref, gain_ref,
    layer_ref, ffn_ref, upper_ref, dup_ref, dact_ref, dupd_ref, dx_ref, gsum_ref,
):
    mp, _, total = two_ref.shape
    units = total - D
    sub = 512
    middle = mid_ref[...]
    grad = grad_ref[...]
    mean = jnp.mean(middle, axis=1, keepdims=True)
    power = jnp.mean(middle * middle, axis=1, keepdims=True)
    scale = lax.rsqrt(power - mean * mean + EPS)
    normed = (middle - mean) * scale
    gain = gain_ref[...]
    ffn_in = (normed * gain).astype(jnp.bfloat16)
    ffn_ref[...] = ffn_in
    down_out = None
    d_ffn = None
    for m in range(mp):
        for first in range(0, units, sub):
            columns = slice(m * units + first, m * units + first + sub)
            up_weights = two_ref[m, :, first : first + sub]
            down_weights = two_ref[m, first : first + sub, units:]
            up_pre = matmul(ffn_in, up_weights)
            logistic = sigmoid(up_pre)
            value = up_pre * logistic
            upper = value.astype(jnp.bfloat16)
            upper_ref[:, columns] = upper
            slope = logistic + value - value * logistic
            d_up = (matmul_nt(grad, down_weights) * slope).astype(jnp.bfloat16)
            dup_ref[:, columns] = d_up
            term = matmul(upper, down_weights)
            down_out = term if down_out is None else down_out + term
            term = matmul_nt(d_up, up_weights)
            d_ffn = term if d_ffn is None else d_ffn + term
    layer_ref[...] = (middle + down_out).astype(jnp.bfloat16)

    @pl.when(pl.program_id(0) == 0)
    def _():
        gsum_ref[...] = jnp.zeros_like(gsum_ref)

    gsum_ref[...] += jnp.sum(d_ffn * normed, axis=0, keepdims=True)
    scaled = d_ffn * gain
    first = jnp.mean(scaled, axis=1, keepdims=True)
    second = jnp.mean(scaled * normed, axis=1, keepdims=True)
    d_middle = grad.astype(jnp.float32) + scale * (scaled - first - normed * second)
    act = act_ref[...].astype(jnp.float32)
    update = sigmoid(upd_ref[...].astype(jnp.float32))
    logistic = sigmoid(act)
    value = act * logistic
    x = x_ref[...].astype(jnp.float32)
    d_update = d_middle * update
    dact_ref[...] = (d_update * (logistic + value - value * logistic)).astype(jnp.bfloat16)
    dupd_ref[...] = (d_update * (value - x) * (1.0 - update)).astype(jnp.bfloat16)
    dx_ref[...] = (d_middle - d_update).astype(jnp.bfloat16)


def mixer_backward_kernel(
    dact_ref, dupd_ref, vpre_ref, gpre_ref, att_ref, spre_ref, mix_ref, one_ref, shared_ref,
    qgain_ref, qbias_ref, kgain_ref,
    dv_ref, dg_ref, dshared_ref, dmix_ref, dxn_ref, sums_ref,
):
    mp = one_ref.shape[0]
    narrow = D // mp
    wide = vpre_ref.shape[1] // mp
    base = 2 * (wide + narrow)
    groups = ROWS_C // GROUP
    shared_pre = spre_ref[...]
    logistic = sigmoid(shared_pre)
    shared = shared_pre * logistic
    query = (shared * qgain_ref[...] + qbias_ref[...]).astype(jnp.bfloat16)
    keys = (shared * kgain_ref[...]).astype(jnp.bfloat16)
    head_scale = shared.shape[1] ** (-0.5)
    rows = [slice(g * GROUP, (g + 1) * GROUP) for g in range(groups)]
    probs = [causal_probs(query[rows[g]], keys[rows[g]], head_scale) for g in range(groups)]
    probs_low = [item.astype(jnp.bfloat16) for item in probs]
    d_act = dact_ref[...]
    d_probs = [None] * groups
    d_xp = None
    d_xn = None
    for m in range(mp):
        span = slice(m * wide, (m + 1) * wide)
        thin = slice(m * narrow, (m + 1) * narrow)
        d_hidden = matmul_nt(d_act[:, : D // 2], one_ref[m, 0:wide, base:]) + matmul_nt(
            d_act[:, D // 2 :], one_ref[m, wide:, base:]
        )
        gate_pre = gpre_ref[:, span].astype(jnp.float32)
        gate_log = sigmoid(gate_pre)
        gate = gate_pre * gate_log
        attended = att_ref[:, span].astype(jnp.float32)
        d_gate = (d_hidden * attended * (gate_log + gate - gate * gate_log)).astype(jnp.bfloat16)
        dg_ref[:, span] = d_gate
        d_att = (d_hidden * gate).astype(jnp.bfloat16)
        value_pre = vpre_ref[:, span].astype(jnp.float32)
        value_log = sigmoid(value_pre)
        value = value_pre * value_log
        values = value.astype(jnp.bfloat16)
        parts = []
        for g in range(groups):
            term = matmul_nt(d_att[rows[g]], values[rows[g]])
            d_probs[g] = term if d_probs[g] is None else d_probs[g] + term
            parts.append(matmul_tn(probs_low[g], d_att[rows[g]]))
        d_value = jnp.concatenate(parts, axis=0)
        d_value_pre = (d_value * (value_log + value - value * value_log)).astype(jnp.bfloat16)
        dv_ref[:, span] = d_value_pre
        term = (
            matmul_nt(d_gate, one_ref[m, :, wide : 2 * wide])
            + matmul_nt(d_act[:, thin], one_ref[m, :, 2 * wide : 2 * wide + narrow])
            + matmul_nt(dupd_ref[:, thin], one_ref[m, :, 2 * wide + narrow : base])
        )
        d_xp = term if d_xp is None else d_xp + term
        term = matmul_nt(d_value_pre, one_ref[m, :, 0:wide])
        d_xn = term if d_xn is None else d_xn + term
    dxn_ref[...] = d_xn.astype(jnp.bfloat16)
    d_query, d_keys = [], []
    for g in range(groups):
        d_scores = probs[g] * (d_probs[g] - jnp.sum(probs[g] * d_probs[g], axis=1, keepdims=True))
        low = d_scores.astype(jnp.bfloat16)
        d_query.append(matmul(low, keys[rows[g]]) * head_scale)
        d_keys.append(matmul_tn(low, query[rows[g]]) * head_scale)
    d_query = jnp.concatenate(d_query, axis=0)
    d_keys = jnp.concatenate(d_keys, axis=0)

    @pl.when(pl.program_id(0) == 0)
    def _():
        sums_ref[...] = jnp.zeros_like(sums_ref)

    sums_ref[0:1, :] += jnp.sum(d_query * shared, axis=0, keepdims=True)
    sums_ref[1:2, :] += jnp.sum(d_query, axis=0, keepdims=True)
    sums_ref[2:3, :] += jnp.sum(d_keys * shared, axis=0, keepdims=True)
    d_shared = (d_query * qgain_ref[...] + d_keys * kgain_ref[...]) * (
        logistic + shared - shared * logistic
    )
    d_shared = d_shared.astype(jnp.bfloat16)
    dshared_ref[...] = d_shared
    d_xp = d_xp + matmul_nt(d_shared, shared_ref[...])
    mix = mix_ref[...]
    mix_log = sigmoid(mix)
    mix_value = mix * mix_log
    dmix_ref[...] = d_xp * (mix_log + mix_value - mix_value * mix_log)


def mixer_weights_kernel(
    xn_ref, xp_ref, hid_ref, dact_all_ref, dv_ref, dg_ref, dact_ref, dupd_ref, dshared_ref,
    one_ref, shared_ref, xnt, xpt,
):
    wide, narrow = dv_ref.shape[1], dact_ref.shape[1]

    @pl.when(pl.program_id(0) == 0)
    def _():
        xnt[...] = xn_ref[...].T
        xpt[...] = xp_ref[...].T
        shared_ref[...] = matmul(xpt[...], dshared_ref[...]).astype(jnp.bfloat16)

    one_ref[0, :, 0:wide] = matmul(xnt[...], dv_ref[...]).astype(jnp.bfloat16)
    one_ref[0, :, wide : 2 * wide] = matmul(xpt[...], dg_ref[...]).astype(jnp.bfloat16)
    one_ref[0, :, 2 * wide : 2 * wide + narrow] = matmul(xpt[...], dact_ref[...]).astype(jnp.bfloat16)
    base = 2 * (wide + narrow)
    one_ref[0, :, 2 * wide + narrow : base] = matmul(xpt[...], dupd_ref[...]).astype(jnp.bfloat16)
    out = matmul_tn(hid_ref[...], dact_all_ref[...]).astype(jnp.bfloat16)
    one_ref[0, 0:wide, base:] = out[:, : D // 2]
    one_ref[0, wide:, base:] = out[:, D // 2 :]


def ffn_weights_kernel(ffn_ref, grad_ref, upper_ref, dup_ref, two_ref, fft):
    units = dup_ref.shape[1]

    @pl.when(pl.program_id(0) == 0)
    def _():
        fft[...] = ffn_ref[...].T

    two_ref[0, :, 0:units] = matmul(fft[...], dup_ref[...]).astype(jnp.bfloat16)
    two_ref[0, :, units:] = matmul_tn(upper_ref[...], grad_ref[...]).astype(jnp.bfloat16)


def held(*shape):
    return pl.BlockSpec(shape, lambda i: (0,) * len(shape), pipeline_mode=pl.Buffered(1))


def rows_block(width):
    return pl.BlockSpec((ROWS_C, width), lambda i: (i, 0))


BIG = pltpu.CompilerParams(vmem_limit_bytes=60 << 20)


def cost(flops, bytes_accessed):
    return pl.CostEstimate(flops=int(flops), transcendentals=0, bytes_accessed=int(bytes_accessed))


def ffn(middle, grad, x, act, upd, two, gain):
    count = x.shape[0]
    units = two.shape[0] * (two.shape[2] - D)
    low = jnp.bfloat16
    return pl.pallas_call(
        ffn_kernel,
        grid=(count // ROWS_C,),
        in_specs=[rows_block(D)] * 5 + [held(*two.shape), held(1, D)],
        out_specs=[rows_block(D)] * 2 + [rows_block(units)] * 2 + [rows_block(D)] * 3 + [whole(1, D)],
        out_shape=[sds((count, D), low)] * 2
        + [sds((count, units), low)] * 2
        + [sds((count, D), low)] * 3
        + [sds((1, D))],
        compiler_params=BIG,
        cost_estimate=cost(4 * count * two.size, 60 << 20),
        name="ffn",
    )(middle, grad, x, act, upd, two, gain)


def mixer_backward(d_act, d_upd, vpre, gpre, att, spre, mix, one, shared, qgain, qbias, kgain):
    count = d_act.shape[0]
    units = vpre.shape[1]
    z = shared.shape[1]
    low = jnp.bfloat16
    return pl.pallas_call(
        mixer_backward_kernel,
        grid=(count // ROWS_C,),
        in_specs=[rows_block(D)] * 2
        + [rows_block(units)] * 3
        + [rows_block(z), rows_block(D)]
        + [held(*one.shape), held(*shared.shape)]
        + [held(1, z)] * 3,
        out_specs=[rows_block(units)] * 2
        + [rows_block(z), rows_block(D), rows_block(D), whole(8, z)],
        out_shape=[sds((count, units), low)] * 2
        + [sds((count, z), low), sds((count, D)), sds((count, D), low), sds((8, z))],
        compiler_params=BIG,
        cost_estimate=cost(2 * count * (one.size + shared.size), 60 << 20),
        name="mixer_backward",
    )(d_act, d_upd, vpre, gpre, att, spre, mix, one, shared, qgain, qbias, kgain)


def mixer_weights(mp, xn, xp, hidden, d_act, d_value, d_gate, d_upd, d_shared):
    count = xn.shape[0]
    wide, narrow, z = d_value.shape[1] // mp, D // mp, d_shared.shape[1]
    low = jnp.bfloat16

    def part(width):
        return pl.BlockSpec((count, width), lambda i: (0, i))

    return pl.pallas_call(
        mixer_weights_kernel,
        grid=(mp,),
        in_specs=[held(count, D), held(count, D), part(wide), held(count, D)]
        + [part(wide), part(wide), part(narrow), part(narrow), held(count, z)],
        out_specs=[
            pl.BlockSpec((1, D, 2 * (wide + narrow) + D // 2), lambda i: (i, 0, 0)),
            whole(D, z),
        ],
        out_shape=[sds((mp, D, 2 * (wide + narrow) + D // 2), low), sds((D, z), low)],
        scratch_shapes=[pltpu.VMEM((D, count), low), pltpu.VMEM((D, count), low)],
        compiler_params=BIG,
        cost_estimate=cost(2 * count * D * mp * (3 * wide + 2 * narrow), 40 << 20),
        name="mixer_weights",
    )(xn, xp, hidden, d_act, d_value, d_gate, d_act, d_upd, d_shared)


def ffn_weights(mp, ffn_in, grad, upper, d_up):
    count = ffn_in.shape[0]
    units = upper.shape[1] // mp
    low = jnp.bfloat16

    def part(width):
        return pl.BlockSpec((count, width), lambda i: (0, i))

    return pl.pallas_call(
        ffn_weights_kernel,
        grid=(mp,),
        in_specs=[held(count, D), held(count, D), part(units), part(units)],
        out_specs=pl.BlockSpec((1, D, units + D), lambda i: (i, 0, 0)),
        out_shape=sds((mp, D, units + D), low),
        scratch_shapes=[pltpu.VMEM((D, count), low)],
        compiler_params=BIG,
        cost_estimate=cost(4 * count * D * mp * units, 40 << 20),
        name="ffn_weights",
    )(ffn_in, grad, upper, d_up)


MESH = pl.DeviceIdType.MESH


def rank_of(index, order):
    total = 0
    for place, bit in enumerate(order):
        total = total + lax.rem(lax.div(index, 1 << bit), 2) * (1 << place)
    return total


def flip(index, bit):
    low = lax.rem(lax.div(index, 1 << bit), 2)
    return index + (1 - 2 * low) * (1 << bit)


def orders_of(dp):
    bits = dp.bit_length() - 1
    inner = list(range(1, bits))
    return (inner + [0], inner[::-1] + [0])


def greet(dp, mp):
    me = lax.axis_index("dp")
    part = lax.axis_index("mp")
    bits = dp.bit_length() - 1
    barrier = pltpu.get_barrier_semaphore()
    for step in range(1, mp):
        pl.semaphore_signal(
            barrier, inc=1, device_id={"mp": lax.rem(part + step, mp)}, device_id_type=MESH
        )
    for bit in range(bits):
        pl.semaphore_signal(barrier, inc=1, device_id={"dp": flip(me, bit)}, device_id_type=MESH)
    pl.semaphore_wait(barrier, mp - 1 + bits)


def arrived(ref, sem):
    pltpu.make_async_copy(ref, ref, sem).wait()


def remote(src, dst, send_sem, recv_sem, axis, to):
    return pltpu.make_async_remote_copy(
        src_ref=src, dst_ref=dst, send_sem=send_sem, recv_sem=recv_sem,
        device_id={axis: to}, device_id_type=MESH,
    )


def span_of(index, size):
    return pl.ds(pl.multiple_of(index * size, size), size)


class Swap:
    def __init__(self, mp, src, dst, sems, back=False):
        self.mp, self.src, self.dst, self.back = mp, src, dst, back
        self.send, self.recv, self.own = sems
        self.part = lax.axis_index("mp")
        if back:
            self.rows, self.width = src.shape[0], dst.shape[1]
        else:
            self.rows, self.width = dst.shape[0], src.shape[1]

    def piece(self, index):
        if self.back:
            return self.src.at[:, span_of(index, self.width)]
        return self.src.at[span_of(index, self.rows), :]

    def place(self, index):
        if self.back:
            return self.dst.at[span_of(index, self.rows), :]
        return self.dst.at[:, span_of(index, self.width)]

    def local(self):
        return pltpu.make_async_copy(self.piece(self.part), self.place(self.part), self.own.at[0])

    def copies(self):
        for step in range(1, self.mp):
            to = lax.rem(self.part + step, self.mp)
            yield remote(
                self.piece(to), self.place(self.part),
                self.send.at[step], self.recv.at[self.part], "mp", to,
            )

    def start(self):
        self.local().start()
        for copy in self.copies():
            copy.start()

    def receive(self):
        self.local().wait()
        for step in range(1, self.mp):
            source = lax.rem(self.part + step, self.mp)
            arrived(self.place(source), self.recv.at[source])

    def close(self):
        for copy in self.copies():
            copy.wait_send()


class Gather:
    def __init__(self, dp, mp, src, dst, sems):
        self.dp, self.mp, self.src, self.dst = dp, mp, src, dst
        self.line_send, self.pass_send, self.line_recv, self.send, self.recv, self.own = sems
        self.me, self.part = lax.axis_index("dp"), lax.axis_index("mp")
        self.bits = dp.bit_length() - 1
        self.orders = orders_of(dp)

    def region(self, ref, half, index, held):
        total, width = ref.shape[0], ref.shape[1] // 2
        share = total // self.dp
        first = lax.div(rank_of(index, self.orders[half]), 1 << held) * (share << held)
        return ref.at[
            pl.ds(pl.multiple_of(first, share), share << held), half * width : (half + 1) * width
        ]

    def local(self):
        return pltpu.make_async_copy(self.src, self.dst.at[self.part], self.own.at[0])

    def first(self, up):
        to = self.part + 1 if up else self.part - 1
        for half in range(2):
            yield remote(
                self.region(self.src, half, self.me, 0),
                self.region(self.dst.at[self.part], half, self.me, 0),
                self.line_send.at[int(up), half], self.line_recv.at[self.part, half], "mp", to,
            )

    def passed(self, source):
        to = jnp.where(source < self.part, self.part + 1, self.part - 1)
        for half in range(2):
            held = self.region(self.dst.at[source], half, self.me, 0)
            yield remote(
                held, held, self.pass_send.at[source, half], self.line_recv.at[source, half], "mp", to
            )

    def passes(self, source):
        return jnp.logical_or(
            jnp.logical_and(source < self.part, self.part < self.mp - 1),
            jnp.logical_and(source > self.part, self.part > 0),
        )

    def doubled(self, source, stage):
        for half in range(2):
            held = self.region(self.dst.at[source], half, self.me, stage)
            yield remote(
                held, held, self.send.at[stage, source, half], self.recv.at[stage, source, half],
                "dp", flip(self.me, self.orders[half][stage]),
            )

    def source(self, step):
        mp, part = self.mp, self.part
        near = [lax.rem(part + 1, 2) + part - lax.rem(part, 2)]
        low = lax.div(part, mp // 2) == 0
        far = [jnp.where(low, mp // 2 + i, mp // 2 - 1 - i) for i in range(mp // 2)]
        return (near + far)[step]

    def start(self):
        for up in (True, False):

            @pl.when(self.part < self.mp - 1 if up else self.part > 0)
            def _(up=up):
                for copy in self.first(up):
                    copy.start()

        self.local().start()

    def advance(self, step, stage):
        source = self.source(step)
        for half in range(2):
            if stage == 0:
                came = self.region(self.dst.at[source], half, self.me, 0)
                arrived(came, self.line_recv.at[source, half])
            else:
                other = flip(self.me, self.orders[half][stage - 1])
                came = self.region(self.dst.at[source], half, other, stage - 1)
                arrived(came, self.recv.at[stage - 1, source, half])
        if stage == 0:

            @pl.when(self.passes(source))
            def _():
                for copy in self.passed(source):
                    copy.start()

        if stage < self.bits:
            for copy in self.doubled(source, stage):
                copy.start()

    def waves(self):
        return self.mp - 1 + self.bits

    def wave(self, number):
        for stage in range(self.bits, -1, -1):
            if 0 <= number - stage < self.mp - 1:
                self.advance(number - stage, stage)

    def close(self):
        self.local().wait()
        for up in (True, False):

            @pl.when(self.part < self.mp - 1 if up else self.part > 0)
            def _(up=up):
                for copy in self.first(up):
                    copy.wait_send()

        for step in range(self.mp - 1):
            source = self.source(step)

            @pl.when(self.passes(source))
            def _(source=source):
                for copy in self.passed(source):
                    copy.wait_send()

            for stage in range(self.bits):
                for copy in self.doubled(source, stage):
                    copy.wait_send()


def swap_sems(mp):
    dma = pltpu.SemaphoreType.DMA
    return [dma((mp,)), dma((mp,)), dma((1,))]


def gather_sems(dp, mp):
    dma = pltpu.SemaphoreType.DMA
    bits = dp.bit_length() - 1
    return [dma((2, 2)), dma((mp, 2)), dma((mp, 2)), dma((bits, mp, 2)), dma((bits, mp, 2)), dma((1,))]


HBM = pl.BlockSpec(memory_space=pl.ANY)


def opening_kernel(dp, mp, small_ref, pack_ref, tok_ref, small_out, full_ref, rows_ref, *sems):
    swap = Swap(mp, tok_ref, rows_ref, sems[0:3])
    tiny = Swap(mp, small_ref, small_out, sems[3:6], back=True)
    plan = Gather(dp, mp, pack_ref, full_ref, sems[6:12])
    greet(dp, mp)
    tiny.start()
    plan.start()
    for number in range(plan.waves()):
        plan.wave(number)
        if number == mp - 2:
            swap.start()
    for item in (tiny, swap):
        item.receive()
        item.close()
    plan.close()


def opening(dp, mp, small, pack, tokens):
    return pl.pallas_call(
        functools.partial(opening_kernel, dp, mp),
        in_specs=[HBM] * 3,
        out_specs=[HBM] * 3,
        out_shape=[
            sds((mp * small.shape[0], small.shape[1] // mp)),
            sds((mp,) + pack.shape, pack.dtype),
            sds((tokens.shape[0] // mp, tokens.shape[1] * mp), tokens.dtype),
        ],
        scratch_shapes=swap_sems(mp) * 2 + gather_sems(dp, mp),
        compiler_params=pltpu.CompilerParams(
            collective_id=0, has_side_effects=True, vmem_limit_bytes=4 << 20
        ),
        name="opening",
    )(small, pack, tokens)


def forward_kernel(
    dp, mp, span,
    x_ref, gain_ref, keep_ref, weight_ref, omega_ref,
    one_ref, shared_ref, qgain_ref, qbias_ref, kgain_ref, pack_ref, cot_ref,
    xn_ref, xp_ref, mix_ref, starts_ref,
    vpre_ref, gpre_ref, att_ref, hid_ref, act_ref, upd_ref, mid_ref, spre_ref,
    full_ref, grad_ref,
    xn_all, rows, outs, ends, starts, state_ref, carry_send, carry_recv, *sems,
):
    index = pl.program_id(0)
    steps = pl.num_programs(0) // 2
    part = lax.axis_index("mp")
    swap = Swap(mp, cot_ref, grad_ref, sems[0:3])
    plan = Gather(dp, mp, pack_ref, full_ref, sems[3:9])
    gives = lax.rem(part + 1, span) != 0
    takes = lax.rem(part, span) != 0

    def carry():
        return remote(ends, starts, carry_send.at[0], carry_recv.at[0], "mp", part + 1)

    @pl.when(index == 0)
    def _():
        greet(dp, mp)
        plan.start()
        ends[...] = jnp.zeros_like(ends)

    @pl.when(index < steps)
    def _():
        keep = [keep_ref[j] for j in range(NDIM)]
        for piece in range(ROWS_C // TB):
            here = slice(piece * TB, (piece + 1) * TB)
            x = x_ref[here, :].astype(jnp.float32)
            mean = jnp.mean(x, axis=1, keepdims=True)
            power = jnp.mean(x * x, axis=1, keepdims=True)
            scale = lax.rsqrt(power - mean * mean + EPS)
            xn = ((x - mean) * scale * gain_ref[...]).astype(jnp.bfloat16)
            xn_ref[here, :] = xn
            xn_all[pl.ds(pl.multiple_of(index * ROWS_C + piece * TB, TB), TB), :] = xn
            to_rows(rows, xn.astype(jnp.float32))

            def step(t, carried):
                state, slope = carried
                now = row(rows, t)
                slope = tuple(keep[j] * slope[j] + state[j] for j in range(NDIM))
                state = tuple(keep[j] * state[j] + now for j in range(NDIM))
                return (state, slope)

            state = tuple(ends[j] for j in range(NDIM))
            slope = tuple(ends[NDIM + j] for j in range(NDIM))
            state, slope = lax.fori_loop(0, TB, step, (state, slope), unroll=4)
            for j in range(NDIM):
                ends[j] = state[j]
                ends[NDIM + j] = slope[j]

    @pl.when(index == steps - 1)
    def _():
        @pl.when(gives)
        def _():
            carry().start()

        plan.wave(0)

    @pl.when(index == steps)
    def _():
        @pl.when(jnp.logical_not(takes))
        def _():
            starts[...] = jnp.zeros_like(starts)

        @pl.when(takes)
        def _():
            arrived(starts, carry_recv.at[0])

        @pl.when(gives)
        def _():
            carry().wait_send()

        for j in range(NDIM):
            state_ref[j] = starts[j]
        starts_ref[...] = starts[...]

    @pl.when(index >= steps)
    def _():
        for piece in range(ROWS_C // TB):
            here = slice(piece * TB, (piece + 1) * TB)
            xn = xn_all[
                pl.ds(pl.multiple_of((index - steps) * ROWS_C + piece * TB, TB), TB), :
            ].astype(jnp.float32)
            to_rows(rows, xn)
            keep = [keep_ref[j] for j in range(NDIM)]

            def step(t, state):
                now = row(rows, t)
                state = tuple(keep[j] * state[j] + now for j in range(NDIM))
                terms = [weight_ref[j] * state[j] for j in range(NDIM)]
                while len(terms) > 1:
                    terms = [a + b for a, b in zip(terms[::2], terms[1::2])]
                outs[pl.ds(pl.multiple_of(t * SUB, SUB), SUB), :] = terms[0]
                return state

            state = lax.fori_loop(0, TB, step, tuple(state_ref[j] for j in range(NDIM)), unroll=4)
            for j in range(NDIM):
                state_ref[j] = state[j]
            mix = from_rows(outs) + omega_ref[...] * xn
            mix_ref[here, :] = mix
            xp_ref[here, :] = (mix * sigmoid(mix)).astype(jnp.bfloat16)

        xn_block = xn_all.at[pl.ds(pl.multiple_of((index - steps) * ROWS_C, ROWS_C), ROWS_C), :]
        mixer_forward_kernel(
            xn_block, xp_ref, x_ref, one_ref, shared_ref, qgain_ref, qbias_ref, kgain_ref,
            vpre_ref, gpre_ref, att_ref, hid_ref, act_ref, upd_ref, mid_ref, spre_ref,
        )

    for number in range(1, plan.waves()):
        at = jnp.minimum(steps + number - 1, 2 * steps - 1)

        @pl.when(index == at)
        def _(number=number):
            plan.wave(number)
            if number == mp - 2:
                swap.start()

    @pl.when(index == 2 * steps - 1)
    def _():
        swap.receive()
        swap.close()
        plan.close()


def forward(dp, mp, span, units, x, gain, keep, weight, omega, one, shared, vectors, pack, cotangent):
    count = x.shape[0]
    steps = count // ROWS_C
    z = shared.shape[1]
    low = jnp.bfloat16
    early = pl.BlockSpec((ROWS_C, D), lambda i: (jnp.minimum(i, steps - 1), 0))

    def late(width):
        return pl.BlockSpec((ROWS_C, width), lambda i: (jnp.maximum(i - steps, 0), 0))

    dma = pltpu.SemaphoreType.DMA
    return pl.pallas_call(
        functools.partial(forward_kernel, dp, mp, span),
        grid=(2 * steps,),
        in_specs=[pl.BlockSpec((ROWS_C, D), lambda i: (lax.rem(i, steps), 0))]
        + [held(1, D), held(*STATE), held(*STATE), held(1, D)]
        + [held(*one.shape), held(*shared.shape)]
        + [held(1, z)] * 3
        + [HBM] * 2,
        out_specs=[early, late(D), late(D), whole(*STATES)]
        + [late(units)] * 4
        + [late(D)] * 3
        + [late(z)]
        + [HBM] * 2,
        out_shape=[sds((count, D), low), sds((count, D), low), sds((count, D)), sds(STATES)]
        + [sds((count, units), low)] * 4
        + [sds((count, D), low)] * 2
        + [sds((count, D)), sds((count, z))]
        + [sds((mp,) + pack.shape, low), sds((count, D), low)],
        scratch_shapes=[
            pltpu.VMEM((count, D), low), ROWS, ROWS,
            pltpu.VMEM(STATES, jnp.float32), pltpu.VMEM(STATES, jnp.float32),
            pltpu.VMEM(STATE, jnp.float32), dma((1,)), dma((1,)),
        ]
        + swap_sems(mp)
        + gather_sems(dp, mp),
        compiler_params=pltpu.CompilerParams(
            collective_id=1, has_side_effects=True, vmem_limit_bytes=60 << 20
        ),
        name="forward",
    )(x, gain, keep, weight, omega, one, shared, *vectors, pack, cotangent)


def add_rows(acc, first, other, count):
    chunk = min(count, 32)

    def step(index, _):
        there = pl.ds(pl.multiple_of(first + index * chunk, chunk), chunk)
        here = pl.ds(pl.multiple_of(index * chunk, chunk), chunk)
        total = acc[there, :].astype(jnp.float32) + other[here, :].astype(jnp.float32)
        acc[there, :] = total.astype(jnp.bfloat16)
        return 0

    lax.fori_loop(0, count // chunk, step, 0)


class Reduce:
    def __init__(self, dp, mp, src, out, stage, recvs, lines, last, sems, waits):
        self.dp, self.mp, self.src, self.out, self.stage = dp, mp, src, out, stage
        self.recvs, self.lines, self.last, self.waits = recvs, lines, last, waits
        (
            self.load, self.send, self.recv, self.line_send, self.line_recv,
            self.last_send, self.last_recv, self.ring_send, self.ring_recv, self.own,
        ) = sems
        self.me, self.part = lax.axis_index("dp"), lax.axis_index("mp")
        self.bits = dp.bit_length() - 1
        self.orders = orders_of(dp)
        self.share = src.shape[1] // dp
        self.width = src.shape[2] // 2

    def shard(self, i):
        near, far = flip(self.part, 0), flip(self.part, 1)
        return (near, flip(far, 0), far, self.part)[i]

    def rank(self, half, index):
        return rank_of(index, self.orders[half])

    def push(self, copy):
        copy.start()
        self.waits.append(copy.wait_send)

    def begin(self, i, slot):
        m = self.shard(i)
        count = self.share << (self.bits - 1)
        for half in range(2):
            columns = slice(half * self.width, (half + 1) * self.width)
            other = flip(self.me, self.orders[half][self.bits - 1])

            def rows(index):
                return span_of(lax.div(self.rank(half, index), 1 << (self.bits - 1)), count)

            self.push(
                remote(
                    self.src.at[m, rows(other), columns], self.recvs[0].at[m, half],
                    self.send.at[0, i, half], self.recv.at[0, m, half], "dp", other,
                )
            )
            pltpu.make_async_copy(
                self.src.at[m, rows(self.me), columns], self.stage.at[slot, half],
                self.load.at[slot, half],
            ).start()

    def offset(self, half, index, stage):
        low = lax.rem(self.rank(half, index), 1 << (self.bits - 1))
        left = self.bits - 1 - stage
        return lax.div(low, 1 << left) * (self.share << left)

    def fold(self, i, stage, slot):
        m = self.shard(i)
        count = self.share << (self.bits - 1 - stage)
        for half in range(2):
            acc = self.recvs[0].at[m, half]
            came = self.recvs[stage].at[m, half]
            arrived(came, self.recv.at[stage, m, half])
            if stage == 0:
                own = self.stage.at[slot, half]
                arrived(own, self.load.at[slot, half])
                add_rows(acc, 0, own, count)
            else:
                add_rows(acc, self.offset(half, self.me, stage), came, count)
            if stage < self.bits - 1:
                other = flip(self.me, self.orders[half][self.bits - 2 - stage])
                give = self.offset(half, other, stage + 1)
                self.push(
                    remote(
                        acc.at[pl.ds(pl.multiple_of(give, self.share), count // 2), :],
                        self.recvs[stage + 1].at[m, half],
                        self.send.at[stage + 1, i, half], self.recv.at[stage + 1, m, half],
                        "dp", other,
                    )
                )
                continue
            first = self.offset(half, self.me, stage)
            mine = acc.at[pl.ds(pl.multiple_of(first, self.share), self.share), :]
            if i >= 2:
                came = self.lines.at[m, half]
                arrived(came, self.line_recv.at[m, half])
                add_rows(acc, first, came, self.share)
            if i < 2:
                self.push(
                    remote(
                        mine, self.lines.at[m, half],
                        self.line_send.at[i, half], self.line_recv.at[m, half],
                        "mp", flip(self.part, 0),
                    )
                )
            elif i == 2:
                self.push(
                    remote(
                        mine, self.last.at[half], self.last_send.at[half], self.last_recv.at[half],
                        "mp", flip(self.part, 1),
                    )
                )
            else:
                came = self.last.at[half]
                arrived(came, self.last_recv.at[half])
                add_rows(acc, first, came, self.share)
                pltpu.make_async_copy(mine, self.rows_at(half, self.me, 0), self.own.at[half]).start()

    def rows_at(self, half, index, stage):
        first = lax.div(self.rank(half, index), 1 << stage) * (self.share << stage)
        return self.out.at[
            pl.ds(pl.multiple_of(first, self.share), self.share << stage),
            half * self.width : (half + 1) * self.width,
        ]

    def spread(self, stage):
        for half in range(2):
            mine = self.rows_at(half, self.me, stage)
            if stage == 0:
                arrived(mine, self.own.at[half])
            else:
                other = flip(self.me, self.orders[half][stage - 1])
                arrived(self.rows_at(half, other, stage - 1), self.ring_recv.at[stage - 1, half])
            if stage < self.bits:
                self.push(
                    remote(
                        mine, mine, self.ring_send.at[stage, half], self.ring_recv.at[stage, half],
                        "dp", flip(self.me, self.orders[half][stage]),
                    )
                )


def reduce_sems(dp, mp):
    dma = pltpu.SemaphoreType.DMA
    bits = dp.bit_length() - 1
    return [
        dma((bits, mp, 2)), dma((bits, mp, 2)), dma((2, 2)), dma((mp, 2)),
        dma((2,)), dma((2,)), dma((bits, 2)), dma((bits, 2)), dma((2,)),
    ]


class Tiny:
    def __init__(self, dp, mp, piece, line, ring, came, sems, waits):
        self.dp, self.mp, self.piece, self.waits = dp, mp, piece, waits
        self.line, self.ring, self.came = line, ring, came
        self.send, self.recv, self.ring_send, self.ring_recv = sems
        self.me, self.part = lax.axis_index("dp"), lax.axis_index("mp")
        self.bits = dp.bit_length() - 1

    def push(self, copy):
        copy.start()
        self.waits.append(copy.wait_send)

    def start(self):
        for step in range(1, self.mp):
            to = lax.rem(self.part + step, self.mp)
            self.push(
                remote(
                    self.piece(to), self.line.at[self.part],
                    self.send.at[step], self.recv.at[self.part], "mp", to,
                )
            )

    def fold(self, stage):
        if stage == 0:
            total = self.piece(self.part)[...].astype(jnp.float32)
            for step in range(1, self.mp):
                source = lax.rem(self.part + step, self.mp)
                arrived(self.line.at[source], self.recv.at[source])
                total = total + self.line[source].astype(jnp.float32)
        else:
            arrived(self.came.at[stage - 1], self.ring_recv.at[stage - 1])
            total = self.ring[stage - 1] + self.came[stage - 1]
        self.ring[stage] = total
        if stage < self.bits:
            self.push(
                remote(
                    self.ring.at[stage], self.came.at[stage],
                    self.ring_send.at[stage], self.ring_recv.at[stage],
                    "dp", flip(self.me, stage),
                )
            )


def tiny_sems(dp, mp):
    dma = pltpu.SemaphoreType.DMA
    bits = dp.bit_length() - 1
    return [dma((mp,)), dma((mp,)), dma((bits,)), dma((bits,))]


FEATURES = 40


def closing_kernel(
    dp, mp, span,
    one_ref, two_ref, layer_ref, grad_ref, xn_ref, x_ref, normed_ref, direct_ref, shared_ref, vector_ref,
    keep_ref, weight_ref, gain_ref, omega_ref, ffn_ref, starts_ref,
    one_out, two_out, layer_out, token_out, feat_out, shared_out, vector_out,
    stage, *refs,
):
    bits = dp.bit_length() - 1
    me, part = lax.axis_index("dp"), lax.axis_index("mp")
    waits = []
    taken = 0

    def take(count):
        nonlocal taken
        taken += count
        return refs[taken - count : taken]

    recvs = [take(bits), take(bits)]
    lines = take(2)
    last = take(2)
    grad, xn, x, normed_part, direct, tokens, rows, outs, states, ahead, sums, feat = take(12)
    shared, shared_line, shared_ring, shared_came, shared_low = take(5)
    feat_line, feat_ring, feat_came = take(3)
    vector, vector_line, vector_ring, vector_came = take(4)
    (load_sem,) = take(1)
    (in_sem,) = take(1)
    carry_send, carry_recv = take(2)
    spread_send, spread_recv, spread_own = take(3)
    packs = [
        Reduce(dp, mp, src, out, stage, recvs[i], lines[i], last[i], (load_sem,) + take(9), waits)
        for i, (src, out) in enumerate(((two_ref, two_out), (one_ref, one_out)))
    ]
    layer = Swap(mp, layer_ref, layer_out, take(3), back=True)
    token = Swap(mp, tokens, token_out, take(3), back=True)
    quarter = shared.shape[0] // mp
    columns = feat.shape[1] // mp
    tiny_shared = Tiny(
        dp, mp, lambda m: shared.at[span_of(m, quarter), :],
        shared_line, shared_ring, shared_came, take(4), waits,
    )
    tiny_vector = Tiny(
        dp, mp, lambda m: vector, vector_line, vector_ring, vector_came, take(4), waits
    )
    tiny_feat = Tiny(
        dp, mp, lambda m: feat.at[:, span_of(m, columns)],
        feat_line, feat_ring, feat_came, take(4), waits,
    )
    loads = [
        pltpu.make_async_copy(src, dst, in_sem.at[i])
        for i, (src, dst) in enumerate(
            (
                (grad_ref, grad), (xn_ref, xn), (x_ref, x), (normed_ref, normed_part),
                (direct_ref, direct), (shared_ref, shared), (vector_ref, vector),
            )
        )
    ]
    count = grad.shape[0]
    blocks = count // TB
    keep = lambda dims: [keep_ref[j] for j in dims]
    every = range(NDIM)
    gives = lax.rem(part, span) != 0
    takes = lax.rem(part + 1, span) != 0

    def carry():
        return remote(outs.at[0 : NDIM * SUB, :], ahead, carry_send.at[0], carry_recv.at[0], "mp", part - 1)

    def slot_of(j):
        return slice(j * SUB, (j + 1) * SUB)

    def adjoint():
        loads[0].wait()
        kept = keep(every)

        def block_step(number, state):
            first = pl.multiple_of((blocks - 1 - number) * TB, TB)
            to_rows(rows, grad[pl.ds(first, TB), :])

            def step(t, state):
                now = row(rows, TB - 1 - t)
                return tuple(kept[j] * state[j] + now for j in every)

            return lax.fori_loop(0, TB, step, state, unroll=4)

        zero = jnp.zeros((SUB, LANES), jnp.float32)
        state = lax.fori_loop(0, blocks, block_step, tuple(zero for _ in every))
        for j in every:
            outs[slot_of(j), :] = state[j]

        @pl.when(gives)
        def _():
            carry().start()

        for j in range(2 * NDIM):
            states[j] = starts_ref[j]
        sums[...] = jnp.zeros_like(sums)
        feat[...] = jnp.zeros_like(feat)
        feat[34:35, :] = ffn_ref[...]
        loads[1].wait()

    def params(low, high):
        half = NDIM // 2

        def block_step(number, _):
            first = pl.multiple_of(number * TB, TB)
            now_xn = xn[pl.ds(first, TB), :].astype(jnp.float32)
            now_grad = grad[pl.ds(first, TB), :]
            to_rows(rows, now_xn)
            for piece in range(SUB):
                turned[pl.ds(piece, TB, stride=SUB), :] = now_grad[:, piece * LANES : (piece + 1) * LANES]
            feat[32:33, :] += jnp.sum(now_grad * now_xn, axis=0, keepdims=True)
            for start in (0, half):
                dims = range(start, start + half)
                kept = keep(dims)

                def step(t, carried):
                    state, slope, weight_sum, keep_sum = carried
                    now = row(rows, t)
                    grad_now = row(turned, t)
                    slope = tuple(kept[j] * slope[j] + state[j] for j in range(half))
                    state = tuple(kept[j] * state[j] + now for j in range(half))
                    weight_sum = tuple(weight_sum[j] + grad_now * state[j] for j in range(half))
                    keep_sum = tuple(keep_sum[j] + grad_now * slope[j] for j in range(half))
                    return (state, slope, weight_sum, keep_sum)

                carried = (
                    tuple(states[j] for j in dims),
                    tuple(states[NDIM + j] for j in dims),
                    tuple(sums[slot_of(j), :] for j in dims),
                    tuple(sums[slot_of(NDIM + j), :] for j in dims),
                )
                state, slope, weight_sum, keep_sum = lax.fori_loop(0, TB, step, carried, unroll=4)
                for place, j in enumerate(dims):
                    states[j] = state[place]
                    states[NDIM + j] = slope[place]
                    sums[slot_of(j), :] = weight_sum[place]
                    sums[slot_of(NDIM + j), :] = keep_sum[place]
            return 0

        lax.fori_loop(low, high, block_step, 0)

    def meet():
        @pl.when(gives)
        def _():
            carry().wait_send()

        @pl.when(jnp.logical_not(takes))
        def _():
            ahead[...] = jnp.zeros_like(ahead)

        @pl.when(takes)
        def _():
            arrived(ahead, carry_recv.at[0])

        for copy in loads[2:5]:
            copy.wait()

    def token_rows(low, high):
        kept = keep(every)

        def block_step(number, state):
            there = pl.ds(pl.multiple_of((blocks - 1 - number) * TB, TB), TB)
            now_grad = grad[there, :]
            to_rows(rows, now_grad)

            def step(t, state):
                place = TB - 1 - t
                now = row(rows, place)
                state = tuple(kept[j] * state[j] + now for j in every)
                terms = [weight_ref[j] * state[j] for j in every]
                while len(terms) > 1:
                    terms = [a + b for a, b in zip(terms[::2], terms[1::2])]
                outs[pl.ds(pl.multiple_of(place * SUB, SUB), SUB), :] = terms[0]
                return state

            state = lax.fori_loop(0, TB, step, state, unroll=4)
            d_xn = from_rows(outs) + now_grad * omega_ref[...]
            d_xn = d_xn + normed_part[there, :].astype(jnp.float32)
            now_x = x[there, :].astype(jnp.float32)
            mean = jnp.mean(now_x, axis=1, keepdims=True)
            power = jnp.mean(now_x * now_x, axis=1, keepdims=True)
            scale = lax.rsqrt(power - mean * mean + EPS)
            normed = (now_x - mean) * scale
            feat[33:34, :] += jnp.sum(d_xn * normed, axis=0, keepdims=True)
            scaled = d_xn * gain_ref[...]
            first = jnp.mean(scaled, axis=1, keepdims=True)
            second = jnp.mean(scaled * normed, axis=1, keepdims=True)
            back = scale * (scaled - first - normed * second)
            tokens[there, :] = (direct[there, :].astype(jnp.float32) + back).astype(jnp.bfloat16)
            return state

        state = tuple(ahead[slot_of(j), :] for j in every)
        state = lax.fori_loop(low, high, block_step, state)
        for j in every:
            ahead[slot_of(j), :] = state[j]

    def gathered():
        for piece in range(SUB):
            feat[0 : 2 * NDIM, piece * LANES : (piece + 1) * LANES] = sums[
                pl.ds(piece, 2 * NDIM, stride=SUB), :
            ]
        token.start()
        tiny_feat.start()

    def shared_back():
        low = shared_ring[bits].astype(jnp.bfloat16)
        shared_low[...] = low
        there = shared_out.at[span_of(part, quarter), :]
        pltpu.make_async_copy(shared_low, there, spread_own.at[0]).start()
        for step in range(1, mp):
            to = lax.rem(part + step, mp)
            copy = remote(shared_low, there, spread_send.at[step], spread_recv.at[part], "mp", to)
            copy.start()
            waits.append(copy.wait_send)

    (turned,) = take(1)

    greet(dp, mp)
    for copy in loads:
        copy.start()
    layer.start()
    work = {
        0: [adjoint],
        1: [lambda: params(0, blocks // 2)],
        2: [lambda: params(blocks // 2, blocks)],
        3: [meet, lambda: token_rows(0, blocks // 2)],
        4: [lambda: token_rows(blocks // 2, blocks), gathered],
    }
    jobs = [(pack, i) for pack in packs for i in range(mp)]
    finals = {}
    for wave in range(len(jobs) + bits + bits + 2):
        for stage_number in range(bits - 1, -1, -1):
            number = wave - stage_number - 1
            if 0 <= number < len(jobs):
                pack, i = jobs[number]
                pack.fold(i, stage_number, number % 2)
                if stage_number == bits - 1 and i == mp - 1:
                    for step in range(bits + 1):
                        finals.setdefault(wave + step, []).append((pack, step))
        if wave < len(jobs):
            jobs[wave][0].begin(jobs[wave][1], wave % 2)
        for pack, step in finals.get(wave, []):
            pack.spread(step)
        for item in work.get(wave, []):
            item()
        if wave == 1:
            loads[5].wait()
            loads[6].wait()
            tiny_shared.start()
            tiny_vector.start()
        for item, first in ((tiny_shared, 3), (tiny_vector, 3), (tiny_feat, 7)):
            if 0 <= wave - first <= bits:
                item.fold(wave - first)
        if wave == 3 + bits:
            shared_back()
            vector_out[...] = vector_ring[bits]
        if wave == 7 + bits:
            feat_out[...] = feat_ring[bits]
    arrived(shared_low, spread_own.at[0])
    for step in range(1, mp):
        source = lax.rem(part + step, mp)
        arrived(shared_out.at[span_of(source, quarter), :], spread_recv.at[source])
    for item in (layer, token):
        item.receive()
        item.close()
    for wait in waits:
        wait()


def closing(dp, mp, span, packs, layer_rows, inputs, shared, vector, params, starts):
    one, two = packs
    low, full = jnp.bfloat16, jnp.float32
    bits = dp.bit_length() - 1
    dma = pltpu.SemaphoreType.DMA
    count = layer_rows.shape[0]
    _, total, width = one.shape
    z = shared.shape[1]
    quarter, columns = D // mp, D // mp

    def vmem(*shape, dtype=full):
        return pltpu.VMEM(shape, dtype)

    scratch = [vmem(2, 2, total // 2, width // 2, dtype=low)]
    for _ in range(2):
        scratch += [vmem(mp, 2, total >> (i + 1), width // 2, dtype=low) for i in range(bits)]
    scratch += [vmem(mp, 2, total // dp, width // 2, dtype=low)] * 2
    scratch += [vmem(2, total // dp, width // 2, dtype=low)] * 2
    scratch += [vmem(count, D)] + [vmem(count, D, dtype=low)] * 5
    scratch += [ROWS, ROWS, pltpu.VMEM(STATES, full), vmem(NDIM * SUB, LANES)]
    scratch += [vmem(2 * NDIM * SUB, LANES), vmem(FEATURES, D)]
    scratch += [
        vmem(D, z, dtype=low), vmem(mp, quarter, z, dtype=low), vmem(bits + 1, quarter, z),
        vmem(bits, quarter, z), vmem(quarter, z, dtype=low),
    ]
    scratch += [vmem(mp, FEATURES, columns), vmem(bits + 1, FEATURES, columns), vmem(bits, FEATURES, columns)]
    scratch += [vmem(8, z), vmem(mp, 8, z), vmem(bits + 1, 8, z), vmem(bits, 8, z)]
    scratch += [dma((2, 2)), dma((7,)), dma((1,)), dma((1,)), dma((mp,)), dma((mp,)), dma((1,))]
    scratch += reduce_sems(dp, mp) * 2 + swap_sems(mp) * 2 + tiny_sems(dp, mp) * 3
    scratch += [ROWS]
    near = pl.BlockSpec(memory_space=pltpu.VMEM)
    return pl.pallas_call(
        functools.partial(closing_kernel, dp, mp, span),
        in_specs=[HBM] * 10 + [near] * 6,
        out_specs=[HBM] * 4 + [near, HBM, near],
        out_shape=[
            sds((total, width), low), sds((total, width), low),
            sds((count * mp, D // mp), low), sds((count * mp, D // mp), low),
            sds((FEATURES, columns)), sds((D, z), low), sds((8, z)),
        ],
        scratch_shapes=scratch,
        compiler_params=pltpu.CompilerParams(
            collective_id=2, has_side_effects=True, vmem_limit_bytes=61 << 20
        ),
        name="closing",
    )(one, two, layer_rows, *inputs, shared, vector, *params, starts)


def local(
    dp,
    mp,
    tokens,
    cotangent,
    norm_gain,
    ema_delta,
    ema_alpha,
    ema_beta,
    ema_eta,
    ema_omega,
    shared_proj,
    query_gain,
    query_bias,
    key_gain,
    value_proj,
    gate_proj,
    mixer_proj,
    update_proj,
    output_proj,
    ffn_gain,
    up_proj,
    down_proj,
):
    width = tokens.shape[1]
    count = tokens.shape[0] // mp
    span = LEN // count
    small = jnp.concatenate(
        [
            ema_delta, ema_alpha, ema_beta, ema_eta,
            norm_gain[:, None], ema_omega[:, None], ffn_gain[:, None],
        ],
        axis=1,
    ).T
    lines = small.shape[0]
    small = jnp.pad(small, ((0, -lines % 8), (0, 0)))
    folded = jnp.concatenate([output_proj[:, : D // 2], output_proj[:, D // 2 :]], axis=0)
    pack_one = jnp.concatenate([value_proj, gate_proj, mixer_proj, update_proj, folded], axis=1)
    pack_two = jnp.concatenate([up_proj, down_proj], axis=1)
    small, one, x_low = opening(dp, mp, jnp.tile(small, (1, mp)), pack_one, tokens)
    small = small.reshape(mp, -1, width).transpose(1, 0, 2).reshape(-1, D)
    delta, alpha, beta, eta = (small[NDIM * i : NDIM * (i + 1)] for i in range(4))
    gain = small[4 * NDIM : 4 * NDIM + 1]
    omega = small[4 * NDIM + 1 : 4 * NDIM + 2]
    gain_two = small[4 * NDIM + 2 : 4 * NDIM + 3]
    rate = jax.nn.sigmoid(delta)
    damp = jax.nn.sigmoid(alpha)
    keep = (1.0 - rate * damp).reshape(STATE)
    weight = (rate * beta * eta).reshape(STATE)

    vectors = (query_gain[None], query_bias[None], key_gain[None])
    wide, narrow = value_proj.shape[1], mixer_proj.shape[1]
    (
        xn, xp, mix_pre, starts, vpre, gpre, att, hidden, act_pre, upd_pre, middle, spre, two, grad_out,
    ) = forward(
        dp, mp, span, mp * wide, x_low, gain, keep, weight, omega, one, shared_proj, vectors,
        pack_two, cotangent,
    )
    layer_rows, ffn_in, upper, d_up, d_act, d_upd, d_inputs, ffn_part = ffn(
        middle, grad_out, x_low, act_pre, upd_pre, two, gain_two
    )
    two_grad = ffn_weights(mp, ffn_in, grad_out, upper, d_up)
    d_value, d_gate, d_shared, d_mix_pre, normed_part, vector_sums = mixer_backward(
        d_act, d_upd, vpre, gpre, att, spre, mix_pre, one, shared_proj, *vectors
    )
    one_grad, shared_part = mixer_weights(
        mp, xn, xp, hidden, d_act, d_value, d_gate, d_upd, d_shared
    )

    one_grad, two_grad, layer_out, token_grad, feature, shared_grad, vector_sums = closing(
        dp, mp, span, (one_grad, two_grad), layer_rows,
        (d_mix_pre, xn, x_low, normed_part, d_inputs), shared_part, vector_sums,
        (keep, weight, gain, omega, ffn_part), starts,
    )
    up_grad = two_grad[:, : up_proj.shape[1]].astype(jnp.float32)
    down_grad = two_grad[:, up_proj.shape[1] :].astype(jnp.float32)
    base = 2 * (wide + narrow)
    value_grad = one_grad[:, :wide].astype(jnp.float32)
    gate_grad = one_grad[:, wide : 2 * wide].astype(jnp.float32)
    mixer_grad = one_grad[:, 2 * wide : 2 * wide + narrow].astype(jnp.float32)
    update_grad = one_grad[:, 2 * wide + narrow : base].astype(jnp.float32)
    output_grad = jnp.concatenate(
        [one_grad[:wide, base:], one_grad[wide:, base:]], axis=1
    ).astype(jnp.float32)

    shared_grad = shared_grad.astype(jnp.float32)
    query_grad, bias_grad, key_grad = vector_sums[0], vector_sums[1], vector_sums[2]
    delta, alpha, beta, eta = (
        item.T for item in (ema_delta, ema_alpha, ema_beta, ema_eta)
    )
    rate = jax.nn.sigmoid(delta)
    damp = jax.nn.sigmoid(alpha)
    weight_sum = feature[:NDIM]
    keep_sum = feature[NDIM : 2 * NDIM] * (rate * beta * eta)
    d_rate = weight_sum * beta * eta - keep_sum * damp
    delta_grad = (d_rate * rate * (1.0 - rate)).T
    alpha_grad = (-keep_sum * rate * damp * (1.0 - damp)).T
    beta_grad = (weight_sum * rate * eta).T
    eta_grad = (weight_sum * rate * beta).T
    omega_grad, gain_grad, ffn_grad = feature[2 * NDIM], feature[2 * NDIM + 1], feature[2 * NDIM + 2]
    return (
        layer_out, token_grad, gain_grad, delta_grad, alpha_grad, beta_grad, eta_grad, omega_grad,
        shared_grad, query_grad, bias_grad, key_grad, value_grad, gate_grad, mixer_grad,
        update_grad, output_grad, ffn_grad, up_grad, down_grad,
    )


def solution(mesh):
    dp, mp = mesh.shape["dp"], mesh.shape["mp"]
    params = (
        P("mp"), P("mp", None), P("mp", None), P("mp", None), P("mp", None), P("mp"),
        P(), P(), P(), P(),
        P(None, "mp"), P(None, "mp"), P(None, "mp"), P(None, "mp"), P("mp", None),
        P("mp"), P(None, "mp"), P("mp", None),
    )
    specs = (P("dp", "mp"), P("dp", "mp")) + params
    return jax.shard_map(
        functools.partial(local, dp, mp), mesh=mesh, in_specs=specs, out_specs=specs, check_vma=False
    )
```

```python
import functools

import jax
import jax.numpy as jnp
from jax import lax
from jax.experimental import pallas as pl
from jax.experimental.pallas import tpu as pltpu
from jax.sharding import PartitionSpec as P

D = 1024
GROUP = 128
LEN = 2048
NDIM = 16
LANES = 128
SUB = D // LANES
EPS = 1e-05
TB = 128


def matmul(left, right):
    return jnp.dot(left, right, preferred_element_type=jnp.float32)


def matmul_tn(left, right):
    return lax.dot_general(
        left, right, (((0,), (0,)), ((), ())), preferred_element_type=jnp.float32
    )


def matmul_nt(left, right):
    return lax.dot_general(
        left, right, (((1,), (1,)), ((), ())), preferred_element_type=jnp.float32
    )


def to_rows(scratch, value):
    for part in range(SUB):
        scratch[pl.ds(part, TB, stride=SUB), :] = value[:, part * LANES : (part + 1) * LANES]


def from_rows(scratch):
    return jnp.concatenate(
        [scratch[pl.ds(part, TB, stride=SUB), :] for part in range(SUB)], axis=1
    )


def row(scratch, index):
    return scratch[pl.ds(pl.multiple_of(index * SUB, SUB), SUB), :]


def sds(shape, dtype=jnp.float32):
    return jax.ShapeDtypeStruct(shape, dtype)


def block(reverse=None):
    if reverse is None:
        return pl.BlockSpec((TB, D), lambda i: (i, 0))
    return pl.BlockSpec((TB, D), lambda i: (reverse - 1 - i, 0))


def whole(*shape):
    return pl.BlockSpec(shape, lambda i: (0,) * len(shape))


STATE = (NDIM, SUB, LANES)
STATES = (2 * NDIM, SUB, LANES)
ROWS = pltpu.VMEM((TB * SUB, LANES), jnp.float32)
PARAMS = pltpu.CompilerParams(vmem_limit_bytes=32 << 20)


ROWS_C = 256


def sigmoid(value):
    return 0.5 + 0.5 * jnp.tanh(0.5 * value)


def causal_probs(query, keys, head_scale):
    scores = matmul_nt(query, keys) * head_scale
    down = lax.broadcasted_iota(jnp.int32, scores.shape, 0)
    across = lax.broadcasted_iota(jnp.int32, scores.shape, 1)
    scores = jnp.where(down >= across, scores, -1e30)
    weights = jnp.exp(scores - jnp.max(scores, axis=1, keepdims=True))
    return weights / jnp.sum(weights, axis=1, keepdims=True)


def mixer_forward_kernel(
    xn_ref, xp_ref, x_ref, one_ref, shared_ref, qgain_ref, qbias_ref, kgain_ref,
    vpre_ref, gpre_ref, att_ref, hid_ref, act_ref, upd_ref, mid_ref, spre_ref,
):
    mp = one_ref.shape[0]
    narrow = D // mp
    wide = vpre_ref.shape[1] // mp
    base = 2 * (wide + narrow)
    groups = ROWS_C // GROUP
    xn, xp = xn_ref[...], xp_ref[...]
    shared_pre = matmul(xp, shared_ref[...])
    spre_ref[...] = shared_pre
    shared = shared_pre * sigmoid(shared_pre)
    query = (shared * qgain_ref[...] + qbias_ref[...]).astype(jnp.bfloat16)
    keys = (shared * kgain_ref[...]).astype(jnp.bfloat16)
    head_scale = shared.shape[1] ** (-0.5)
    probs = [
        causal_probs(
            query[g * GROUP : (g + 1) * GROUP], keys[g * GROUP : (g + 1) * GROUP], head_scale
        ).astype(jnp.bfloat16)
        for g in range(groups)
    ]
    attn_out = None
    for m in range(mp):
        span = slice(m * wide, (m + 1) * wide)
        value_pre = matmul(xn, one_ref[m, :, 0:wide])
        values = (value_pre * sigmoid(value_pre)).astype(jnp.bfloat16)
        vpre_ref[:, span] = value_pre.astype(jnp.bfloat16)
        gate_pre = matmul(xp, one_ref[m, :, wide : 2 * wide])
        gate = gate_pre * sigmoid(gate_pre)
        gpre_ref[:, span] = gate_pre.astype(jnp.bfloat16)
        attended = jnp.concatenate(
            [matmul(probs[g], values[g * GROUP : (g + 1) * GROUP]) for g in range(groups)], axis=0
        )
        att_ref[:, span] = attended.astype(jnp.bfloat16)
        hidden = (gate * attended).astype(jnp.bfloat16)
        hid_ref[:, span] = hidden
        term = jnp.concatenate(
            [matmul(hidden, one_ref[m, 0:wide, base:]), matmul(hidden, one_ref[m, wide:, base:])], axis=1
        )
        attn_out = term if attn_out is None else attn_out + term
    for m in range(mp):
        span = slice(m * narrow, (m + 1) * narrow)
        act = matmul(xp, one_ref[m, :, 2 * wide : 2 * wide + narrow]) + attn_out[:, span]
        upd = matmul(xp, one_ref[m, :, 2 * wide + narrow : base])
        update = sigmoid(upd)
        act_ref[:, span] = act.astype(jnp.bfloat16)
        upd_ref[:, span] = upd.astype(jnp.bfloat16)
        x = x_ref[:, span].astype(jnp.float32)
        mid_ref[:, span] = x + update * (act * sigmoid(act) - x)


def ffn_kernel(
    mid_ref, grad_ref, x_ref, act_ref, upd_ref, two_ref, gain_ref,
    layer_ref, ffn_ref, upper_ref, dup_ref, dact_ref, dupd_ref, dx_ref, gsum_ref,
):
    mp, _, total = two_ref.shape
    units = total - D
    sub = 512
    middle = mid_ref[...]
    grad = grad_ref[...]
    mean = jnp.mean(middle, axis=1, keepdims=True)
    power = jnp.mean(middle * middle, axis=1, keepdims=True)
    scale = lax.rsqrt(power - mean * mean + EPS)
    normed = (middle - mean) * scale
    gain = gain_ref[...]
    ffn_in = (normed * gain).astype(jnp.bfloat16)
    ffn_ref[...] = ffn_in
    down_out = None
    d_ffn = None
    for m in range(mp):
        for first in range(0, units, sub):
            columns = slice(m * units + first, m * units + first + sub)
            up_weights = two_ref[m, :, first : first + sub]
            down_weights = two_ref[m, first : first + sub, units:]
            up_pre = matmul(ffn_in, up_weights)
            logistic = sigmoid(up_pre)
            value = up_pre * logistic
            upper = value.astype(jnp.bfloat16)
            upper_ref[:, columns] = upper
            slope = logistic + value - value * logistic
            d_up = (matmul_nt(grad, down_weights) * slope).astype(jnp.bfloat16)
            dup_ref[:, columns] = d_up
            term = matmul(upper, down_weights)
            down_out = term if down_out is None else down_out + term
            term = matmul_nt(d_up, up_weights)
            d_ffn = term if d_ffn is None else d_ffn + term
    layer_ref[...] = (middle + down_out).astype(jnp.bfloat16)

    @pl.when(pl.program_id(0) == 0)
    def _():
        gsum_ref[...] = jnp.zeros_like(gsum_ref)

    gsum_ref[...] += jnp.sum(d_ffn * normed, axis=0, keepdims=True)
    scaled = d_ffn * gain
    first = jnp.mean(scaled, axis=1, keepdims=True)
    second = jnp.mean(scaled * normed, axis=1, keepdims=True)
    d_middle = grad.astype(jnp.float32) + scale * (scaled - first - normed * second)
    act = act_ref[...].astype(jnp.float32)
    update = sigmoid(upd_ref[...].astype(jnp.float32))
    logistic = sigmoid(act)
    value = act * logistic
    x = x_ref[...].astype(jnp.float32)
    d_update = d_middle * update
    dact_ref[...] = (d_update * (logistic + value - value * logistic)).astype(jnp.bfloat16)
    dupd_ref[...] = (d_update * (value - x) * (1.0 - update)).astype(jnp.bfloat16)
    dx_ref[...] = (d_middle - d_update).astype(jnp.bfloat16)


def mixer_backward_kernel(
    dact_ref, dupd_ref, vpre_ref, gpre_ref, att_ref, spre_ref, mix_ref, one_ref, shared_ref,
    qgain_ref, qbias_ref, kgain_ref,
    dv_ref, dg_ref, dshared_ref, dmix_ref, dxn_ref, sums_ref,
):
    mp = one_ref.shape[0]
    narrow = D // mp
    wide = vpre_ref.shape[1] // mp
    base = 2 * (wide + narrow)
    groups = ROWS_C // GROUP
    shared_pre = spre_ref[...]
    logistic = sigmoid(shared_pre)
    shared = shared_pre * logistic
    query = (shared * qgain_ref[...] + qbias_ref[...]).astype(jnp.bfloat16)
    keys = (shared * kgain_ref[...]).astype(jnp.bfloat16)
    head_scale = shared.shape[1] ** (-0.5)
    rows = [slice(g * GROUP, (g + 1) * GROUP) for g in range(groups)]
    probs = [causal_probs(query[rows[g]], keys[rows[g]], head_scale) for g in range(groups)]
    probs_low = [item.astype(jnp.bfloat16) for item in probs]
    d_act = dact_ref[...]
    d_probs = [None] * groups
    d_xp = None
    d_xn = None
    for m in range(mp):
        span = slice(m * wide, (m + 1) * wide)
        thin = slice(m * narrow, (m + 1) * narrow)
        d_hidden = matmul_nt(d_act[:, : D // 2], one_ref[m, 0:wide, base:]) + matmul_nt(
            d_act[:, D // 2 :], one_ref[m, wide:, base:]
        )
        gate_pre = gpre_ref[:, span].astype(jnp.float32)
        gate_log = sigmoid(gate_pre)
        gate = gate_pre * gate_log
        attended = att_ref[:, span].astype(jnp.float32)
        d_gate = (d_hidden * attended * (gate_log + gate - gate * gate_log)).astype(jnp.bfloat16)
        dg_ref[:, span] = d_gate
        d_att = (d_hidden * gate).astype(jnp.bfloat16)
        value_pre = vpre_ref[:, span].astype(jnp.float32)
        value_log = sigmoid(value_pre)
        value = value_pre * value_log
        values = value.astype(jnp.bfloat16)
        parts = []
        for g in range(groups):
            term = matmul_nt(d_att[rows[g]], values[rows[g]])
            d_probs[g] = term if d_probs[g] is None else d_probs[g] + term
            parts.append(matmul_tn(probs_low[g], d_att[rows[g]]))
        d_value = jnp.concatenate(parts, axis=0)
        d_value_pre = (d_value * (value_log + value - value * value_log)).astype(jnp.bfloat16)
        dv_ref[:, span] = d_value_pre
        term = (
            matmul_nt(d_gate, one_ref[m, :, wide : 2 * wide])
            + matmul_nt(d_act[:, thin], one_ref[m, :, 2 * wide : 2 * wide + narrow])
            + matmul_nt(dupd_ref[:, thin], one_ref[m, :, 2 * wide + narrow : base])
        )
        d_xp = term if d_xp is None else d_xp + term
        term = matmul_nt(d_value_pre, one_ref[m, :, 0:wide])
        d_xn = term if d_xn is None else d_xn + term
    dxn_ref[...] = d_xn.astype(jnp.bfloat16)
    d_query, d_keys = [], []
    for g in range(groups):
        d_scores = probs[g] * (d_probs[g] - jnp.sum(probs[g] * d_probs[g], axis=1, keepdims=True))
        low = d_scores.astype(jnp.bfloat16)
        d_query.append(matmul(low, keys[rows[g]]) * head_scale)
        d_keys.append(matmul_tn(low, query[rows[g]]) * head_scale)
    d_query = jnp.concatenate(d_query, axis=0)
    d_keys = jnp.concatenate(d_keys, axis=0)

    @pl.when(pl.program_id(0) == 0)
    def _():
        sums_ref[...] = jnp.zeros_like(sums_ref)

    sums_ref[0:1, :] += jnp.sum(d_query * shared, axis=0, keepdims=True)
    sums_ref[1:2, :] += jnp.sum(d_query, axis=0, keepdims=True)
    sums_ref[2:3, :] += jnp.sum(d_keys * shared, axis=0, keepdims=True)
    d_shared = (d_query * qgain_ref[...] + d_keys * kgain_ref[...]) * (
        logistic + shared - shared * logistic
    )
    d_shared = d_shared.astype(jnp.bfloat16)
    dshared_ref[...] = d_shared
    d_xp = d_xp + matmul_nt(d_shared, shared_ref[...])
    mix = mix_ref[...]
    mix_log = sigmoid(mix)
    mix_value = mix * mix_log
    dmix_ref[...] = d_xp * (mix_log + mix_value - mix_value * mix_log)


def mixer_weights_kernel(
    xn_ref, xp_ref, hid_ref, dact_all_ref, dv_ref, dg_ref, dact_ref, dupd_ref, dshared_ref,
    one_ref, shared_ref, xnt, xpt,
):
    wide, narrow = dv_ref.shape[1], dact_ref.shape[1]

    @pl.when(pl.program_id(0) == 0)
    def _():
        xnt[...] = xn_ref[...].T
        xpt[...] = xp_ref[...].T
        shared_ref[...] = matmul(xpt[...], dshared_ref[...]).astype(jnp.bfloat16)

    one_ref[0, :, 0:wide] = matmul(xnt[...], dv_ref[...]).astype(jnp.bfloat16)
    one_ref[0, :, wide : 2 * wide] = matmul(xpt[...], dg_ref[...]).astype(jnp.bfloat16)
    one_ref[0, :, 2 * wide : 2 * wide + narrow] = matmul(xpt[...], dact_ref[...]).astype(jnp.bfloat16)
    base = 2 * (wide + narrow)
    one_ref[0, :, 2 * wide + narrow : base] = matmul(xpt[...], dupd_ref[...]).astype(jnp.bfloat16)
    out = matmul_tn(hid_ref[...], dact_all_ref[...]).astype(jnp.bfloat16)
    one_ref[0, 0:wide, base:] = out[:, : D // 2]
    one_ref[0, wide:, base:] = out[:, D // 2 :]


def ffn_weights_kernel(ffn_ref, grad_ref, upper_ref, dup_ref, two_ref, fft):
    units = dup_ref.shape[1]

    @pl.when(pl.program_id(0) == 0)
    def _():
        fft[...] = ffn_ref[...].T

    two_ref[0, :, 0:units] = matmul(fft[...], dup_ref[...]).astype(jnp.bfloat16)
    two_ref[0, :, units:] = matmul_tn(upper_ref[...], grad_ref[...]).astype(jnp.bfloat16)


def held(*shape):
    return pl.BlockSpec(shape, lambda i: (0,) * len(shape), pipeline_mode=pl.Buffered(1))


def rows_block(width):
    return pl.BlockSpec((ROWS_C, width), lambda i: (i, 0))


BIG = pltpu.CompilerParams(vmem_limit_bytes=60 << 20)


def cost(flops, bytes_accessed):
    return pl.CostEstimate(flops=int(flops), transcendentals=0, bytes_accessed=int(bytes_accessed))


def ffn(middle, grad, x, act, upd, two, gain):
    count = x.shape[0]
    units = two.shape[0] * (two.shape[2] - D)
    low = jnp.bfloat16
    return pl.pallas_call(
        ffn_kernel,
        grid=(count // ROWS_C,),
        in_specs=[rows_block(D)] * 5 + [held(*two.shape), held(1, D)],
        out_specs=[rows_block(D)] * 2 + [rows_block(units)] * 2 + [rows_block(D)] * 3 + [whole(1, D)],
        out_shape=[sds((count, D), low)] * 2
        + [sds((count, units), low)] * 2
        + [sds((count, D), low)] * 3
        + [sds((1, D))],
        compiler_params=BIG,
        cost_estimate=cost(4 * count * two.size, 60 << 20),
        name="ffn",
    )(middle, grad, x, act, upd, two, gain)


def mixer_backward(d_act, d_upd, vpre, gpre, att, spre, mix, one, shared, qgain, qbias, kgain):
    count = d_act.shape[0]
    units = vpre.shape[1]
    z = shared.shape[1]
    low = jnp.bfloat16
    return pl.pallas_call(
        mixer_backward_kernel,
        grid=(count // ROWS_C,),
        in_specs=[rows_block(D)] * 2
        + [rows_block(units)] * 3
        + [rows_block(z), rows_block(D)]
        + [held(*one.shape), held(*shared.shape)]
        + [held(1, z)] * 3,
        out_specs=[rows_block(units)] * 2
        + [rows_block(z), rows_block(D), rows_block(D), whole(8, z)],
        out_shape=[sds((count, units), low)] * 2
        + [sds((count, z), low), sds((count, D)), sds((count, D), low), sds((8, z))],
        compiler_params=BIG,
        cost_estimate=cost(2 * count * (one.size + shared.size), 60 << 20),
        name="mixer_backward",
    )(d_act, d_upd, vpre, gpre, att, spre, mix, one, shared, qgain, qbias, kgain)


def mixer_weights(mp, xn, xp, hidden, d_act, d_value, d_gate, d_upd, d_shared):
    count = xn.shape[0]
    wide, narrow, z = d_value.shape[1] // mp, D // mp, d_shared.shape[1]
    low = jnp.bfloat16

    def part(width):
        return pl.BlockSpec((count, width), lambda i: (0, i))

    return pl.pallas_call(
        mixer_weights_kernel,
        grid=(mp,),
        in_specs=[held(count, D), held(count, D), part(wide), held(count, D)]
        + [part(wide), part(wide), part(narrow), part(narrow), held(count, z)],
        out_specs=[
            pl.BlockSpec((1, D, 2 * (wide + narrow) + D // 2), lambda i: (i, 0, 0)),
            whole(D, z),
        ],
        out_shape=[sds((mp, D, 2 * (wide + narrow) + D // 2), low), sds((D, z), low)],
        scratch_shapes=[pltpu.VMEM((D, count), low), pltpu.VMEM((D, count), low)],
        compiler_params=BIG,
        cost_estimate=cost(2 * count * D * mp * (3 * wide + 2 * narrow), 40 << 20),
        name="mixer_weights",
    )(xn, xp, hidden, d_act, d_value, d_gate, d_act, d_upd, d_shared)


def ffn_weights(mp, ffn_in, grad, upper, d_up):
    count = ffn_in.shape[0]
    units = upper.shape[1] // mp
    low = jnp.bfloat16

    def part(width):
        return pl.BlockSpec((count, width), lambda i: (0, i))

    return pl.pallas_call(
        ffn_weights_kernel,
        grid=(mp,),
        in_specs=[held(count, D), held(count, D), part(units), part(units)],
        out_specs=pl.BlockSpec((1, D, units + D), lambda i: (i, 0, 0)),
        out_shape=sds((mp, D, units + D), low),
        scratch_shapes=[pltpu.VMEM((D, count), low)],
        compiler_params=BIG,
        cost_estimate=cost(4 * count * D * mp * units, 40 << 20),
        name="ffn_weights",
    )(ffn_in, grad, upper, d_up)


MESH = pl.DeviceIdType.MESH


def rank_of(index, order):
    total = 0
    for place, bit in enumerate(order):
        total = total + lax.rem(lax.div(index, 1 << bit), 2) * (1 << place)
    return total


def flip(index, bit):
    low = lax.rem(lax.div(index, 1 << bit), 2)
    return index + (1 - 2 * low) * (1 << bit)


def orders_of(dp):
    bits = dp.bit_length() - 1
    inner = list(range(1, bits))
    return (inner + [0], inner[::-1] + [0])


def greet(dp, mp):
    me = lax.axis_index("dp")
    part = lax.axis_index("mp")
    bits = dp.bit_length() - 1
    barrier = pltpu.get_barrier_semaphore()
    for step in range(1, mp):
        pl.semaphore_signal(
            barrier, inc=1, device_id={"mp": lax.rem(part + step, mp)}, device_id_type=MESH
        )
    for bit in range(bits):
        pl.semaphore_signal(barrier, inc=1, device_id={"dp": flip(me, bit)}, device_id_type=MESH)
    pl.semaphore_wait(barrier, mp - 1 + bits)


def arrived(ref, sem):
    pltpu.make_async_copy(ref, ref, sem).wait()


def remote(src, dst, send_sem, recv_sem, axis, to):
    return pltpu.make_async_remote_copy(
        src_ref=src, dst_ref=dst, send_sem=send_sem, recv_sem=recv_sem,
        device_id={axis: to}, device_id_type=MESH,
    )


def span_of(index, size):
    return pl.ds(pl.multiple_of(index * size, size), size)


class Swap:
    def __init__(self, mp, src, dst, sems, back=False):
        self.mp, self.src, self.dst, self.back = mp, src, dst, back
        self.hold, self.send, self.recv, self.own = sems
        self.part = lax.axis_index("mp")
        if back:
            self.rows, self.width = src.shape[0], dst.shape[1]
        else:
            self.rows, self.width = dst.shape[0], src.shape[1]

    def piece(self, index):
        if self.back:
            return self.src.at[:, span_of(index, self.width)]
        return self.src.at[span_of(index, self.rows), :]

    def place(self, index):
        if self.back:
            return self.dst.at[span_of(index, self.rows), :]
        return self.dst.at[:, span_of(index, self.width)]

    def load(self):
        return pltpu.make_async_copy(self.piece(self.part), self.hold, self.own.at[0])

    def store(self):
        return pltpu.make_async_copy(self.hold, self.place(self.part), self.own.at[1])

    def copies(self):
        for step in range(1, self.mp):
            to = lax.rem(self.part + step, self.mp)
            yield remote(
                self.piece(to), self.place(self.part),
                self.send.at[step], self.recv.at[self.part], "mp", to,
            )

    def start(self):
        self.load().start()
        for copy in self.copies():
            copy.start()

    def turn(self):
        self.load().wait()
        self.store().start()

    def receive(self):
        self.store().wait()
        for step in range(1, self.mp):
            source = lax.rem(self.part + step, self.mp)
            arrived(self.place(source), self.recv.at[source])

    def close(self):
        for copy in self.copies():
            copy.wait_send()


class Gather:
    def __init__(self, dp, mp, src, dst, sems):
        self.dp, self.mp, self.src, self.dst = dp, mp, src, dst
        self.hold, self.line_send, self.pass_send, self.line_recv, self.send, self.recv, self.own = sems
        self.me, self.part = lax.axis_index("dp"), lax.axis_index("mp")
        self.bits = dp.bit_length() - 1
        self.orders = orders_of(dp)

    def region(self, ref, half, index, held):
        total = ref.shape[0] // 2
        share = total // self.dp
        first = lax.div(rank_of(index, self.orders[half]), 1 << held) * (share << held)
        return ref.at[pl.ds(pl.multiple_of(half * total + first, share), share << held), :]

    def load(self):
        there = self.dst.at[self.part] if self.hold is None else self.hold
        return pltpu.make_async_copy(self.src, there, self.own.at[0])

    def store(self):
        return pltpu.make_async_copy(self.hold, self.dst.at[self.part], self.own.at[1])

    def turn(self):
        self.load().wait()
        if self.hold is not None:
            self.store().start()

    def first(self, up):
        to = self.part + 1 if up else self.part - 1
        for half in range(2):
            yield remote(
                self.region(self.src, half, self.me, 0),
                self.region(self.dst.at[self.part], half, self.me, 0),
                self.line_send.at[int(up), half], self.line_recv.at[self.part, half], "mp", to,
            )

    def passed(self, source):
        to = jnp.where(source < self.part, self.part + 1, self.part - 1)
        for half in range(2):
            held = self.region(self.dst.at[source], half, self.me, 0)
            yield remote(
                held, held, self.pass_send.at[source, half], self.line_recv.at[source, half], "mp", to
            )

    def passes(self, source):
        return jnp.logical_or(
            jnp.logical_and(source < self.part, self.part < self.mp - 1),
            jnp.logical_and(source > self.part, self.part > 0),
        )

    def doubled(self, source, stage):
        for half in range(2):
            held = self.region(self.dst.at[source], half, self.me, stage)
            yield remote(
                held, held, self.send.at[stage, source, half], self.recv.at[stage, source, half],
                "dp", flip(self.me, self.orders[half][stage]),
            )

    def source(self, step):
        mp, part = self.mp, self.part
        near = [lax.rem(part + 1, 2) + part - lax.rem(part, 2)]
        low = lax.div(part, mp // 2) == 0
        far = [jnp.where(low, mp // 2 + i, mp // 2 - 1 - i) for i in range(mp // 2)]
        return (near + far)[step]

    def start(self):
        for up in (True, False):

            @pl.when(self.part < self.mp - 1 if up else self.part > 0)
            def _(up=up):
                for copy in self.first(up):
                    copy.start()

        self.load().start()

    def advance(self, step, stage):
        source = self.source(step)
        for half in range(2):
            if stage == 0:
                came = self.region(self.dst.at[source], half, self.me, 0)
                arrived(came, self.line_recv.at[source, half])
            else:
                other = flip(self.me, self.orders[half][stage - 1])
                came = self.region(self.dst.at[source], half, other, stage - 1)
                arrived(came, self.recv.at[stage - 1, source, half])
        if stage == 0:

            @pl.when(self.passes(source))
            def _():
                for copy in self.passed(source):
                    copy.start()

        if stage < self.bits:
            for copy in self.doubled(source, stage):
                copy.start()

    def waves(self):
        return self.mp - 1 + self.bits

    def wave(self, number):
        for stage in range(self.bits, -1, -1):
            if 0 <= number - stage < self.mp - 1:
                self.advance(number - stage, stage)

    def close(self):
        if self.hold is not None:
            self.store().wait()
        for up in (True, False):

            @pl.when(self.part < self.mp - 1 if up else self.part > 0)
            def _(up=up):
                for copy in self.first(up):
                    copy.wait_send()

        for step in range(self.mp - 1):
            source = self.source(step)

            @pl.when(self.passes(source))
            def _(source=source):
                for copy in self.passed(source):
                    copy.wait_send()

            for stage in range(self.bits):
                for copy in self.doubled(source, stage):
                    copy.wait_send()


def swap_scratch(mp, rows, width, dtype=jnp.bfloat16):
    dma = pltpu.SemaphoreType.DMA
    return [pltpu.VMEM((rows, width), dtype), dma((mp,)), dma((mp,)), dma((2,))]


def gather_scratch(dp, mp, pack):
    dma = pltpu.SemaphoreType.DMA
    bits = dp.bit_length() - 1
    return [
        pltpu.VMEM(pack.shape, pack.dtype), dma((2, 2)), dma((mp, 2)), dma((mp, 2)),
        dma((bits, mp, 2)), dma((bits, mp, 2)), dma((2,)),
    ]


HBM = pl.BlockSpec(memory_space=pl.ANY)


def forward_kernel(
    dp, mp, span,
    small_ref, first_ref, tok_ref, shared_ref, qgain_ref, qbias_ref, kgain_ref, pack_ref, cot_ref,
    xn_ref, xp_ref, mix_ref, starts_ref, keep_ref, weight_ref, gains_ref,
    vpre_ref, gpre_ref, att_ref, hid_ref, act_ref, upd_ref, mid_ref, spre_ref,
    one_out, x_out, full_ref, grad_ref,
    one_ref, x_all, small_all, xn_all, rows, outs, ends, starts, state_ref,
    carry_send, carry_recv, out_sem, *sems,
):
    index = pl.program_id(0)
    steps = pl.num_programs(0) // 2
    part = lax.axis_index("mp")
    swap = Swap(mp, cot_ref, grad_ref, sems[0:4])
    plan = Gather(dp, mp, pack_ref, full_ref, sems[4:11])
    tokens = Swap(mp, tok_ref, x_all, sems[11:15])
    tiny = Swap(mp, small_ref, small_all, sems[15:19], back=True)
    opening = Gather(dp, mp, first_ref, one_ref, (None,) + tuple(sems[19:25]))
    gives = lax.rem(part + 1, span) != 0
    takes = lax.rem(part, span) != 0
    gain_ref, omega_ref = gains_ref.at[0:1, :], gains_ref.at[1:2, :]

    def carry():
        return remote(ends, starts, carry_send.at[0], carry_recv.at[0], "mp", part + 1)

    def one_copy():
        return pltpu.make_async_copy(one_ref, one_out, out_sem.at[0])

    def x_copy():
        return pltpu.make_async_copy(x_all, x_out, out_sem.at[1])

    @pl.when(index == 0)
    def _():
        greet(dp, mp)
        tiny.start()
        opening.start()
        tiny.turn()
        opening.turn()
        for number in range(opening.waves()):
            opening.wave(number)
            if number == mp - 2:
                tokens.start()
        plan.start()
        tokens.turn()
        tiny.receive()
        lines = small_all.shape[0] // mp
        width = small_all.shape[1]
        gains_ref[...] = jnp.zeros_like(gains_ref)
        for m in range(mp):
            block = small_all[m * lines : (m + 1) * lines, :]
            delta, alpha, beta, eta = (block[NDIM * i : NDIM * (i + 1), :] for i in range(4))
            rate = jax.nn.sigmoid(delta)
            keep = 1.0 - rate * jax.nn.sigmoid(alpha)
            weight = rate * beta * eta
            for piece in range(width // LANES):
                there = pl.ds(m * (width // LANES) + piece, NDIM, stride=SUB)
                keep_ref[there, :] = keep[:, piece * LANES : (piece + 1) * LANES]
                weight_ref[there, :] = weight[:, piece * LANES : (piece + 1) * LANES]
            gains_ref[0:3, m * width : (m + 1) * width] = block[4 * NDIM : 4 * NDIM + 3, :]
        tokens.receive()
        one_copy().start()
        x_copy().start()
        ends[...] = jnp.zeros_like(ends)

    @pl.when(index < steps)
    def _():
        keep = [keep_ref[j * SUB : (j + 1) * SUB, :] for j in range(NDIM)]
        for piece in range(ROWS_C // TB):
            here = slice(piece * TB, (piece + 1) * TB)
            x = x_all[
                pl.ds(pl.multiple_of(index * ROWS_C + piece * TB, TB), TB), :
            ].astype(jnp.float32)
            mean = jnp.mean(x, axis=1, keepdims=True)
            power = jnp.mean(x * x, axis=1, keepdims=True)
            scale = lax.rsqrt(power - mean * mean + EPS)
            xn = ((x - mean) * scale * gain_ref[...]).astype(jnp.bfloat16)
            xn_ref[here, :] = xn
            xn_all[pl.ds(pl.multiple_of(index * ROWS_C + piece * TB, TB), TB), :] = xn
            to_rows(rows, xn.astype(jnp.float32))

            def step(t, carried):
                state, slope = carried
                now = row(rows, t)
                slope = tuple(keep[j] * slope[j] + state[j] for j in range(NDIM))
                state = tuple(keep[j] * state[j] + now for j in range(NDIM))
                return (state, slope)

            state = tuple(ends[j] for j in range(NDIM))
            slope = tuple(ends[NDIM + j] for j in range(NDIM))
            state, slope = lax.fori_loop(0, TB, step, (state, slope), unroll=4)
            for j in range(NDIM):
                ends[j] = state[j]
                ends[NDIM + j] = slope[j]

    @pl.when(index == steps - 1)
    def _():
        @pl.when(gives)
        def _():
            carry().start()

        plan.turn()

    @pl.when(index == steps)
    def _():
        @pl.when(jnp.logical_not(takes))
        def _():
            starts[...] = jnp.zeros_like(starts)

        @pl.when(takes)
        def _():
            arrived(starts, carry_recv.at[0])

        @pl.when(gives)
        def _():
            carry().wait_send()

        for j in range(NDIM):
            state_ref[j] = starts[j]
        starts_ref[...] = starts[...]

    @pl.when(index >= steps)
    def _():
        for piece in range(ROWS_C // TB):
            here = slice(piece * TB, (piece + 1) * TB)
            xn = xn_all[
                pl.ds(pl.multiple_of((index - steps) * ROWS_C + piece * TB, TB), TB), :
            ].astype(jnp.float32)
            to_rows(rows, xn)
            keep = [keep_ref[j * SUB : (j + 1) * SUB, :] for j in range(NDIM)]

            def step(t, state):
                now = row(rows, t)
                state = tuple(keep[j] * state[j] + now for j in range(NDIM))
                terms = [weight_ref[j * SUB : (j + 1) * SUB, :] * state[j] for j in range(NDIM)]
                while len(terms) > 1:
                    terms = [a + b for a, b in zip(terms[::2], terms[1::2])]
                outs[pl.ds(pl.multiple_of(t * SUB, SUB), SUB), :] = terms[0]
                return state

            state = lax.fori_loop(0, TB, step, tuple(state_ref[j] for j in range(NDIM)), unroll=4)
            for j in range(NDIM):
                state_ref[j] = state[j]
            mix = from_rows(outs) + omega_ref[...] * xn
            mix_ref[here, :] = mix
            xp_ref[here, :] = (mix * sigmoid(mix)).astype(jnp.bfloat16)

        there = pl.ds(pl.multiple_of((index - steps) * ROWS_C, ROWS_C), ROWS_C)
        mixer_forward_kernel(
            xn_all.at[there, :], xp_ref, x_all.at[there, :], one_ref, shared_ref, qgain_ref, qbias_ref, kgain_ref,
            vpre_ref, gpre_ref, att_ref, hid_ref, act_ref, upd_ref, mid_ref, spre_ref,
        )

    for number in range(plan.waves()):

        @pl.when(index == jnp.minimum(number + 2, 2 * steps - 1))
        def _(number=number):
            plan.wave(number)
            if number == 0:
                swap.start()

    @pl.when(index == 2 * steps - 1)
    def _():
        swap.turn()
        swap.receive()
        for item in (swap, plan, tokens, tiny, opening):
            item.close()
        one_copy().wait()
        x_copy().wait()


def forward(dp, mp, span, units, small, first, tokens, shared, vectors, pack, cotangent):
    count = tokens.shape[0] // mp
    steps = count // ROWS_C
    z = shared.shape[1]
    low = jnp.bfloat16
    early = pl.BlockSpec((ROWS_C, D), lambda i: (jnp.minimum(i, steps - 1), 0))

    def late(width):
        return pl.BlockSpec((ROWS_C, width), lambda i: (jnp.maximum(i - steps, 0), 0))

    dma = pltpu.SemaphoreType.DMA
    lines, width = small.shape[0], small.shape[1] // mp
    return pl.pallas_call(
        functools.partial(forward_kernel, dp, mp, span),
        grid=(2 * steps,),
        in_specs=[HBM] * 3 + [held(*shared.shape)] + [held(1, z)] * 3 + [HBM] * 2,
        out_specs=[early, late(D), late(D), whole(*STATES)]
        + [whole(NDIM * SUB, LANES)] * 2
        + [whole(8, D)]
        + [late(units)] * 4
        + [late(D)] * 3
        + [late(z)]
        + [HBM] * 4,
        out_shape=[sds((count, D), low), sds((count, D), low), sds((count, D)), sds(STATES)]
        + [sds((NDIM * SUB, LANES))] * 2
        + [sds((8, D))]
        + [sds((count, units), low)] * 4
        + [sds((count, D), low)] * 2
        + [sds((count, D)), sds((count, z))]
        + [sds((mp,) + first.shape, low), sds((count, D), low)]
        + [sds((mp,) + pack.shape, low), sds((count, D), low)],
        scratch_shapes=[
            pltpu.VMEM((mp,) + first.shape, low), pltpu.VMEM((count, D), low),
            pltpu.VMEM((mp * lines, width), jnp.float32), pltpu.VMEM((count, D), low), ROWS, ROWS,
            pltpu.VMEM(STATES, jnp.float32), pltpu.VMEM(STATES, jnp.float32),
            pltpu.VMEM(STATE, jnp.float32), dma((1,)), dma((1,)), dma((2,)),
        ]
        + swap_scratch(mp, count, cotangent.shape[1])
        + gather_scratch(dp, mp, pack)
        + swap_scratch(mp, count, tokens.shape[1])
        + swap_scratch(mp, lines, width, small.dtype)
        + gather_scratch(dp, mp, first)[1:],
        compiler_params=pltpu.CompilerParams(
            collective_id=1, has_side_effects=True, vmem_limit_bytes=61 << 20
        ),
        name="forward",
    )(small, first, tokens, shared, *vectors, pack, cotangent)


def add_rows(acc, first, other, count):
    chunk = min(count, 32)

    def step(index, _):
        there = pl.ds(pl.multiple_of(first + index * chunk, chunk), chunk)
        here = pl.ds(pl.multiple_of(index * chunk, chunk), chunk)
        total = acc[there, :].astype(jnp.float32) + other[here, :].astype(jnp.float32)
        acc[there, :] = total.astype(jnp.bfloat16)
        return 0

    lax.fori_loop(0, count // chunk, step, 0)


class Reduce:
    def __init__(self, dp, mp, src, out, stage, recvs, lines, last, sems, waits):
        self.dp, self.mp, self.src, self.out, self.stage = dp, mp, src, out, stage
        self.recvs, self.lines, self.last, self.waits = recvs, lines, last, waits
        (
            self.load, self.send, self.recv, self.line_send, self.line_recv,
            self.last_send, self.last_recv, self.ring_send, self.ring_recv, self.own,
        ) = sems
        self.me, self.part = lax.axis_index("dp"), lax.axis_index("mp")
        self.bits = dp.bit_length() - 1
        self.orders = orders_of(dp)
        self.share = src.shape[1] // dp
        self.width = src.shape[2] // 2

    def shard(self, i):
        near, far = flip(self.part, 0), flip(self.part, 1)
        return (near, flip(far, 0), far, self.part)[i]

    def rank(self, half, index):
        return rank_of(index, self.orders[half])

    def push(self, copy):
        copy.start()
        self.waits.append(copy.wait_send)

    def begin(self, i, slot):
        m = self.shard(i)
        count = self.share << (self.bits - 1)
        for half in range(2):
            columns = slice(half * self.width, (half + 1) * self.width)
            other = flip(self.me, self.orders[half][self.bits - 1])

            def rows(index):
                return span_of(lax.div(self.rank(half, index), 1 << (self.bits - 1)), count)

            self.push(
                remote(
                    self.src.at[m, rows(other), columns], self.recvs[0].at[m, half],
                    self.send.at[0, i, half], self.recv.at[0, m, half], "dp", other,
                )
            )
            pltpu.make_async_copy(
                self.src.at[m, rows(self.me), columns], self.stage.at[slot, half],
                self.load.at[slot, half],
            ).start()

    def offset(self, half, index, stage):
        low = lax.rem(self.rank(half, index), 1 << (self.bits - 1))
        left = self.bits - 1 - stage
        return lax.div(low, 1 << left) * (self.share << left)

    def fold(self, i, stage, slot):
        m = self.shard(i)
        count = self.share << (self.bits - 1 - stage)
        for half in range(2):
            acc = self.recvs[0].at[m, half]
            came = self.recvs[stage].at[m, half]
            arrived(came, self.recv.at[stage, m, half])
            if stage == 0:
                own = self.stage.at[slot, half]
                arrived(own, self.load.at[slot, half])
                add_rows(acc, 0, own, count)
            else:
                add_rows(acc, self.offset(half, self.me, stage), came, count)
            if stage < self.bits - 1:
                other = flip(self.me, self.orders[half][self.bits - 2 - stage])
                give = self.offset(half, other, stage + 1)
                self.push(
                    remote(
                        acc.at[pl.ds(pl.multiple_of(give, self.share), count // 2), :],
                        self.recvs[stage + 1].at[m, half],
                        self.send.at[stage + 1, i, half], self.recv.at[stage + 1, m, half],
                        "dp", other,
                    )
                )
                continue
            first = self.offset(half, self.me, stage)
            mine = acc.at[pl.ds(pl.multiple_of(first, self.share), self.share), :]
            if i >= 2:
                came = self.lines.at[m, half]
                arrived(came, self.line_recv.at[m, half])
                add_rows(acc, first, came, self.share)
            if i < 2:
                self.push(
                    remote(
                        mine, self.lines.at[m, half],
                        self.line_send.at[i, half], self.line_recv.at[m, half],
                        "mp", flip(self.part, 0),
                    )
                )
            elif i == 2:
                self.push(
                    remote(
                        mine, self.last.at[half], self.last_send.at[half], self.last_recv.at[half],
                        "mp", flip(self.part, 1),
                    )
                )
            else:
                came = self.last.at[half]
                arrived(came, self.last_recv.at[half])
                add_rows(acc, first, came, self.share)
                pltpu.make_async_copy(mine, self.rows_at(half, self.me, 0), self.own.at[half]).start()

    def rows_at(self, half, index, stage):
        first = lax.div(self.rank(half, index), 1 << stage) * (self.share << stage)
        return self.out.at[
            pl.ds(pl.multiple_of(first, self.share), self.share << stage),
            half * self.width : (half + 1) * self.width,
        ]

    def spread(self, stage):
        for half in range(2):
            mine = self.rows_at(half, self.me, stage)
            if stage == 0:
                arrived(mine, self.own.at[half])
            else:
                other = flip(self.me, self.orders[half][stage - 1])
                arrived(self.rows_at(half, other, stage - 1), self.ring_recv.at[stage - 1, half])
            if stage < self.bits:
                self.push(
                    remote(
                        mine, mine, self.ring_send.at[stage, half], self.ring_recv.at[stage, half],
                        "dp", flip(self.me, self.orders[half][stage]),
                    )
                )


def reduce_sems(dp, mp):
    dma = pltpu.SemaphoreType.DMA
    bits = dp.bit_length() - 1
    return [
        dma((bits, mp, 2)), dma((bits, mp, 2)), dma((2, 2)), dma((mp, 2)),
        dma((2,)), dma((2,)), dma((bits, 2)), dma((bits, 2)), dma((2,)),
    ]


class Tiny:
    def __init__(self, dp, mp, piece, line, ring, came, sems, waits):
        self.dp, self.mp, self.piece, self.waits = dp, mp, piece, waits
        self.line, self.ring, self.came = line, ring, came
        self.send, self.recv, self.ring_send, self.ring_recv = sems
        self.me, self.part = lax.axis_index("dp"), lax.axis_index("mp")
        self.bits = dp.bit_length() - 1

    def push(self, copy):
        copy.start()
        self.waits.append(copy.wait_send)

    def start(self):
        for step in range(1, self.mp):
            to = lax.rem(self.part + step, self.mp)
            self.push(
                remote(
                    self.piece(to), self.line.at[self.part],
                    self.send.at[step], self.recv.at[self.part], "mp", to,
                )
            )

    def fold(self, stage):
        if stage == 0:
            total = self.piece(self.part)[...].astype(jnp.float32)
            for step in range(1, self.mp):
                source = lax.rem(self.part + step, self.mp)
                arrived(self.line.at[source], self.recv.at[source])
                total = total + self.line[source].astype(jnp.float32)
        else:
            arrived(self.came.at[stage - 1], self.ring_recv.at[stage - 1])
            total = self.ring[stage - 1] + self.came[stage - 1]
        self.ring[stage] = total
        if stage < self.bits:
            self.push(
                remote(
                    self.ring.at[stage], self.came.at[stage],
                    self.ring_send.at[stage], self.ring_recv.at[stage],
                    "dp", flip(self.me, stage),
                )
            )


def tiny_sems(dp, mp):
    dma = pltpu.SemaphoreType.DMA
    bits = dp.bit_length() - 1
    return [dma((mp,)), dma((mp,)), dma((bits,)), dma((bits,))]


FEATURES = 40
LAG = 2


def closing_kernel(
    dp, mp, span,
    one_ref, two_ref, layer_ref, grad_ref, xn_ref, x_ref, normed_ref, direct_ref, shared_ref, vector_ref,
    keep_ref, weight_ref, gain_ref, omega_ref, ffn_ref, starts_ref,
    one_out, two_out, layer_out, token_out, feat_out, shared_out, vector_out,
    stage, *refs,
):
    bits = dp.bit_length() - 1
    me, part = lax.axis_index("dp"), lax.axis_index("mp")
    waits = []
    taken = 0

    def take(count):
        nonlocal taken
        taken += count
        return refs[taken - count : taken]

    recvs = [take(bits), take(bits)]
    lines = take(2)
    last = take(2)
    grad, xn, x, normed_part, direct, tokens, rows, outs, states, ahead, sums, feat = take(12)
    shared, shared_line, shared_ring, shared_came, shared_low = take(5)
    feat_line, feat_ring, feat_came = take(3)
    vector, vector_line, vector_ring, vector_came = take(4)
    (load_sem,) = take(1)
    (in_sem,) = take(1)
    carry_send, carry_recv = take(2)
    spread_send, spread_recv, spread_own = take(3)
    packs = [
        Reduce(dp, mp, src, out, stage, recvs[i], lines[i], last[i], (load_sem,) + take(9), waits)
        for i, (src, out) in enumerate(((two_ref, two_out), (one_ref, one_out)))
    ]
    layer = Swap(mp, layer_ref, layer_out, take(4), back=True)
    token = Swap(mp, tokens, token_out, take(4), back=True)
    quarter = shared.shape[0] // mp
    columns = feat.shape[1] // mp
    tiny_shared = Tiny(
        dp, mp, lambda m: shared.at[span_of(m, quarter), :],
        shared_line, shared_ring, shared_came, take(4), waits,
    )
    tiny_vector = Tiny(
        dp, mp, lambda m: vector, vector_line, vector_ring, vector_came, take(4), waits
    )
    tiny_feat = Tiny(
        dp, mp, lambda m: feat.at[:, span_of(m, columns)],
        feat_line, feat_ring, feat_came, take(4), waits,
    )
    loads = [
        pltpu.make_async_copy(src, dst, in_sem.at[i])
        for i, (src, dst) in enumerate(
            (
                (grad_ref, grad), (xn_ref, xn), (x_ref, x), (normed_ref, normed_part),
                (direct_ref, direct), (shared_ref, shared), (vector_ref, vector),
            )
        )
    ]
    count = grad.shape[0]
    blocks = count // TB
    keep = lambda dims: [keep_ref[j] for j in dims]
    every = range(NDIM)
    gives = lax.rem(part, span) != 0
    takes = lax.rem(part + 1, span) != 0

    def carry():
        return remote(outs.at[0 : NDIM * SUB, :], ahead, carry_send.at[0], carry_recv.at[0], "mp", part - 1)

    def slot_of(j):
        return slice(j * SUB, (j + 1) * SUB)

    def adjoint():
        loads[0].wait()
        kept = keep(every)

        def block_step(number, state):
            first = pl.multiple_of((blocks - 1 - number) * TB, TB)
            to_rows(rows, grad[pl.ds(first, TB), :])

            def step(t, state):
                now = row(rows, TB - 1 - t)
                return tuple(kept[j] * state[j] + now for j in every)

            return lax.fori_loop(0, TB, step, state, unroll=4)

        zero = jnp.zeros((SUB, LANES), jnp.float32)
        state = lax.fori_loop(0, blocks, block_step, tuple(zero for _ in every))
        for j in every:
            outs[slot_of(j), :] = state[j]

        @pl.when(gives)
        def _():
            carry().start()

        for j in range(2 * NDIM):
            states[j] = starts_ref[j]
        sums[...] = jnp.zeros_like(sums)
        feat[...] = jnp.zeros_like(feat)
        feat[34:35, :] = ffn_ref[...]
        loads[1].wait()

    def params(low, high):
        half = NDIM // 2

        def block_step(number, _):
            first = pl.multiple_of(number * TB, TB)
            now_xn = xn[pl.ds(first, TB), :].astype(jnp.float32)
            now_grad = grad[pl.ds(first, TB), :]
            to_rows(rows, now_xn)
            for piece in range(SUB):
                turned[pl.ds(piece, TB, stride=SUB), :] = now_grad[:, piece * LANES : (piece + 1) * LANES]
            feat[32:33, :] += jnp.sum(now_grad * now_xn, axis=0, keepdims=True)
            for start in (0, half):
                dims = range(start, start + half)
                kept = keep(dims)

                def step(t, carried):
                    state, slope, weight_sum, keep_sum = carried
                    now = row(rows, t)
                    grad_now = row(turned, t)
                    slope = tuple(kept[j] * slope[j] + state[j] for j in range(half))
                    state = tuple(kept[j] * state[j] + now for j in range(half))
                    weight_sum = tuple(weight_sum[j] + grad_now * state[j] for j in range(half))
                    keep_sum = tuple(keep_sum[j] + grad_now * slope[j] for j in range(half))
                    return (state, slope, weight_sum, keep_sum)

                carried = (
                    tuple(states[j] for j in dims),
                    tuple(states[NDIM + j] for j in dims),
                    tuple(sums[slot_of(j), :] for j in dims),
                    tuple(sums[slot_of(NDIM + j), :] for j in dims),
                )
                state, slope, weight_sum, keep_sum = lax.fori_loop(0, TB, step, carried, unroll=4)
                for place, j in enumerate(dims):
                    states[j] = state[place]
                    states[NDIM + j] = slope[place]
                    sums[slot_of(j), :] = weight_sum[place]
                    sums[slot_of(NDIM + j), :] = keep_sum[place]
            return 0

        lax.fori_loop(low, high, block_step, 0)

    def meet():
        @pl.when(gives)
        def _():
            carry().wait_send()

        @pl.when(jnp.logical_not(takes))
        def _():
            ahead[...] = jnp.zeros_like(ahead)

        @pl.when(takes)
        def _():
            arrived(ahead, carry_recv.at[0])

        for copy in loads[2:5]:
            copy.wait()

    def token_rows(low, high):
        kept = keep(every)

        def block_step(number, state):
            there = pl.ds(pl.multiple_of((blocks - 1 - number) * TB, TB), TB)
            now_grad = grad[there, :]
            to_rows(rows, now_grad)

            def step(t, state):
                place = TB - 1 - t
                now = row(rows, place)
                state = tuple(kept[j] * state[j] + now for j in every)
                terms = [weight_ref[j] * state[j] for j in every]
                while len(terms) > 1:
                    terms = [a + b for a, b in zip(terms[::2], terms[1::2])]
                outs[pl.ds(pl.multiple_of(place * SUB, SUB), SUB), :] = terms[0]
                return state

            state = lax.fori_loop(0, TB, step, state, unroll=4)
            d_xn = from_rows(outs) + now_grad * omega_ref[...]
            d_xn = d_xn + normed_part[there, :].astype(jnp.float32)
            now_x = x[there, :].astype(jnp.float32)
            mean = jnp.mean(now_x, axis=1, keepdims=True)
            power = jnp.mean(now_x * now_x, axis=1, keepdims=True)
            scale = lax.rsqrt(power - mean * mean + EPS)
            normed = (now_x - mean) * scale
            feat[33:34, :] += jnp.sum(d_xn * normed, axis=0, keepdims=True)
            scaled = d_xn * gain_ref[...]
            first = jnp.mean(scaled, axis=1, keepdims=True)
            second = jnp.mean(scaled * normed, axis=1, keepdims=True)
            back = scale * (scaled - first - normed * second)
            tokens[there, :] = (direct[there, :].astype(jnp.float32) + back).astype(jnp.bfloat16)
            return state

        state = tuple(ahead[slot_of(j), :] for j in every)
        state = lax.fori_loop(low, high, block_step, state)
        for j in every:
            ahead[slot_of(j), :] = state[j]

    def gathered():
        for piece in range(SUB):
            feat[0 : 2 * NDIM, piece * LANES : (piece + 1) * LANES] = sums[
                pl.ds(piece, 2 * NDIM, stride=SUB), :
            ]
        token.start()
        tiny_feat.start()

    def shared_back():
        low = shared_ring[bits].astype(jnp.bfloat16)
        shared_low[...] = low
        there = shared_out.at[span_of(part, quarter), :]
        pltpu.make_async_copy(shared_low, there, spread_own.at[0]).start()
        for step in range(1, mp):
            to = lax.rem(part + step, mp)
            copy = remote(shared_low, there, spread_send.at[step], spread_recv.at[part], "mp", to)
            copy.start()
            waits.append(copy.wait_send)

    (turned,) = take(1)

    greet(dp, mp)
    for copy in loads:
        copy.start()
    layer.start()
    work = {
        0: [adjoint],
        1: [lambda: params(0, blocks // 2)],
        2: [lambda: params(blocks // 2, blocks)],
        3: [meet, lambda: token_rows(0, blocks // 2)],
        4: [lambda: token_rows(blocks // 2, blocks), gathered],
    }
    jobs = [(pack, i) for pack in packs for i in range(mp)]
    finals = {}
    lags = [1 + LAG * stage_number for stage_number in range(bits)]
    for wave in range(len(jobs) + lags[-1] + bits + 2):
        for stage_number in range(bits):
            number = wave - lags[stage_number]
            if 0 <= number < len(jobs):
                pack, i = jobs[number]
                pack.fold(i, stage_number, number % 2)
                if stage_number == bits - 1 and i == mp - 1:
                    for step in range(bits + 1):
                        finals.setdefault(wave + step, []).append((pack, step))
        if wave < len(jobs):
            jobs[wave][0].begin(jobs[wave][1], wave % 2)
        for pack, step in finals.get(wave, []):
            pack.spread(step)
        for item in work.get(wave, []):
            item()
        if wave == 1:
            layer.turn()
            loads[5].wait()
            loads[6].wait()
            tiny_shared.start()
            tiny_vector.start()
        for item, first in ((tiny_shared, 3), (tiny_vector, 3), (tiny_feat, 7)):
            if 0 <= wave - first <= bits:
                item.fold(wave - first)
        if wave == 3 + bits:
            shared_back()
            vector_out[...] = vector_ring[bits]
        if wave == 7 + bits:
            feat_out[...] = feat_ring[bits]
    arrived(shared_low, spread_own.at[0])
    for step in range(1, mp):
        source = lax.rem(part + step, mp)
        arrived(shared_out.at[span_of(source, quarter), :], spread_recv.at[source])
    token.turn()
    for item in (layer, token):
        item.receive()
        item.close()
    for wait in waits:
        wait()


def closing(dp, mp, span, packs, layer_rows, inputs, shared, vector, params, starts):
    one, two = packs
    low, full = jnp.bfloat16, jnp.float32
    bits = dp.bit_length() - 1
    dma = pltpu.SemaphoreType.DMA
    count = layer_rows.shape[0]
    _, total, width = one.shape
    z = shared.shape[1]
    quarter, columns = D // mp, D // mp

    def vmem(*shape, dtype=full):
        return pltpu.VMEM(shape, dtype)

    scratch = [vmem(2, 2, total // 2, width // 2, dtype=low)]
    for _ in range(2):
        scratch += [vmem(mp, 2, total >> (i + 1), width // 2, dtype=low) for i in range(bits)]
    scratch += [vmem(mp, 2, total // dp, width // 2, dtype=low)] * 2
    scratch += [vmem(2, total // dp, width // 2, dtype=low)] * 2
    scratch += [vmem(count, D)] + [vmem(count, D, dtype=low)] * 5
    scratch += [ROWS, ROWS, pltpu.VMEM(STATES, full), vmem(NDIM * SUB, LANES)]
    scratch += [vmem(2 * NDIM * SUB, LANES), vmem(FEATURES, D)]
    scratch += [
        vmem(D, z, dtype=low), vmem(mp, quarter, z, dtype=low), vmem(bits + 1, quarter, z),
        vmem(bits, quarter, z), vmem(quarter, z, dtype=low),
    ]
    scratch += [vmem(mp, FEATURES, columns), vmem(bits + 1, FEATURES, columns), vmem(bits, FEATURES, columns)]
    scratch += [vmem(8, z), vmem(mp, 8, z), vmem(bits + 1, 8, z), vmem(bits, 8, z)]
    scratch += [dma((2, 2)), dma((7,)), dma((1,)), dma((1,)), dma((mp,)), dma((mp,)), dma((1,))]
    scratch += reduce_sems(dp, mp) * 2 + swap_scratch(mp, count, D // mp) * 2 + tiny_sems(dp, mp) * 3
    scratch += [ROWS]
    near = pl.BlockSpec(memory_space=pltpu.VMEM)
    return pl.pallas_call(
        functools.partial(closing_kernel, dp, mp, span),
        in_specs=[HBM] * 10 + [near] * 6,
        out_specs=[HBM] * 4 + [near, HBM, near],
        out_shape=[
            sds((total, width), low), sds((total, width), low),
            sds((count * mp, D // mp), low), sds((count * mp, D // mp), low),
            sds((FEATURES, columns)), sds((D, z), low), sds((8, z)),
        ],
        scratch_shapes=scratch,
        compiler_params=pltpu.CompilerParams(
            collective_id=2, has_side_effects=True, vmem_limit_bytes=61 << 20
        ),
        name="closing",
    )(one, two, layer_rows, *inputs, shared, vector, *params, starts)


def local(
    dp,
    mp,
    tokens,
    cotangent,
    norm_gain,
    ema_delta,
    ema_alpha,
    ema_beta,
    ema_eta,
    ema_omega,
    shared_proj,
    query_gain,
    query_bias,
    key_gain,
    value_proj,
    gate_proj,
    mixer_proj,
    update_proj,
    output_proj,
    ffn_gain,
    up_proj,
    down_proj,
):
    width = tokens.shape[1]
    count = tokens.shape[0] // mp
    span = LEN // count
    small = jnp.concatenate(
        [
            ema_delta, ema_alpha, ema_beta, ema_eta,
            norm_gain[:, None], ema_omega[:, None], ffn_gain[:, None],
        ],
        axis=1,
    ).T
    lines = small.shape[0]
    small = jnp.pad(small, ((0, -lines % 8), (0, 0)))
    folded = jnp.concatenate([output_proj[:, : D // 2], output_proj[:, D // 2 :]], axis=0)
    pack_one = jnp.concatenate([value_proj, gate_proj, mixer_proj, update_proj, folded], axis=1)
    pack_two = jnp.concatenate([up_proj, down_proj], axis=1)
    vectors = (query_gain[None], query_bias[None], key_gain[None])
    wide, narrow = value_proj.shape[1], mixer_proj.shape[1]
    (
        xn, xp, mix_pre, starts, keep, weight, gains,
        vpre, gpre, att, hidden, act_pre, upd_pre, middle, spre, one, x_low, two, grad_out,
    ) = forward(
        dp, mp, span, mp * wide, jnp.tile(small, (1, mp)), pack_one, tokens, shared_proj, vectors,
        pack_two, cotangent,
    )
    keep, weight = keep.reshape(STATE), weight.reshape(STATE)
    gain, omega, gain_two = gains[0:1], gains[1:2], gains[2:3]
    layer_rows, ffn_in, upper, d_up, d_act, d_upd, d_inputs, ffn_part = ffn(
        middle, grad_out, x_low, act_pre, upd_pre, two, gain_two
    )
    two_grad = ffn_weights(mp, ffn_in, grad_out, upper, d_up)
    d_value, d_gate, d_shared, d_mix_pre, normed_part, vector_sums = mixer_backward(
        d_act, d_upd, vpre, gpre, att, spre, mix_pre, one, shared_proj, *vectors
    )
    one_grad, shared_part = mixer_weights(
        mp, xn, xp, hidden, d_act, d_value, d_gate, d_upd, d_shared
    )

    one_grad, two_grad, layer_out, token_grad, feature, shared_grad, vector_sums = closing(
        dp, mp, span, (one_grad, two_grad), layer_rows,
        (d_mix_pre, xn, x_low, normed_part, d_inputs), shared_part, vector_sums,
        (keep, weight, gain, omega, ffn_part), starts,
    )
    up_grad = two_grad[:, : up_proj.shape[1]].astype(jnp.float32)
    down_grad = two_grad[:, up_proj.shape[1] :].astype(jnp.float32)
    base = 2 * (wide + narrow)
    value_grad = one_grad[:, :wide].astype(jnp.float32)
    gate_grad = one_grad[:, wide : 2 * wide].astype(jnp.float32)
    mixer_grad = one_grad[:, 2 * wide : 2 * wide + narrow].astype(jnp.float32)
    update_grad = one_grad[:, 2 * wide + narrow : base].astype(jnp.float32)
    output_grad = jnp.concatenate(
        [one_grad[:wide, base:], one_grad[wide:, base:]], axis=1
    ).astype(jnp.float32)

    shared_grad = shared_grad.astype(jnp.float32)
    query_grad, bias_grad, key_grad = vector_sums[0], vector_sums[1], vector_sums[2]
    delta, alpha, beta, eta = (
        item.T for item in (ema_delta, ema_alpha, ema_beta, ema_eta)
    )
    rate = jax.nn.sigmoid(delta)
    damp = jax.nn.sigmoid(alpha)
    weight_sum = feature[:NDIM]
    keep_sum = feature[NDIM : 2 * NDIM] * (rate * beta * eta)
    d_rate = weight_sum * beta * eta - keep_sum * damp
    delta_grad = (d_rate * rate * (1.0 - rate)).T
    alpha_grad = (-keep_sum * rate * damp * (1.0 - damp)).T
    beta_grad = (weight_sum * rate * eta).T
    eta_grad = (weight_sum * rate * beta).T
    omega_grad, gain_grad, ffn_grad = feature[2 * NDIM], feature[2 * NDIM + 1], feature[2 * NDIM + 2]
    return (
        layer_out, token_grad, gain_grad, delta_grad, alpha_grad, beta_grad, eta_grad, omega_grad,
        shared_grad, query_grad, bias_grad, key_grad, value_grad, gate_grad, mixer_grad,
        update_grad, output_grad, ffn_grad, up_grad, down_grad,
    )


def solution(mesh):
    dp, mp = mesh.shape["dp"], mesh.shape["mp"]
    params = (
        P("mp"), P("mp", None), P("mp", None), P("mp", None), P("mp", None), P("mp"),
        P(), P(), P(), P(),
        P(None, "mp"), P(None, "mp"), P(None, "mp"), P(None, "mp"), P("mp", None),
        P("mp"), P(None, "mp"), P("mp", None),
    )
    specs = (P("dp", "mp"), P("dp", "mp")) + params
    return jax.shard_map(
        functools.partial(local, dp, mp), mesh=mesh, in_specs=specs, out_specs=specs, check_vma=False
    )
```

```python
import functools

import jax
import jax.numpy as jnp
from jax import lax
from jax.experimental import pallas as pl
from jax.experimental.pallas import tpu as pltpu
from jax.sharding import PartitionSpec as P

D = 1024
GROUP = 128
LEN = 2048
NDIM = 16
LANES = 128
SUB = D // LANES
EPS = 1e-05
TB = 128


def matmul(left, right):
    return jnp.dot(left, right, preferred_element_type=jnp.float32)


def matmul_tn(left, right):
    return lax.dot_general(
        left, right, (((0,), (0,)), ((), ())), preferred_element_type=jnp.float32
    )


def matmul_nt(left, right):
    return lax.dot_general(
        left, right, (((1,), (1,)), ((), ())), preferred_element_type=jnp.float32
    )


def to_rows(scratch, value):
    for part in range(SUB):
        scratch[pl.ds(part, TB, stride=SUB), :] = value[:, part * LANES : (part + 1) * LANES]


def from_rows(scratch):
    return jnp.concatenate(
        [scratch[pl.ds(part, TB, stride=SUB), :] for part in range(SUB)], axis=1
    )


def row(scratch, index):
    return scratch[pl.ds(pl.multiple_of(index * SUB, SUB), SUB), :]


def sds(shape, dtype=jnp.float32):
    return jax.ShapeDtypeStruct(shape, dtype)


def block(reverse=None):
    if reverse is None:
        return pl.BlockSpec((TB, D), lambda i: (i, 0))
    return pl.BlockSpec((TB, D), lambda i: (reverse - 1 - i, 0))


def whole(*shape):
    return pl.BlockSpec(shape, lambda i: (0,) * len(shape))


STATE = (NDIM, SUB, LANES)
STATES = (2 * NDIM, SUB, LANES)
ROWS = pltpu.VMEM((TB * SUB, LANES), jnp.float32)
PARAMS = pltpu.CompilerParams(vmem_limit_bytes=32 << 20)


ROWS_C = 256
ROWS_E = 128
LEAD = 8
LAG = 2
SPLIT = 2


def sigmoid(value):
    return 0.5 + 0.5 * jnp.tanh(0.5 * value)


def causal_probs(query, keys, head_scale):
    scores = matmul_nt(query, keys) * head_scale
    down = lax.broadcasted_iota(jnp.int32, scores.shape, 0)
    across = lax.broadcasted_iota(jnp.int32, scores.shape, 1)
    scores = jnp.where(down >= across, scores, -1e30)
    weights = jnp.exp(scores - jnp.max(scores, axis=1, keepdims=True))
    return weights / jnp.sum(weights, axis=1, keepdims=True)


def mixer_forward_kernel(
    xn_ref, xp_ref, x_ref, one_ref, shared_ref, qgain_ref, qbias_ref, kgain_ref,
    vpre_ref, gpre_ref, att_ref, hid_ref, act_ref, upd_ref, mid_ref, spre_ref,
):
    mp = one_ref.shape[0]
    narrow = D // mp
    wide = vpre_ref.shape[1] // mp
    base = 2 * (wide + narrow)
    groups = ROWS_C // GROUP
    xn, xp = xn_ref[...], xp_ref[...]
    shared_pre = matmul(xp, shared_ref[...])
    spre_ref[...] = shared_pre
    shared = shared_pre * sigmoid(shared_pre)
    query = (shared * qgain_ref[...] + qbias_ref[...]).astype(jnp.bfloat16)
    keys = (shared * kgain_ref[...]).astype(jnp.bfloat16)
    head_scale = shared.shape[1] ** (-0.5)
    probs = [
        causal_probs(
            query[g * GROUP : (g + 1) * GROUP], keys[g * GROUP : (g + 1) * GROUP], head_scale
        ).astype(jnp.bfloat16)
        for g in range(groups)
    ]
    attn_out = None
    for m in range(mp):
        span = slice(m * wide, (m + 1) * wide)
        value_pre = matmul(xn, one_ref[m, :, 0:wide])
        values = (value_pre * sigmoid(value_pre)).astype(jnp.bfloat16)
        vpre_ref[:, span] = value_pre.astype(jnp.bfloat16)
        gate_pre = matmul(xp, one_ref[m, :, wide : 2 * wide])
        gate = gate_pre * sigmoid(gate_pre)
        gpre_ref[:, span] = gate_pre.astype(jnp.bfloat16)
        attended = jnp.concatenate(
            [matmul(probs[g], values[g * GROUP : (g + 1) * GROUP]) for g in range(groups)], axis=0
        )
        att_ref[:, span] = attended.astype(jnp.bfloat16)
        hidden = (gate * attended).astype(jnp.bfloat16)
        hid_ref[:, span] = hidden
        term = jnp.concatenate(
            [matmul(hidden, one_ref[m, 0:wide, base:]), matmul(hidden, one_ref[m, wide:, base:])], axis=1
        )
        attn_out = term if attn_out is None else attn_out + term
    for m in range(mp):
        span = slice(m * narrow, (m + 1) * narrow)
        act = matmul(xp, one_ref[m, :, 2 * wide : 2 * wide + narrow]) + attn_out[:, span]
        upd = matmul(xp, one_ref[m, :, 2 * wide + narrow : base])
        update = sigmoid(upd)
        act_ref[:, span] = act.astype(jnp.bfloat16)
        upd_ref[:, span] = upd.astype(jnp.bfloat16)
        x = x_ref[:, span].astype(jnp.float32)
        mid_ref[:, span] = x + update * (act * sigmoid(act) - x)


def ffn_kernel(
    mid_ref, grad_ref, x_ref, act_ref, upd_ref, two_ref, gain_ref,
    layer_ref, ffn_ref, upper_ref, dup_ref, dact_ref, dupd_ref, dx_ref, gsum_ref,
):
    mp, _, total = two_ref.shape
    units = total - D
    sub = 512
    middle = mid_ref[...]
    grad = grad_ref[...]
    mean = jnp.mean(middle, axis=1, keepdims=True)
    power = jnp.mean(middle * middle, axis=1, keepdims=True)
    scale = lax.rsqrt(power - mean * mean + EPS)
    normed = (middle - mean) * scale
    gain = gain_ref[...]
    ffn_in = (normed * gain).astype(jnp.bfloat16)
    ffn_ref[...] = ffn_in
    down_out = None
    d_ffn = None
    for m in range(mp):
        for first in range(0, units, sub):
            columns = slice(m * units + first, m * units + first + sub)
            up_weights = two_ref[m, :, first : first + sub]
            down_weights = two_ref[m, first : first + sub, units:]
            up_pre = matmul(ffn_in, up_weights)
            logistic = sigmoid(up_pre)
            value = up_pre * logistic
            upper = value.astype(jnp.bfloat16)
            upper_ref[:, columns] = upper
            slope = logistic + value - value * logistic
            d_up = (matmul_nt(grad, down_weights) * slope).astype(jnp.bfloat16)
            dup_ref[:, columns] = d_up
            term = matmul(upper, down_weights)
            down_out = term if down_out is None else down_out + term
            term = matmul_nt(d_up, up_weights)
            d_ffn = term if d_ffn is None else d_ffn + term
    layer_ref[...] = (middle + down_out).astype(jnp.bfloat16)

    @pl.when(pl.program_id(0) == 0)
    def _():
        gsum_ref[...] = jnp.zeros_like(gsum_ref)

    gsum_ref[...] += jnp.sum(d_ffn * normed, axis=0, keepdims=True)
    scaled = d_ffn * gain
    first = jnp.mean(scaled, axis=1, keepdims=True)
    second = jnp.mean(scaled * normed, axis=1, keepdims=True)
    d_middle = grad.astype(jnp.float32) + scale * (scaled - first - normed * second)
    act = act_ref[...].astype(jnp.float32)
    update = sigmoid(upd_ref[...].astype(jnp.float32))
    logistic = sigmoid(act)
    value = act * logistic
    x = x_ref[...].astype(jnp.float32)
    d_update = d_middle * update
    dact_ref[...] = (d_update * (logistic + value - value * logistic)).astype(jnp.bfloat16)
    dupd_ref[...] = (d_update * (value - x) * (1.0 - update)).astype(jnp.bfloat16)
    dx_ref[...] = (d_middle - d_update).astype(jnp.bfloat16)


def backward_kernel(dp, mp, pack_ref, layer_ref, *refs):
    ins, outs, refs = refs[:12], refs[12:18], refs[18:]
    sums_out, layer_out = refs[:2]
    layer = Swap(mp, layer_ref, layer_out, refs[2:6], back=True)
    _, total, width = pack_ref.shape
    plan, refs = reduce_plan(dp, mp, pack_ref, total, width, refs[6:], 0, SPLIT)
    plan.sums, plan.sums_sem = sums_out, refs[0]
    index = pl.program_id(0)
    steps = pl.num_programs(0)

    @pl.when(index == 0)
    def _():
        greet(dp, mp)
        plan.wave(0)
        layer.start()

    for number in range(1, LEAD):

        @pl.when(index == number)
        def _(number=number):
            plan.wave(number)
            if number == 1:
                layer.turn()

    mixer_backward_kernel(*ins, *outs)

    @pl.when(index == steps - 1)
    def _():
        for number in range(LEAD, plan.waves()):
            plan.wave(number)
        layer.receive()
        layer.close()
        plan.close()


def mixer_backward_kernel(
    dact_ref, dupd_ref, vpre_ref, gpre_ref, att_ref, spre_ref, mix_ref, one_ref, shared_ref,
    qgain_ref, qbias_ref, kgain_ref,
    dv_ref, dg_ref, dshared_ref, dmix_ref, dxn_ref, sums_ref,
):
    mp = one_ref.shape[0]
    narrow = D // mp
    wide = vpre_ref.shape[1] // mp
    base = 2 * (wide + narrow)
    groups = dact_ref.shape[0] // GROUP
    shared_pre = spre_ref[...]
    logistic = sigmoid(shared_pre)
    shared = shared_pre * logistic
    query = (shared * qgain_ref[...] + qbias_ref[...]).astype(jnp.bfloat16)
    keys = (shared * kgain_ref[...]).astype(jnp.bfloat16)
    head_scale = shared.shape[1] ** (-0.5)
    rows = [slice(g * GROUP, (g + 1) * GROUP) for g in range(groups)]
    probs = [causal_probs(query[rows[g]], keys[rows[g]], head_scale) for g in range(groups)]
    probs_low = [item.astype(jnp.bfloat16) for item in probs]
    d_act = dact_ref[...]
    d_probs = [None] * groups
    d_xp = None
    d_xn = None
    for m in range(mp):
        span = slice(m * wide, (m + 1) * wide)
        thin = slice(m * narrow, (m + 1) * narrow)
        d_hidden = matmul_nt(d_act[:, : D // 2], one_ref[m, 0:wide, base:]) + matmul_nt(
            d_act[:, D // 2 :], one_ref[m, wide:, base:]
        )
        gate_pre = gpre_ref[:, span].astype(jnp.float32)
        gate_log = sigmoid(gate_pre)
        gate = gate_pre * gate_log
        attended = att_ref[:, span].astype(jnp.float32)
        d_gate = (d_hidden * attended * (gate_log + gate - gate * gate_log)).astype(jnp.bfloat16)
        dg_ref[:, span] = d_gate
        d_att = (d_hidden * gate).astype(jnp.bfloat16)
        value_pre = vpre_ref[:, span].astype(jnp.float32)
        value_log = sigmoid(value_pre)
        value = value_pre * value_log
        values = value.astype(jnp.bfloat16)
        parts = []
        for g in range(groups):
            term = matmul_nt(d_att[rows[g]], values[rows[g]])
            d_probs[g] = term if d_probs[g] is None else d_probs[g] + term
            parts.append(matmul_tn(probs_low[g], d_att[rows[g]]))
        d_value = jnp.concatenate(parts, axis=0)
        d_value_pre = (d_value * (value_log + value - value * value_log)).astype(jnp.bfloat16)
        dv_ref[:, span] = d_value_pre
        term = (
            matmul_nt(d_gate, one_ref[m, :, wide : 2 * wide])
            + matmul_nt(d_act[:, thin], one_ref[m, :, 2 * wide : 2 * wide + narrow])
            + matmul_nt(dupd_ref[:, thin], one_ref[m, :, 2 * wide + narrow : base])
        )
        d_xp = term if d_xp is None else d_xp + term
        term = matmul_nt(d_value_pre, one_ref[m, :, 0:wide])
        d_xn = term if d_xn is None else d_xn + term
    dxn_ref[...] = d_xn.astype(jnp.bfloat16)
    d_query, d_keys = [], []
    for g in range(groups):
        d_scores = probs[g] * (d_probs[g] - jnp.sum(probs[g] * d_probs[g], axis=1, keepdims=True))
        low = d_scores.astype(jnp.bfloat16)
        d_query.append(matmul(low, keys[rows[g]]) * head_scale)
        d_keys.append(matmul_tn(low, query[rows[g]]) * head_scale)
    d_query = jnp.concatenate(d_query, axis=0)
    d_keys = jnp.concatenate(d_keys, axis=0)

    @pl.when(pl.program_id(0) == 0)
    def _():
        sums_ref[...] = jnp.zeros_like(sums_ref)

    sums_ref[0:1, :] += jnp.sum(d_query * shared, axis=0, keepdims=True)
    sums_ref[1:2, :] += jnp.sum(d_query, axis=0, keepdims=True)
    sums_ref[2:3, :] += jnp.sum(d_keys * shared, axis=0, keepdims=True)
    d_shared = (d_query * qgain_ref[...] + d_keys * kgain_ref[...]) * (
        logistic + shared - shared * logistic
    )
    d_shared = d_shared.astype(jnp.bfloat16)
    dshared_ref[...] = d_shared
    d_xp = d_xp + matmul_nt(d_shared, shared_ref[...])
    mix = mix_ref[...]
    mix_log = sigmoid(mix)
    mix_value = mix * mix_log
    dmix_ref[...] = d_xp * (mix_log + mix_value - mix_value * mix_log)


def mixer_weights_kernel(
    xn_ref, xp_ref, hid_ref, dact_all_ref, dv_ref, dg_ref, dact_ref, dupd_ref, dshared_ref,
    one_ref, shared_ref, xnt, xpt,
):
    wide, narrow = dv_ref.shape[1], dact_ref.shape[1]

    @pl.when(pl.program_id(0) == 0)
    def _():
        xnt[...] = xn_ref[...].T
        xpt[...] = xp_ref[...].T
        shared_ref[...] = matmul(xpt[...], dshared_ref[...]).astype(jnp.bfloat16)

    one_ref[0, :, 0:wide] = matmul(xnt[...], dv_ref[...]).astype(jnp.bfloat16)
    one_ref[0, :, wide : 2 * wide] = matmul(xpt[...], dg_ref[...]).astype(jnp.bfloat16)
    one_ref[0, :, 2 * wide : 2 * wide + narrow] = matmul(xpt[...], dact_ref[...]).astype(jnp.bfloat16)
    base = 2 * (wide + narrow)
    one_ref[0, :, 2 * wide + narrow : base] = matmul(xpt[...], dupd_ref[...]).astype(jnp.bfloat16)
    out = matmul_tn(hid_ref[...], dact_all_ref[...]).astype(jnp.bfloat16)
    one_ref[0, 0:wide, base:] = out[:, : D // 2]
    one_ref[0, wide:, base:] = out[:, D // 2 :]


def ffn_weights_kernel(ffn_ref, grad_ref, upper_ref, dup_ref, two_ref, fft):
    units = dup_ref.shape[1]

    @pl.when(pl.program_id(0) == 0)
    def _():
        fft[...] = ffn_ref[...].T

    two_ref[0, :, 0:units] = matmul(fft[...], dup_ref[...]).astype(jnp.bfloat16)
    two_ref[0, :, units:] = matmul_tn(upper_ref[...], grad_ref[...]).astype(jnp.bfloat16)


def held(*shape):
    return pl.BlockSpec(shape, lambda i: (0,) * len(shape), pipeline_mode=pl.Buffered(1))


def rows_block(width):
    return pl.BlockSpec((ROWS_C, width), lambda i: (i, 0))


BIG = pltpu.CompilerParams(vmem_limit_bytes=60 << 20)


def cost(flops, bytes_accessed):
    return pl.CostEstimate(flops=int(flops), transcendentals=0, bytes_accessed=int(bytes_accessed))


def ffn(middle, grad, x, act, upd, two, gain):
    count = x.shape[0]
    units = two.shape[0] * (two.shape[2] - D)
    low = jnp.bfloat16
    return pl.pallas_call(
        ffn_kernel,
        grid=(count // ROWS_C,),
        in_specs=[rows_block(D)] * 5 + [held(*two.shape), held(1, D)],
        out_specs=[rows_block(D)] * 2 + [rows_block(units)] * 2 + [rows_block(D)] * 3 + [whole(1, D)],
        out_shape=[sds((count, D), low)] * 2
        + [sds((count, units), low)] * 2
        + [sds((count, D), low)] * 3
        + [sds((1, D))],
        compiler_params=BIG,
        cost_estimate=cost(4 * count * two.size, 60 << 20),
        name="ffn",
    )(middle, grad, x, act, upd, two, gain)


def mixer_backward(
    dp, mp, d_act, d_upd, vpre, gpre, att, spre, mix, one, shared, qgain, qbias, kgain, pack, layer
):
    count = d_act.shape[0]
    units = vpre.shape[1]
    z = shared.shape[1]
    low = jnp.bfloat16

    def part(width):
        return pl.BlockSpec((ROWS_E, width), lambda i: (i, 0))

    return pl.pallas_call(
        functools.partial(backward_kernel, dp, mp),
        grid=(count // ROWS_E,),
        in_specs=[HBM, HBM]
        + [part(D)] * 2
        + [part(units)] * 3
        + [part(z), part(D)]
        + [held(*one.shape), held(*shared.shape)]
        + [held(1, z)] * 3,
        out_specs=[part(units)] * 2 + [part(z), part(D), part(D), whole(8, z)] + [HBM] * 2,
        out_shape=[sds((count, units), low)] * 2
        + [sds((count, z), low), sds((count, D)), sds((count, D), low), sds((8, z))]
        + [sds((mp, 2, pack.shape[1] >> SPLIT, pack.shape[2] // 2), low), sds((count * mp, D // mp), low)],
        scratch_shapes=swap_scratch(mp, count, D // mp)
        + reduce_scratch(dp, mp, pack.shape[1], pack.shape[2], 0, SPLIT)
        + [pltpu.SemaphoreType.DMA((mp, 2))],
        compiler_params=pltpu.CompilerParams(
            collective_id=3, has_side_effects=True, vmem_limit_bytes=61 << 20
        ),
        name="mixer_backward",
    )(pack, layer, d_act, d_upd, vpre, gpre, att, spre, mix, one, shared, qgain, qbias, kgain)


def mixer_weights(mp, xn, xp, hidden, d_act, d_value, d_gate, d_upd, d_shared):
    count = xn.shape[0]
    wide, narrow, z = d_value.shape[1] // mp, D // mp, d_shared.shape[1]
    low = jnp.bfloat16

    def part(width):
        return pl.BlockSpec((count, width), lambda i: (0, i))

    return pl.pallas_call(
        mixer_weights_kernel,
        grid=(mp,),
        in_specs=[held(count, D), held(count, D), part(wide), held(count, D)]
        + [part(wide), part(wide), part(narrow), part(narrow), held(count, z)],
        out_specs=[
            pl.BlockSpec((1, D, 2 * (wide + narrow) + D // 2), lambda i: (i, 0, 0)),
            whole(D, z),
        ],
        out_shape=[sds((mp, D, 2 * (wide + narrow) + D // 2), low), sds((D, z), low)],
        scratch_shapes=[pltpu.VMEM((D, count), low), pltpu.VMEM((D, count), low)],
        compiler_params=BIG,
        cost_estimate=cost(2 * count * D * mp * (3 * wide + 2 * narrow), 40 << 20),
        name="mixer_weights",
    )(xn, xp, hidden, d_act, d_value, d_gate, d_act, d_upd, d_shared)


def ffn_weights(mp, ffn_in, grad, upper, d_up):
    count = ffn_in.shape[0]
    units = upper.shape[1] // mp
    low = jnp.bfloat16

    def part(width):
        return pl.BlockSpec((count, width), lambda i: (0, i))

    return pl.pallas_call(
        ffn_weights_kernel,
        grid=(mp,),
        in_specs=[held(count, D), held(count, D), part(units), part(units)],
        out_specs=pl.BlockSpec((1, D, units + D), lambda i: (i, 0, 0)),
        out_shape=sds((mp, D, units + D), low),
        scratch_shapes=[pltpu.VMEM((D, count), low)],
        compiler_params=BIG,
        cost_estimate=cost(4 * count * D * mp * units, 40 << 20),
        name="ffn_weights",
    )(ffn_in, grad, upper, d_up)


MESH = pl.DeviceIdType.MESH


def rank_of(index, order):
    total = 0
    for place, bit in enumerate(order):
        total = total + lax.rem(lax.div(index, 1 << bit), 2) * (1 << place)
    return total


def flip(index, bit):
    low = lax.rem(lax.div(index, 1 << bit), 2)
    return index + (1 - 2 * low) * (1 << bit)


def orders_of(dp):
    bits = dp.bit_length() - 1
    inner = list(range(1, bits))
    return (inner + [0], inner[::-1] + [0])


def greet(dp, mp):
    me = lax.axis_index("dp")
    part = lax.axis_index("mp")
    bits = dp.bit_length() - 1
    barrier = pltpu.get_barrier_semaphore()
    for step in range(1, mp):
        pl.semaphore_signal(
            barrier, inc=1, device_id={"mp": lax.rem(part + step, mp)}, device_id_type=MESH
        )
    for bit in range(bits):
        pl.semaphore_signal(barrier, inc=1, device_id={"dp": flip(me, bit)}, device_id_type=MESH)
    pl.semaphore_wait(barrier, mp - 1 + bits)


def arrived(ref, sem):
    pltpu.make_async_copy(ref, ref, sem).wait()


def remote(src, dst, send_sem, recv_sem, axis, to):
    return pltpu.make_async_remote_copy(
        src_ref=src, dst_ref=dst, send_sem=send_sem, recv_sem=recv_sem,
        device_id={axis: to}, device_id_type=MESH,
    )


def span_of(index, size):
    return pl.ds(pl.multiple_of(index * size, size), size)


class Swap:
    def __init__(self, mp, src, dst, sems, back=False):
        self.mp, self.src, self.dst, self.back = mp, src, dst, back
        self.hold, self.send, self.recv, self.own = sems
        self.part = lax.axis_index("mp")
        if back:
            self.rows, self.width = src.shape[0], dst.shape[1]
        else:
            self.rows, self.width = dst.shape[0], src.shape[1]

    def piece(self, index):
        if self.back:
            return self.src.at[:, span_of(index, self.width)]
        return self.src.at[span_of(index, self.rows), :]

    def place(self, index):
        if self.back:
            return self.dst.at[span_of(index, self.rows), :]
        return self.dst.at[:, span_of(index, self.width)]

    def load(self):
        return pltpu.make_async_copy(self.piece(self.part), self.hold, self.own.at[0])

    def store(self):
        return pltpu.make_async_copy(self.hold, self.place(self.part), self.own.at[1])

    def copies(self):
        for step in range(1, self.mp):
            to = lax.rem(self.part + step, self.mp)
            yield remote(
                self.piece(to), self.place(self.part),
                self.send.at[step], self.recv.at[self.part], "mp", to,
            )

    def start(self):
        self.load().start()
        for copy in self.copies():
            copy.start()

    def turn(self):
        self.load().wait()
        self.store().start()

    def receive(self):
        self.store().wait()
        for step in range(1, self.mp):
            source = lax.rem(self.part + step, self.mp)
            arrived(self.place(source), self.recv.at[source])

    def close(self):
        for copy in self.copies():
            copy.wait_send()


class Gather:
    def __init__(self, dp, mp, srcs, dst, sems):
        self.dp, self.mp, self.srcs, self.dst = dp, mp, srcs, dst
        self.hold, self.line_send, self.pass_send, self.line_recv, self.send, self.recv, self.own = sems
        self.me, self.part = lax.axis_index("dp"), lax.axis_index("mp")
        self.bits = dp.bit_length() - 1
        self.orders = orders_of(dp)

    def region(self, ref, half, index, held):
        total = ref.shape[0] // 2
        share = total // self.dp
        first = lax.div(rank_of(index, self.orders[half]), 1 << held) * (share << held)
        return ref.at[pl.ds(pl.multiple_of(half * total + first, share), share << held), :]

    def spans(self):
        first = 0
        for ref in self.srcs:
            folded = ref.shape[0] < self.dst.shape[1]
            width = ref.shape[1] // 2 if folded else ref.shape[1]
            yield ref, slice(first, first + width), width, folded
            first += width

    def loads(self):
        there = self.dst.at[self.part] if self.hold is None else self.hold
        total = self.dst.shape[1] // 2
        for place, (ref, columns, width, folded) in enumerate(self.spans()):
            if not folded:
                yield pltpu.make_async_copy(ref, there.at[:, columns], self.own.at[place])
                continue
            for half in range(2):
                yield pltpu.make_async_copy(
                    ref.at[:, half * width : (half + 1) * width],
                    there.at[half * total : (half + 1) * total, columns],
                    self.own.at[place + half],
                )

    def store(self):
        return pltpu.make_async_copy(self.hold, self.dst.at[self.part], self.own.at[7])

    def turn(self):
        for copy in self.loads():
            copy.wait()
        if self.hold is not None:
            self.store().start()

    def first(self, up):
        to = self.part + 1 if up else self.part - 1
        total = self.dst.shape[1] // 2
        share = total // self.dp
        for half in range(2):
            first = pl.multiple_of(rank_of(self.me, self.orders[half]) * share, share)
            whole_rows = pl.ds(pl.multiple_of(half * total + first, share), share)
            for place, (ref, columns, width, folded) in enumerate(self.spans()):
                if folded:
                    piece = ref.at[pl.ds(first, share), half * width : (half + 1) * width]
                else:
                    piece = ref.at[whole_rows, :]
                yield remote(
                    piece, self.dst.at[self.part].at[whole_rows, columns],
                    self.line_send.at[place, int(up), half], self.line_recv.at[self.part, half],
                    "mp", to,
                )

    def passed(self, source):
        to = jnp.where(source < self.part, self.part + 1, self.part - 1)
        for half in range(2):
            held = self.region(self.dst.at[source], half, self.me, 0)
            yield remote(
                held, held, self.pass_send.at[source, half], self.line_recv.at[source, half], "mp", to
            )

    def passes(self, source):
        return jnp.logical_or(
            jnp.logical_and(source < self.part, self.part < self.mp - 1),
            jnp.logical_and(source > self.part, self.part > 0),
        )

    def doubled(self, source, stage):
        for half in range(2):
            held = self.region(self.dst.at[source], half, self.me, stage)
            yield remote(
                held, held, self.send.at[stage, source, half], self.recv.at[stage, source, half],
                "dp", flip(self.me, self.orders[half][stage]),
            )

    def source(self, step):
        mp, part = self.mp, self.part
        near = [lax.rem(part + 1, 2) + part - lax.rem(part, 2)]
        low = lax.div(part, mp // 2) == 0
        far = [jnp.where(low, mp // 2 + i, mp // 2 - 1 - i) for i in range(mp // 2)]
        return (near + far)[step]

    def start(self):
        for up in (True, False):

            @pl.when(self.part < self.mp - 1 if up else self.part > 0)
            def _(up=up):
                for copy in self.first(up):
                    copy.start()

        for copy in self.loads():
            copy.start()

    def advance(self, step, stage):
        source = self.source(step)
        for half in range(2):
            if stage == 0:
                came = self.region(self.dst.at[source], half, self.me, 0)
                arrived(came, self.line_recv.at[source, half])
            else:
                other = flip(self.me, self.orders[half][stage - 1])
                came = self.region(self.dst.at[source], half, other, stage - 1)
                arrived(came, self.recv.at[stage - 1, source, half])
        if stage == 0:

            @pl.when(self.passes(source))
            def _():
                for copy in self.passed(source):
                    copy.start()

        if stage < self.bits:
            for copy in self.doubled(source, stage):
                copy.start()

    def waves(self):
        return self.mp - 1 + self.bits

    def wave(self, number):
        for stage in range(self.bits, -1, -1):
            if 0 <= number - stage < self.mp - 1:
                self.advance(number - stage, stage)

    def close(self):
        if self.hold is not None:
            self.store().wait()
        for up in (True, False):

            @pl.when(self.part < self.mp - 1 if up else self.part > 0)
            def _(up=up):
                for copy in self.first(up):
                    copy.wait_send()

        for step in range(self.mp - 1):
            source = self.source(step)

            @pl.when(self.passes(source))
            def _(source=source):
                for copy in self.passed(source):
                    copy.wait_send()

            for stage in range(self.bits):
                for copy in self.doubled(source, stage):
                    copy.wait_send()


def swap_scratch(mp, rows, width, dtype=jnp.bfloat16):
    dma = pltpu.SemaphoreType.DMA
    return [pltpu.VMEM((rows, width), dtype), dma((mp,)), dma((mp,)), dma((2,))]


def gather_scratch(dp, mp, pack):
    dma = pltpu.SemaphoreType.DMA
    bits = dp.bit_length() - 1
    return [
        pltpu.VMEM(pack.shape, pack.dtype), dma((5, 2, 2)), dma((mp, 2)), dma((mp, 2)),
        dma((bits, mp, 2)), dma((bits, mp, 2)), dma((8,)),
    ]


HBM = pl.BlockSpec(memory_space=pl.ANY)


def forward_kernel(
    dp, mp, span,
    small_ref, v_ref, g_ref, m_ref, u_ref, o_ref, tok_ref, shared_ref, qgain_ref, qbias_ref, kgain_ref,
    up_ref, down_ref, cot_ref,
    xn_ref, xp_ref, mix_ref, starts_ref, keep_ref, weight_ref, gains_ref,
    vpre_ref, gpre_ref, att_ref, hid_ref, act_ref, upd_ref, mid_ref, spre_ref,
    one_out, x_out, full_ref, grad_ref,
    one_ref, x_all, small_all, xn_all, rows, outs, ends, starts, state_ref,
    carry_send, carry_recv, out_sem, *sems,
):
    index = pl.program_id(0)
    steps = pl.num_programs(0) // 2
    part = lax.axis_index("mp")
    swap = Swap(mp, cot_ref, grad_ref, sems[0:4])
    plan = Gather(dp, mp, (up_ref, down_ref), full_ref, sems[4:11])
    tokens = Swap(mp, tok_ref, x_all, sems[11:15])
    tiny = Swap(mp, small_ref, small_all, sems[15:19], back=True)
    firsts = (v_ref, g_ref, m_ref, u_ref, o_ref)
    opening = Gather(dp, mp, firsts, one_ref, (None,) + tuple(sems[19:25]))
    gives = lax.rem(part + 1, span) != 0
    takes = lax.rem(part, span) != 0
    gain_ref, omega_ref = gains_ref.at[0:1, :], gains_ref.at[1:2, :]

    def carry():
        return remote(ends, starts, carry_send.at[0], carry_recv.at[0], "mp", part + 1)

    def one_copy():
        return pltpu.make_async_copy(one_ref, one_out, out_sem.at[0])

    def x_copy():
        return pltpu.make_async_copy(x_all, x_out, out_sem.at[1])

    @pl.when(index == 0)
    def _():
        greet(dp, mp)
        tiny.start()
        opening.start()
        tiny.turn()
        opening.turn()
        for number in range(opening.waves()):
            opening.wave(number)
            if number == 0:
                tokens.start()
            if number == 2:
                plan.start()
            if number == 4:
                swap.start()
        tokens.turn()
        tiny.receive()
        lines = small_all.shape[0] // mp
        width = small_all.shape[1]
        gains_ref[...] = jnp.zeros_like(gains_ref)
        for m in range(mp):
            block = small_all[m * lines : (m + 1) * lines, :]
            delta, alpha, beta, eta = (block[NDIM * i : NDIM * (i + 1), :] for i in range(4))
            rate = jax.nn.sigmoid(delta)
            keep = 1.0 - rate * jax.nn.sigmoid(alpha)
            weight = rate * beta * eta
            for piece in range(width // LANES):
                there = pl.ds(m * (width // LANES) + piece, NDIM, stride=SUB)
                keep_ref[there, :] = keep[:, piece * LANES : (piece + 1) * LANES]
                weight_ref[there, :] = weight[:, piece * LANES : (piece + 1) * LANES]
            gains_ref[0:3, m * width : (m + 1) * width] = block[4 * NDIM : 4 * NDIM + 3, :]
        tokens.receive()
        one_copy().start()
        x_copy().start()
        ends[...] = jnp.zeros_like(ends)

    @pl.when(index < steps)
    def _():
        keep = [keep_ref[j * SUB : (j + 1) * SUB, :] for j in range(NDIM)]
        for piece in range(ROWS_C // TB):
            here = slice(piece * TB, (piece + 1) * TB)
            x = x_all[
                pl.ds(pl.multiple_of(index * ROWS_C + piece * TB, TB), TB), :
            ].astype(jnp.float32)
            mean = jnp.mean(x, axis=1, keepdims=True)
            power = jnp.mean(x * x, axis=1, keepdims=True)
            scale = lax.rsqrt(power - mean * mean + EPS)
            xn = ((x - mean) * scale * gain_ref[...]).astype(jnp.bfloat16)
            xn_ref[here, :] = xn
            xn_all[pl.ds(pl.multiple_of(index * ROWS_C + piece * TB, TB), TB), :] = xn
            to_rows(rows, xn.astype(jnp.float32))

            def step(t, carried):
                state, slope = carried
                now = row(rows, t)
                slope = tuple(keep[j] * slope[j] + state[j] for j in range(NDIM))
                state = tuple(keep[j] * state[j] + now for j in range(NDIM))
                return (state, slope)

            state = tuple(ends[j] for j in range(NDIM))
            slope = tuple(ends[NDIM + j] for j in range(NDIM))
            state, slope = lax.fori_loop(0, TB, step, (state, slope), unroll=4)
            for j in range(NDIM):
                ends[j] = state[j]
                ends[NDIM + j] = slope[j]

    @pl.when(index == steps - 1)
    def _():
        @pl.when(gives)
        def _():
            carry().start()

        plan.turn()

    @pl.when(index == steps)
    def _():
        @pl.when(jnp.logical_not(takes))
        def _():
            starts[...] = jnp.zeros_like(starts)

        @pl.when(takes)
        def _():
            arrived(starts, carry_recv.at[0])

        @pl.when(gives)
        def _():
            carry().wait_send()

        for j in range(NDIM):
            state_ref[j] = starts[j]
        starts_ref[...] = starts[...]

    @pl.when(index >= steps)
    def _():
        for piece in range(ROWS_C // TB):
            here = slice(piece * TB, (piece + 1) * TB)
            xn = xn_all[
                pl.ds(pl.multiple_of((index - steps) * ROWS_C + piece * TB, TB), TB), :
            ].astype(jnp.float32)
            to_rows(rows, xn)
            keep = [keep_ref[j * SUB : (j + 1) * SUB, :] for j in range(NDIM)]

            def step(t, state):
                now = row(rows, t)
                state = tuple(keep[j] * state[j] + now for j in range(NDIM))
                terms = [weight_ref[j * SUB : (j + 1) * SUB, :] * state[j] for j in range(NDIM)]
                while len(terms) > 1:
                    terms = [a + b for a, b in zip(terms[::2], terms[1::2])]
                outs[pl.ds(pl.multiple_of(t * SUB, SUB), SUB), :] = terms[0]
                return state

            state = lax.fori_loop(0, TB, step, tuple(state_ref[j] for j in range(NDIM)), unroll=4)
            for j in range(NDIM):
                state_ref[j] = state[j]
            mix = from_rows(outs) + omega_ref[...] * xn
            mix_ref[here, :] = mix
            xp_ref[here, :] = (mix * sigmoid(mix)).astype(jnp.bfloat16)

        there = pl.ds(pl.multiple_of((index - steps) * ROWS_C, ROWS_C), ROWS_C)
        mixer_forward_kernel(
            xn_all.at[there, :], xp_ref, x_all.at[there, :], one_ref, shared_ref, qgain_ref, qbias_ref, kgain_ref,
            vpre_ref, gpre_ref, att_ref, hid_ref, act_ref, upd_ref, mid_ref, spre_ref,
        )

    for number in range(plan.waves()):

        @pl.when(index == jnp.minimum(number + 2, 2 * steps - 1))
        def _(number=number):
            plan.wave(number)

    @pl.when(index == 2 * steps - 1)
    def _():
        swap.turn()
        swap.receive()
        for item in (swap, plan, tokens, tiny, opening):
            item.close()
        one_copy().wait()
        x_copy().wait()


def forward(dp, mp, span, units, small, firsts, tokens, shared, vectors, packs, cotangent):
    count = tokens.shape[0] // mp
    steps = count // ROWS_C
    z = shared.shape[1]
    low = jnp.bfloat16
    early = pl.BlockSpec((ROWS_C, D), lambda i: (jnp.minimum(i, steps - 1), 0))

    def late(width):
        return pl.BlockSpec((ROWS_C, width), lambda i: (jnp.maximum(i - steps, 0), 0))

    dma = pltpu.SemaphoreType.DMA
    lines, width = small.shape[0], small.shape[1] // mp
    first = sds((D, sum(item.size for item in firsts) // D), low)
    pack = sds((D, sum(item.size for item in packs) // D), low)
    return pl.pallas_call(
        functools.partial(forward_kernel, dp, mp, span),
        grid=(2 * steps,),
        in_specs=[HBM] * 7 + [held(*shared.shape)] + [held(1, z)] * 3 + [HBM] * 3,
        out_specs=[early, late(D), late(D), whole(*STATES)]
        + [whole(NDIM * SUB, LANES)] * 2
        + [whole(8, D)]
        + [late(units)] * 4
        + [late(D)] * 3
        + [late(z)]
        + [HBM] * 4,
        out_shape=[sds((count, D), low), sds((count, D), low), sds((count, D)), sds(STATES)]
        + [sds((NDIM * SUB, LANES))] * 2
        + [sds((8, D))]
        + [sds((count, units), low)] * 4
        + [sds((count, D), low)] * 2
        + [sds((count, D)), sds((count, z))]
        + [sds((mp,) + first.shape, low), sds((count, D), low)]
        + [sds((mp,) + pack.shape, low), sds((count, D), low)],
        scratch_shapes=[
            pltpu.VMEM((mp,) + first.shape, low), pltpu.VMEM((count, D), low),
            pltpu.VMEM((mp * lines, width), jnp.float32), pltpu.VMEM((count, D), low), ROWS, ROWS,
            pltpu.VMEM(STATES, jnp.float32), pltpu.VMEM(STATES, jnp.float32),
            pltpu.VMEM(STATE, jnp.float32), dma((1,)), dma((1,)), dma((2,)),
        ]
        + swap_scratch(mp, count, cotangent.shape[1])
        + gather_scratch(dp, mp, pack)
        + swap_scratch(mp, count, tokens.shape[1])
        + swap_scratch(mp, lines, width, small.dtype)
        + gather_scratch(dp, mp, first)[1:],
        compiler_params=pltpu.CompilerParams(
            collective_id=1, has_side_effects=True, vmem_limit_bytes=61 << 20
        ),
        name="forward",
    )(small, *firsts, tokens, shared, *vectors, *packs, cotangent)


def add_rows(acc, first, other, count):
    chunk = min(count, 32)

    def step(index, _):
        there = pl.ds(pl.multiple_of(first + index * chunk, chunk), chunk)
        here = pl.ds(pl.multiple_of(index * chunk, chunk), chunk)
        total = acc[there, :].astype(jnp.float32) + other[here, :].astype(jnp.float32)
        acc[there, :] = total.astype(jnp.bfloat16)
        return 0

    lax.fori_loop(0, count // chunk, step, 0)


class Across:
    def __init__(self, dp, mp, mine, out, refs, sums=None):
        self.dp, self.mp, self.mine, self.out, self.sums = dp, mp, mine, out, sums
        (
            self.lines, self.last, self.line_send, self.line_recv,
            self.last_send, self.last_recv, self.ring_send, self.ring_recv, self.own,
        ) = refs
        self.me, self.part = lax.axis_index("dp"), lax.axis_index("mp")
        self.bits = dp.bit_length() - 1
        self.orders = orders_of(dp)
        if sums is None:
            self.share = out.shape[0] // dp
            self.width = out.shape[1] // 2
        else:
            self.share, self.width = sums.shape[1], sums.shape[2]

    def shard(self, i):
        near, far = flip(self.part, 0), flip(self.part, 1)
        return (flip(far, 0), far, near, self.part)[i]

    def kept(self, half, src=None):
        src = self.mine(self.mp - 1, half) if src is None else src
        dst = self.rows_at(half, self.me, 0) if self.sums is None else self.sums.at[half]
        return pltpu.make_async_copy(src, dst, self.own.at[half])

    def across(self, i, half):
        if i % 2 == 0:
            return remote(
                self.mine(i, half), self.lines.at[self.shard(i), half],
                self.line_send.at[i // 2, half], self.line_recv.at[self.shard(i), half],
                "mp", flip(self.part, 0),
            )
        return remote(
            self.mine(i, half), self.last.at[half],
            self.last_send.at[half], self.last_recv.at[half], "mp", flip(self.part, 1),
        )

    def ring(self, half, stage):
        rows = self.rows_at(half, self.me, stage)
        return remote(
            rows, rows, self.ring_send.at[stage, half], self.ring_recv.at[stage, half],
            "dp", flip(self.me, self.orders[half][stage]),
        )

    def rows_at(self, half, index, stage):
        rank = rank_of(index, self.orders[half])
        first = lax.div(rank, 1 << stage) * (self.share << stage)
        return self.out.at[
            pl.ds(pl.multiple_of(first, self.share), self.share << stage),
            half * self.width : (half + 1) * self.width,
        ]

    def fold(self, i):
        for half in range(2):
            mine = self.mine(i, half)
            if i % 2:
                came = self.lines.at[self.shard(i), half]
                arrived(came, self.line_recv.at[self.shard(i), half])
                add_rows(mine, 0, came, self.share)
            if i < self.mp - 1:
                self.across(i, half).start()
            else:
                came = self.last.at[half]
                arrived(came, self.last_recv.at[half])
                add_rows(mine, 0, came, self.share)
                self.kept(half).start()

    def spread(self, stage):
        for half in range(2):
            if stage == 0:
                arrived(self.rows_at(half, self.me, 0), self.own.at[half])
            else:
                other = flip(self.me, self.orders[half][stage - 1])
                arrived(self.rows_at(half, other, stage - 1), self.ring_recv.at[stage - 1, half])
            if stage < self.bits:
                self.ring(half, stage).start()

    def close(self, summed=True):
        for half in range(2):
            for i in range(self.mp - 1):
                if summed:
                    self.across(i, half).wait_send()
            if self.sums is not None:
                self.kept(half).wait()
                continue
            for stage in range(self.bits):
                self.ring(half, stage).wait_send()


class Reduce:
    def __init__(self, dp, mp, src, share, width, stage, load, recvs, send, recv, first, stop):
        self.dp, self.mp, self.src, self.stage, self.load = dp, mp, src, stage, load
        self.share, self.width, self.first, self.stop = share, width, first, stop
        self.recvs, self.send, self.recv = recvs, send, recv
        self.acc = recvs[0] if first == 0 else stage
        self.base = max(first, 1)
        self.tail = self.sums = self.sums_sem = None
        self.me, self.part = lax.axis_index("dp"), lax.axis_index("mp")
        self.bits = dp.bit_length() - 1
        self.orders = orders_of(dp)

    def shard(self, i):
        near, far = flip(self.part, 0), flip(self.part, 1)
        return (flip(far, 0), far, near, self.part)[i]

    def rank(self, half, index):
        return rank_of(index, self.orders[half])

    def top(self, half, index):
        count = self.share << (self.bits - 1)
        return span_of(lax.div(self.rank(half, index), 1 << (self.bits - 1)), count)

    def offset(self, half, index, stage):
        low = lax.rem(self.rank(half, index), 1 << (self.bits - self.base))
        left = self.bits - 1 - stage
        return pl.multiple_of(lax.div(low, 1 << left) * (self.share << left), self.share)

    def columns(self, half):
        return slice(half * self.width, (half + 1) * self.width)

    def rows(self, i, half, index, stage):
        first = self.offset(half, index, stage)
        count = self.share << (self.bits - 1 - stage)
        return self.acc.at[self.shard(i), half].at[pl.ds(first, count), :]

    def give(self, i, half, stage):
        m = self.shard(i)
        place = stage - self.first
        other = flip(self.me, self.orders[half][self.bits - 1 - stage])
        if stage == 0:
            rows = self.src.at[m, self.top(half, other), self.columns(half)]
        else:
            rows = self.rows(i, half, other, stage)
        return remote(
            rows, self.recvs[place].at[m, half],
            self.send.at[place, i, half], self.recv.at[place, m, half], "dp", other,
        )

    def mine(self, i, half):
        return self.rows(i, half, self.me, self.bits - 1)

    def saved(self, i, half):
        return pltpu.make_async_copy(
            self.rows(i, half, self.me, self.stop - 1),
            self.sums.at[self.shard(i), half],
            self.sums_sem.at[i, half],
        )

    def begin(self, i):
        for half in range(2):
            self.give(i, half, self.first).start()
            if self.first == 0:
                pltpu.make_async_copy(
                    self.src.at[self.shard(i), self.top(half, self.me), self.columns(half)],
                    self.stage.at[i, half], self.load.at[i, half],
                ).start()

    def fold(self, i, stage):
        m = self.shard(i)
        place = stage - self.first
        count = self.share << (self.bits - 1 - stage)
        for half in range(2):
            acc = self.acc.at[m, half]
            came = self.recvs[place].at[m, half]
            arrived(came, self.recv.at[place, m, half])
            if stage == 0:
                own = self.stage.at[i, half]
                arrived(own, self.load.at[i, half])
                add_rows(acc, 0, own, count)
            else:
                add_rows(acc, self.offset(half, self.me, stage), came, count)
            if stage < self.stop - 1:
                self.give(i, half, stage + 1).start()
            elif self.sums is not None:
                self.saved(i, half).start()
        if stage == self.bits - 1:
            self.tail.fold(i)

    def waves(self):
        return self.mp + LAG * (self.stop - 1) + 1

    def wave(self, number):
        for stage in range(self.stop):
            i = number - 1 - LAG * stage
            if 0 <= i < self.mp:
                self.fold(i, stage)
        if number == 0:
            for i in range(self.mp):
                self.begin(i)

    def close(self):
        for half in range(2):
            for i in range(self.mp):
                for stage in range(self.first, self.stop):
                    self.give(i, half, stage).wait_send()
                if self.sums is not None:
                    self.saved(i, half).wait()
        if self.tail is not None:
            self.tail.close()


def across_scratch(dp, mp, total, width):
    low = jnp.bfloat16
    dma = pltpu.SemaphoreType.DMA
    bits = dp.bit_length() - 1
    return [
        pltpu.VMEM((mp, 2, total // dp, width // 2), low), pltpu.VMEM((2, total // dp, width // 2), low),
        dma((2, 2)), dma((mp, 2)), dma((2,)), dma((2,)), dma((bits, 2)), dma((bits, 2)), dma((2,)),
    ]


def reduce_scratch(dp, mp, total, width, first, stop):
    low = jnp.bfloat16
    dma = pltpu.SemaphoreType.DMA
    half = width // 2
    held = total // 2 if first == 0 else total >> first
    stages = [pltpu.VMEM((mp, 2, held, half), low), dma((mp, 2))]
    stages += [pltpu.VMEM((mp, 2, total >> (i + 1), half), low) for i in range(first, stop)]
    return stages + [dma((stop - first, mp, 2)), dma((stop - first, mp, 2))]


def reduce_plan(dp, mp, src, total, width, refs, first, stop):
    count = stop - first
    plan = Reduce(
        dp, mp, src, total // dp, width // 2, refs[0], refs[1], refs[2 : 2 + count],
        refs[2 + count], refs[3 + count], first, stop,
    )
    return plan, refs[4 + count :]


class Tiny:
    def __init__(self, dp, mp, piece, line, ring, came, sems, waits):
        self.dp, self.mp, self.piece, self.waits = dp, mp, piece, waits
        self.line, self.ring, self.came = line, ring, came
        self.send, self.recv, self.ring_send, self.ring_recv = sems
        self.me, self.part = lax.axis_index("dp"), lax.axis_index("mp")
        self.bits = dp.bit_length() - 1

    def push(self, copy):
        copy.start()
        self.waits.append(copy.wait_send)

    def start(self):
        for step in range(1, self.mp):
            to = lax.rem(self.part + step, self.mp)
            self.push(
                remote(
                    self.piece(to), self.line.at[self.part],
                    self.send.at[step], self.recv.at[self.part], "mp", to,
                )
            )

    def fold(self, stage):
        if stage == 0:
            total = self.piece(self.part)[...].astype(jnp.float32)
            for step in range(1, self.mp):
                source = lax.rem(self.part + step, self.mp)
                arrived(self.line.at[source], self.recv.at[source])
                total = total + self.line[source].astype(jnp.float32)
        else:
            arrived(self.came.at[stage - 1], self.ring_recv.at[stage - 1])
            total = self.ring[stage - 1] + self.came[stage - 1]
        self.ring[stage] = total
        if stage < self.bits:
            self.push(
                remote(
                    self.ring.at[stage], self.came.at[stage],
                    self.ring_send.at[stage], self.ring_recv.at[stage],
                    "dp", flip(self.me, stage),
                )
            )


def tiny_sems(dp, mp):
    dma = pltpu.SemaphoreType.DMA
    bits = dp.bit_length() - 1
    return [dma((mp,)), dma((mp,)), dma((bits,)), dma((bits,))]


FEATURES = 40


def closing_kernel(
    dp, mp, span,
    one_ref, two_ref, grad_ref, xn_ref, x_ref, normed_ref, direct_ref, shared_ref, vector_ref,
    keep_ref, weight_ref, gain_ref, omega_ref, ffn_ref, starts_ref,
    one_out, two_out, token_out, feat_out, shared_out, vector_out,
    *refs,
):
    bits = dp.bit_length() - 1
    me, part = lax.axis_index("dp"), lax.axis_index("mp")
    waits = []
    taken = 0
    _, total, width = one_ref.shape
    pack, refs = reduce_plan(dp, mp, one_ref, total, width, refs, 0, bits)
    pack.tail = Across(dp, mp, pack.mine, one_out, refs[:9])
    other, refs = reduce_plan(dp, mp, None, total, width, refs[9:], SPLIT, bits)
    other.tail = Across(dp, mp, other.mine, two_out, refs[:9])
    refs = refs[9:]

    def take(count):
        nonlocal taken
        taken += count
        return refs[taken - count : taken]

    grad, xn, x, normed_part, direct, tokens, rows, outs, states, ahead, sums, feat = take(12)
    shared, shared_line, shared_ring, shared_came, shared_low = take(5)
    feat_line, feat_ring, feat_came = take(3)
    vector, vector_line, vector_ring, vector_came = take(4)
    (in_sem,) = take(1)
    carry_send, carry_recv = take(2)
    spread_send, spread_recv, spread_own = take(3)
    token = Swap(mp, tokens, token_out, take(4), back=True)
    quarter = shared.shape[0] // mp
    columns = feat.shape[1] // mp
    tiny_shared = Tiny(
        dp, mp, lambda m: shared.at[span_of(m, quarter), :],
        shared_line, shared_ring, shared_came, take(4), waits,
    )
    tiny_vector = Tiny(
        dp, mp, lambda m: vector, vector_line, vector_ring, vector_came, take(4), waits
    )
    tiny_feat = Tiny(
        dp, mp, lambda m: feat.at[:, span_of(m, columns)],
        feat_line, feat_ring, feat_came, take(4), waits,
    )
    loads = [
        pltpu.make_async_copy(src, dst, in_sem.at[i])
        for i, (src, dst) in enumerate(
            (
                (grad_ref, grad), (xn_ref, xn), (x_ref, x), (normed_ref, normed_part),
                (direct_ref, direct), (shared_ref, shared), (vector_ref, vector),
            )
        )
    ]
    count = grad.shape[0]
    blocks = count // TB
    keep = lambda dims: [keep_ref[j] for j in dims]
    every = range(NDIM)
    gives = lax.rem(part, span) != 0
    takes = lax.rem(part + 1, span) != 0

    def carry():
        return remote(outs.at[0 : NDIM * SUB, :], ahead, carry_send.at[0], carry_recv.at[0], "mp", part - 1)

    def slot_of(j):
        return slice(j * SUB, (j + 1) * SUB)

    def adjoint():
        loads[0].wait()
        kept = keep(every)

        def block_step(number, state):
            first = pl.multiple_of((blocks - 1 - number) * TB, TB)
            to_rows(rows, grad[pl.ds(first, TB), :])

            def step(t, state):
                now = row(rows, TB - 1 - t)
                return tuple(kept[j] * state[j] + now for j in every)

            return lax.fori_loop(0, TB, step, state, unroll=4)

        zero = jnp.zeros((SUB, LANES), jnp.float32)
        state = lax.fori_loop(0, blocks, block_step, tuple(zero for _ in every))
        for j in every:
            outs[slot_of(j), :] = state[j]

        @pl.when(gives)
        def _():
            carry().start()

        for j in range(2 * NDIM):
            states[j] = starts_ref[j]
        sums[...] = jnp.zeros_like(sums)
        feat[...] = jnp.zeros_like(feat)
        feat[34:35, :] = ffn_ref[...]
        loads[1].wait()

    def params(low, high):
        half = NDIM // 2

        def block_step(number, _):
            first = pl.multiple_of(number * TB, TB)
            now_xn = xn[pl.ds(first, TB), :].astype(jnp.float32)
            now_grad = grad[pl.ds(first, TB), :]
            to_rows(rows, now_xn)
            for piece in range(SUB):
                turned[pl.ds(piece, TB, stride=SUB), :] = now_grad[:, piece * LANES : (piece + 1) * LANES]
            feat[32:33, :] += jnp.sum(now_grad * now_xn, axis=0, keepdims=True)
            for start in (0, half):
                dims = range(start, start + half)
                kept = keep(dims)

                def step(t, carried):
                    state, slope, weight_sum, keep_sum = carried
                    now = row(rows, t)
                    grad_now = row(turned, t)
                    slope = tuple(kept[j] * slope[j] + state[j] for j in range(half))
                    state = tuple(kept[j] * state[j] + now for j in range(half))
                    weight_sum = tuple(weight_sum[j] + grad_now * state[j] for j in range(half))
                    keep_sum = tuple(keep_sum[j] + grad_now * slope[j] for j in range(half))
                    return (state, slope, weight_sum, keep_sum)

                carried = (
                    tuple(states[j] for j in dims),
                    tuple(states[NDIM + j] for j in dims),
                    tuple(sums[slot_of(j), :] for j in dims),
                    tuple(sums[slot_of(NDIM + j), :] for j in dims),
                )
                state, slope, weight_sum, keep_sum = lax.fori_loop(0, TB, step, carried, unroll=4)
                for place, j in enumerate(dims):
                    states[j] = state[place]
                    states[NDIM + j] = slope[place]
                    sums[slot_of(j), :] = weight_sum[place]
                    sums[slot_of(NDIM + j), :] = keep_sum[place]
            return 0

        lax.fori_loop(low, high, block_step, 0)

    def meet():
        @pl.when(gives)
        def _():
            carry().wait_send()

        @pl.when(jnp.logical_not(takes))
        def _():
            ahead[...] = jnp.zeros_like(ahead)

        @pl.when(takes)
        def _():
            arrived(ahead, carry_recv.at[0])

        for copy in loads[2:5]:
            copy.wait()

    def token_rows(low, high):
        kept = keep(every)

        def block_step(number, state):
            there = pl.ds(pl.multiple_of((blocks - 1 - number) * TB, TB), TB)
            now_grad = grad[there, :]
            to_rows(rows, now_grad)

            def step(t, state):
                place = TB - 1 - t
                now = row(rows, place)
                state = tuple(kept[j] * state[j] + now for j in every)
                terms = [weight_ref[j] * state[j] for j in every]
                while len(terms) > 1:
                    terms = [a + b for a, b in zip(terms[::2], terms[1::2])]
                outs[pl.ds(pl.multiple_of(place * SUB, SUB), SUB), :] = terms[0]
                return state

            state = lax.fori_loop(0, TB, step, state, unroll=4)
            d_xn = from_rows(outs) + now_grad * omega_ref[...]
            d_xn = d_xn + normed_part[there, :].astype(jnp.float32)
            now_x = x[there, :].astype(jnp.float32)
            mean = jnp.mean(now_x, axis=1, keepdims=True)
            power = jnp.mean(now_x * now_x, axis=1, keepdims=True)
            scale = lax.rsqrt(power - mean * mean + EPS)
            normed = (now_x - mean) * scale
            feat[33:34, :] += jnp.sum(d_xn * normed, axis=0, keepdims=True)
            scaled = d_xn * gain_ref[...]
            first = jnp.mean(scaled, axis=1, keepdims=True)
            second = jnp.mean(scaled * normed, axis=1, keepdims=True)
            back = scale * (scaled - first - normed * second)
            tokens[there, :] = (direct[there, :].astype(jnp.float32) + back).astype(jnp.bfloat16)
            return state

        state = tuple(ahead[slot_of(j), :] for j in every)
        state = lax.fori_loop(low, high, block_step, state)
        for j in every:
            ahead[slot_of(j), :] = state[j]

    def gathered():
        for piece in range(SUB):
            feat[0 : 2 * NDIM, piece * LANES : (piece + 1) * LANES] = sums[
                pl.ds(piece, 2 * NDIM, stride=SUB), :
            ]
        token.start()
        tiny_feat.start()

    def shared_back():
        low = shared_ring[bits].astype(jnp.bfloat16)
        shared_low[...] = low
        there = shared_out.at[span_of(part, quarter), :]
        pltpu.make_async_copy(shared_low, there, spread_own.at[0]).start()
        for step in range(1, mp):
            to = lax.rem(part + step, mp)
            copy = remote(shared_low, there, spread_send.at[step], spread_recv.at[part], "mp", to)
            copy.start()
            waits.append(copy.wait_send)

    (turned,) = take(1)

    greet(dp, mp)
    for copy in loads:
        copy.start()
    def parts():
        return pltpu.make_async_copy(two_ref, other.stage, other.load.at[0, 0])

    def sums_ready():
        parts().wait()
        for i in range(mp):
            other.begin(i)

    def tiny_ready():
        loads[5].wait()
        loads[6].wait()
        tiny_shared.start()
        tiny_vector.start()

    def vector_ready():
        shared_back()
        vector_out[...] = vector_ring[bits]

    def feat_ready():
        feat_out[...] = feat_ring[bits]

    parts().start()
    for i in range(mp):
        pack.begin(i)
    pace = max(blocks // 4, 1)
    late = [
        lambda i=i, stage=stage: other.fold(i, stage)
        for stage in range(SPLIT, bits)
        for i in range(mp)
    ]
    work = [sums_ready, adjoint, lambda: pack.fold(0, 0), lambda: params(0, pace)]
    work += [lambda: pack.fold(1, 0), late[0], tiny_ready, lambda: params(pace, 2 * pace)]
    work += [lambda: pack.fold(2, 0), lambda: pack.fold(3, 0), late[1], lambda: params(2 * pace, 3 * pace)]
    work += [late[2], lambda: pack.fold(0, 1), lambda: params(3 * pace, blocks)]
    work += [meet, lambda: pack.fold(1, 1), lambda: token_rows(0, blocks // 2)]
    work += [lambda: pack.fold(2, 1), lambda: token_rows(blocks // 2, blocks), gathered]
    work += [lambda: pack.fold(3, 1)] + late[3:] + [lambda: other.tail.spread(0)]
    for stage in range(2, bits):
        for i in range(mp):
            work.append(lambda i=i, stage=stage: pack.fold(i, stage))
            if stage == 2 and i < 3:
                work.append(lambda i=i: other.tail.spread(1 + i))
            if stage == 2 and i <= bits:
                work.append(lambda i=i: tiny_shared.fold(i))
                work.append(lambda i=i: tiny_vector.fold(i))
    for i in range(mp, bits + 1):
        work.append(lambda i=i: other.tail.spread(i))
        work.append(lambda i=i: tiny_shared.fold(i))
        work.append(lambda i=i: tiny_vector.fold(i))
    work.append(vector_ready)
    for step in range(bits + 1):
        work.append(lambda step=step: pack.tail.spread(step))
        work.append(lambda step=step: tiny_feat.fold(step))
    work.append(feat_ready)
    for item in work:
        item()
    arrived(shared_low, spread_own.at[0])
    for step in range(1, mp):
        source = lax.rem(part + step, mp)
        arrived(shared_out.at[span_of(source, quarter), :], spread_recv.at[source])
    token.turn()
    token.receive()
    token.close()
    pack.close()
    other.close()
    for wait in waits:
        wait()


def closing(dp, mp, span, one, two, inputs, shared, vector, params, starts):
    low, full = jnp.bfloat16, jnp.float32
    bits = dp.bit_length() - 1
    dma = pltpu.SemaphoreType.DMA
    count = inputs[0].shape[0]
    _, total, width = one.shape
    z = shared.shape[1]
    quarter, columns = D // mp, D // mp

    def vmem(*shape, dtype=full):
        return pltpu.VMEM(shape, dtype)

    scratch = reduce_scratch(dp, mp, total, width, 0, bits) + across_scratch(dp, mp, total, width)
    scratch += reduce_scratch(dp, mp, total, width, SPLIT, bits) + across_scratch(dp, mp, total, width)
    scratch += [vmem(count, D)] + [vmem(count, D, dtype=low)] * 5
    scratch += [ROWS, ROWS, pltpu.VMEM(STATES, full), vmem(NDIM * SUB, LANES)]
    scratch += [vmem(2 * NDIM * SUB, LANES), vmem(FEATURES, D)]
    scratch += [
        vmem(D, z, dtype=low), vmem(mp, quarter, z, dtype=low), vmem(bits + 1, quarter, z),
        vmem(bits, quarter, z), vmem(quarter, z, dtype=low),
    ]
    scratch += [vmem(mp, FEATURES, columns), vmem(bits + 1, FEATURES, columns), vmem(bits, FEATURES, columns)]
    scratch += [vmem(8, z), vmem(mp, 8, z), vmem(bits + 1, 8, z), vmem(bits, 8, z)]
    scratch += [dma((7,)), dma((1,)), dma((1,)), dma((mp,)), dma((mp,)), dma((1,))]
    scratch += swap_scratch(mp, count, D // mp) + tiny_sems(dp, mp) * 3
    scratch += [ROWS]
    near = pl.BlockSpec(memory_space=pltpu.VMEM)
    return pl.pallas_call(
        functools.partial(closing_kernel, dp, mp, span),
        in_specs=[HBM] * 9 + [near] * 6,
        out_specs=[HBM] * 3 + [near, HBM, near],
        out_shape=[
            sds((total, width), low), sds((total, width), low), sds((count * mp, D // mp), low),
            sds((FEATURES, columns)), sds((D, z), low), sds((8, z)),
        ],
        scratch_shapes=scratch,
        compiler_params=pltpu.CompilerParams(
            collective_id=2, has_side_effects=True, vmem_limit_bytes=61 << 20
        ),
        name="closing",
    )(one, two, *inputs, shared, vector, *params, starts)


def local(
    dp,
    mp,
    tokens,
    cotangent,
    norm_gain,
    ema_delta,
    ema_alpha,
    ema_beta,
    ema_eta,
    ema_omega,
    shared_proj,
    query_gain,
    query_bias,
    key_gain,
    value_proj,
    gate_proj,
    mixer_proj,
    update_proj,
    output_proj,
    ffn_gain,
    up_proj,
    down_proj,
):
    width = tokens.shape[1]
    count = tokens.shape[0] // mp
    span = LEN // count
    small = jnp.concatenate(
        [
            ema_delta, ema_alpha, ema_beta, ema_eta,
            norm_gain[:, None], ema_omega[:, None], ffn_gain[:, None],
        ],
        axis=1,
    ).T
    lines = small.shape[0]
    small = jnp.pad(small, ((0, -lines % 8), (0, 0)))
    firsts = (value_proj, gate_proj, mixer_proj, update_proj, output_proj)
    vectors = (query_gain[None], query_bias[None], key_gain[None])
    wide, narrow = value_proj.shape[1], mixer_proj.shape[1]
    (
        xn, xp, mix_pre, starts, keep, weight, gains,
        vpre, gpre, att, hidden, act_pre, upd_pre, middle, spre, one, x_low, two, grad_out,
    ) = forward(
        dp, mp, span, mp * wide, jnp.tile(small, (1, mp)), firsts, tokens, shared_proj, vectors,
        (up_proj, down_proj), cotangent,
    )
    keep, weight = keep.reshape(STATE), weight.reshape(STATE)
    gain, omega, gain_two = gains[0:1], gains[1:2], gains[2:3]
    layer_rows, ffn_in, upper, d_up, d_act, d_upd, d_inputs, ffn_part = ffn(
        middle, grad_out, x_low, act_pre, upd_pre, two, gain_two
    )
    two_grad = ffn_weights(mp, ffn_in, grad_out, upper, d_up)
    (
        d_value, d_gate, d_shared, d_mix_pre, normed_part, vector_sums, two_sums, layer_out,
    ) = mixer_backward(
        dp, mp, d_act, d_upd, vpre, gpre, att, spre, mix_pre, one, shared_proj, *vectors,
        two_grad, layer_rows,
    )
    one_grad, shared_part = mixer_weights(
        mp, xn, xp, hidden, d_act, d_value, d_gate, d_upd, d_shared
    )

    one_grad, two_grad, token_grad, feature, shared_grad, vector_sums = closing(
        dp, mp, span, one_grad, two_sums,
        (d_mix_pre, xn, x_low, normed_part, d_inputs), shared_part, vector_sums,
        (keep, weight, gain, omega, ffn_part), starts,
    )
    up_grad = two_grad[:, : up_proj.shape[1]].astype(jnp.float32)
    down_grad = two_grad[:, up_proj.shape[1] :].astype(jnp.float32)
    base = 2 * (wide + narrow)
    value_grad = one_grad[:, :wide].astype(jnp.float32)
    gate_grad = one_grad[:, wide : 2 * wide].astype(jnp.float32)
    mixer_grad = one_grad[:, 2 * wide : 2 * wide + narrow].astype(jnp.float32)
    update_grad = one_grad[:, 2 * wide + narrow : base].astype(jnp.float32)
    output_grad = jnp.concatenate(
        [one_grad[:wide, base:], one_grad[wide:, base:]], axis=1
    ).astype(jnp.float32)

    shared_grad = shared_grad.astype(jnp.float32)
    query_grad, bias_grad, key_grad = vector_sums[0], vector_sums[1], vector_sums[2]
    delta, alpha, beta, eta = (
        item.T for item in (ema_delta, ema_alpha, ema_beta, ema_eta)
    )
    rate = jax.nn.sigmoid(delta)
    damp = jax.nn.sigmoid(alpha)
    weight_sum = feature[:NDIM]
    keep_sum = feature[NDIM : 2 * NDIM] * (rate * beta * eta)
    d_rate = weight_sum * beta * eta - keep_sum * damp
    delta_grad = (d_rate * rate * (1.0 - rate)).T
    alpha_grad = (-keep_sum * rate * damp * (1.0 - damp)).T
    beta_grad = (weight_sum * rate * eta).T
    eta_grad = (weight_sum * rate * beta).T
    omega_grad, gain_grad, ffn_grad = feature[2 * NDIM], feature[2 * NDIM + 1], feature[2 * NDIM + 2]
    return (
        layer_out, token_grad, gain_grad, delta_grad, alpha_grad, beta_grad, eta_grad, omega_grad,
        shared_grad, query_grad, bias_grad, key_grad, value_grad, gate_grad, mixer_grad,
        update_grad, output_grad, ffn_grad, up_grad, down_grad,
    )


def solution(mesh):
    dp, mp = mesh.shape["dp"], mesh.shape["mp"]
    params = (
        P("mp"), P("mp", None), P("mp", None), P("mp", None), P("mp", None), P("mp"),
        P(), P(), P(), P(),
        P(None, "mp"), P(None, "mp"), P(None, "mp"), P(None, "mp"), P("mp", None),
        P("mp"), P(None, "mp"), P("mp", None),
    )
    specs = (P("dp", "mp"), P("dp", "mp")) + params
    return jax.shard_map(
        functools.partial(local, dp, mp), mesh=mesh, in_specs=specs, out_specs=specs, check_vma=False
    )
```

```python
import functools

import jax
import jax.numpy as jnp
from jax import lax
from jax.experimental import pallas as pl
from jax.experimental.pallas import tpu as pltpu
from jax.sharding import PartitionSpec as P

D = 1024
GROUP = 128
LEN = 2048
NDIM = 16
LANES = 128
SUB = D // LANES
EPS = 1e-05
TB = 128


def matmul(left, right):
    return jnp.dot(left, right, preferred_element_type=jnp.float32)


def matmul_tn(left, right):
    return lax.dot_general(
        left, right, (((0,), (0,)), ((), ())), preferred_element_type=jnp.float32
    )


def matmul_nt(left, right):
    return lax.dot_general(
        left, right, (((1,), (1,)), ((), ())), preferred_element_type=jnp.float32
    )


def to_rows(scratch, value):
    for part in range(SUB):
        scratch[pl.ds(part, TB, stride=SUB), :] = value[:, part * LANES : (part + 1) * LANES]


def from_rows(scratch):
    return jnp.concatenate(
        [scratch[pl.ds(part, TB, stride=SUB), :] for part in range(SUB)], axis=1
    )


def row(scratch, index):
    return scratch[pl.ds(pl.multiple_of(index * SUB, SUB), SUB), :]


def sds(shape, dtype=jnp.float32):
    return jax.ShapeDtypeStruct(shape, dtype)


def block(reverse=None):
    if reverse is None:
        return pl.BlockSpec((TB, D), lambda i: (i, 0))
    return pl.BlockSpec((TB, D), lambda i: (reverse - 1 - i, 0))


def whole(*shape):
    return pl.BlockSpec(shape, lambda i: (0,) * len(shape))


STATE = (NDIM, SUB, LANES)
STATES = (2 * NDIM, SUB, LANES)
ROWS = pltpu.VMEM((TB * SUB, LANES), jnp.float32)
PARAMS = pltpu.CompilerParams(vmem_limit_bytes=32 << 20)


ROWS_C = 256
ROWS_E = 128
LEAD = 8
LAG = 1
SPLIT = 2


def sigmoid(value):
    return 0.5 + 0.5 * jnp.tanh(0.5 * value)


def causal_probs(query, keys, head_scale):
    scores = matmul_nt(query, keys) * head_scale
    down = lax.broadcasted_iota(jnp.int32, scores.shape, 0)
    across = lax.broadcasted_iota(jnp.int32, scores.shape, 1)
    scores = jnp.where(down >= across, scores, -1e30)
    weights = jnp.exp(scores - jnp.max(scores, axis=1, keepdims=True))
    return weights / jnp.sum(weights, axis=1, keepdims=True)


def mixer_forward_kernel(
    xn_ref, xp_ref, x_ref, one_ref, shared_ref, qgain_ref, qbias_ref, kgain_ref,
    vpre_ref, gpre_ref, att_ref, hid_ref, act_ref, upd_ref, mid_ref, spre_ref,
):
    mp = one_ref.shape[0]
    narrow = D // mp
    wide = vpre_ref.shape[1] // mp
    base = 2 * (wide + narrow)
    groups = ROWS_C // GROUP
    xn, xp = xn_ref[...], xp_ref[...]
    shared_pre = matmul(xp, shared_ref[...])
    spre_ref[...] = shared_pre
    shared = shared_pre * sigmoid(shared_pre)
    query = (shared * qgain_ref[...] + qbias_ref[...]).astype(jnp.bfloat16)
    keys = (shared * kgain_ref[...]).astype(jnp.bfloat16)
    head_scale = shared.shape[1] ** (-0.5)
    probs = [
        causal_probs(
            query[g * GROUP : (g + 1) * GROUP], keys[g * GROUP : (g + 1) * GROUP], head_scale
        ).astype(jnp.bfloat16)
        for g in range(groups)
    ]
    attn_out = None
    for m in range(mp):
        span = slice(m * wide, (m + 1) * wide)
        value_pre = matmul(xn, one_ref[m, :, 0:wide])
        values = (value_pre * sigmoid(value_pre)).astype(jnp.bfloat16)
        vpre_ref[:, span] = value_pre.astype(jnp.bfloat16)
        gate_pre = matmul(xp, one_ref[m, :, wide : 2 * wide])
        gate = gate_pre * sigmoid(gate_pre)
        gpre_ref[:, span] = gate_pre.astype(jnp.bfloat16)
        attended = jnp.concatenate(
            [matmul(probs[g], values[g * GROUP : (g + 1) * GROUP]) for g in range(groups)], axis=0
        )
        att_ref[:, span] = attended.astype(jnp.bfloat16)
        hidden = (gate * attended).astype(jnp.bfloat16)
        hid_ref[:, span] = hidden
        term = jnp.concatenate(
            [matmul(hidden, one_ref[m, 0:wide, base:]), matmul(hidden, one_ref[m, wide:, base:])], axis=1
        )
        attn_out = term if attn_out is None else attn_out + term
    for m in range(mp):
        span = slice(m * narrow, (m + 1) * narrow)
        act = matmul(xp, one_ref[m, :, 2 * wide : 2 * wide + narrow]) + attn_out[:, span]
        upd = matmul(xp, one_ref[m, :, 2 * wide + narrow : base])
        update = sigmoid(upd)
        act_ref[:, span] = act.astype(jnp.bfloat16)
        upd_ref[:, span] = upd.astype(jnp.bfloat16)
        x = x_ref[:, span].astype(jnp.float32)
        mid_ref[:, span] = x + update * (act * sigmoid(act) - x)


def ffn_kernel(
    mid_ref, grad_ref, x_ref, act_ref, upd_ref, two_ref, gain_ref,
    layer_ref, ffn_ref, upper_ref, dup_ref, dact_ref, dupd_ref, dx_ref, gsum_ref,
):
    mp, _, total = two_ref.shape
    units = total - D
    sub = 512
    middle = mid_ref[...]
    grad = grad_ref[...]
    mean = jnp.mean(middle, axis=1, keepdims=True)
    power = jnp.mean(middle * middle, axis=1, keepdims=True)
    scale = lax.rsqrt(power - mean * mean + EPS)
    normed = (middle - mean) * scale
    gain = gain_ref[...]
    ffn_in = (normed * gain).astype(jnp.bfloat16)
    ffn_ref[...] = ffn_in
    down_out = None
    d_ffn = None
    for m in range(mp):
        for first in range(0, units, sub):
            columns = slice(m * units + first, m * units + first + sub)
            up_weights = two_ref[m, :, first : first + sub]
            down_weights = two_ref[m, first : first + sub, units:]
            up_pre = matmul(ffn_in, up_weights)
            logistic = sigmoid(up_pre)
            value = up_pre * logistic
            upper = value.astype(jnp.bfloat16)
            upper_ref[:, columns] = upper
            slope = logistic + value - value * logistic
            d_up = (matmul_nt(grad, down_weights) * slope).astype(jnp.bfloat16)
            dup_ref[:, columns] = d_up
            term = matmul(upper, down_weights)
            down_out = term if down_out is None else down_out + term
            term = matmul_nt(d_up, up_weights)
            d_ffn = term if d_ffn is None else d_ffn + term
    layer_ref[...] = (middle + down_out).astype(jnp.bfloat16)

    @pl.when(pl.program_id(0) == 0)
    def _():
        gsum_ref[...] = jnp.zeros_like(gsum_ref)

    gsum_ref[...] += jnp.sum(d_ffn * normed, axis=0, keepdims=True)
    scaled = d_ffn * gain
    first = jnp.mean(scaled, axis=1, keepdims=True)
    second = jnp.mean(scaled * normed, axis=1, keepdims=True)
    d_middle = grad.astype(jnp.float32) + scale * (scaled - first - normed * second)
    act = act_ref[...].astype(jnp.float32)
    update = sigmoid(upd_ref[...].astype(jnp.float32))
    logistic = sigmoid(act)
    value = act * logistic
    x = x_ref[...].astype(jnp.float32)
    d_update = d_middle * update
    dact_ref[...] = (d_update * (logistic + value - value * logistic)).astype(jnp.bfloat16)
    dupd_ref[...] = (d_update * (value - x) * (1.0 - update)).astype(jnp.bfloat16)
    dx_ref[...] = (d_middle - d_update).astype(jnp.bfloat16)


def backward_kernel(dp, mp, pack_ref, layer_ref, *refs):
    ins, outs, refs = refs[:12], refs[12:18], refs[18:]
    sums_out, layer_out = refs[:2]
    layer = Swap(mp, layer_ref, layer_out, refs[2:6], back=True)
    _, total, width = pack_ref.shape
    plan, refs = reduce_plan(dp, mp, pack_ref, total, width, refs[6:], 0, SPLIT)
    plan.sums, plan.sums_sem = sums_out, refs[0]
    index = pl.program_id(0)
    steps = pl.num_programs(0)

    @pl.when(index == 0)
    def _():
        greet(dp, mp)
        plan.wave(0)
        layer.start()

    for number in range(1, LEAD):

        @pl.when(index == number)
        def _(number=number):
            plan.wave(number)
            if number == 1:
                layer.turn()

    mixer_backward_kernel(*ins, *outs)

    @pl.when(index == steps - 1)
    def _():
        for number in range(LEAD, plan.waves()):
            plan.wave(number)
        layer.receive()
        layer.close()
        plan.close()


def mixer_backward_kernel(
    dact_ref, dupd_ref, vpre_ref, gpre_ref, att_ref, spre_ref, mix_ref, one_ref, shared_ref,
    qgain_ref, qbias_ref, kgain_ref,
    dv_ref, dg_ref, dshared_ref, dmix_ref, dxn_ref, sums_ref,
):
    mp = one_ref.shape[0]
    narrow = D // mp
    wide = vpre_ref.shape[1] // mp
    base = 2 * (wide + narrow)
    groups = dact_ref.shape[0] // GROUP
    shared_pre = spre_ref[...]
    logistic = sigmoid(shared_pre)
    shared = shared_pre * logistic
    query = (shared * qgain_ref[...] + qbias_ref[...]).astype(jnp.bfloat16)
    keys = (shared * kgain_ref[...]).astype(jnp.bfloat16)
    head_scale = shared.shape[1] ** (-0.5)
    rows = [slice(g * GROUP, (g + 1) * GROUP) for g in range(groups)]
    probs = [causal_probs(query[rows[g]], keys[rows[g]], head_scale) for g in range(groups)]
    probs_low = [item.astype(jnp.bfloat16) for item in probs]
    d_act = dact_ref[...]
    d_probs = [None] * groups
    d_xp = None
    d_xn = None
    for m in range(mp):
        span = slice(m * wide, (m + 1) * wide)
        thin = slice(m * narrow, (m + 1) * narrow)
        d_hidden = matmul_nt(d_act[:, : D // 2], one_ref[m, 0:wide, base:]) + matmul_nt(
            d_act[:, D // 2 :], one_ref[m, wide:, base:]
        )
        gate_pre = gpre_ref[:, span].astype(jnp.float32)
        gate_log = sigmoid(gate_pre)
        gate = gate_pre * gate_log
        attended = att_ref[:, span].astype(jnp.float32)
        d_gate = (d_hidden * attended * (gate_log + gate - gate * gate_log)).astype(jnp.bfloat16)
        dg_ref[:, span] = d_gate
        d_att = (d_hidden * gate).astype(jnp.bfloat16)
        value_pre = vpre_ref[:, span].astype(jnp.float32)
        value_log = sigmoid(value_pre)
        value = value_pre * value_log
        values = value.astype(jnp.bfloat16)
        parts = []
        for g in range(groups):
            term = matmul_nt(d_att[rows[g]], values[rows[g]])
            d_probs[g] = term if d_probs[g] is None else d_probs[g] + term
            parts.append(matmul_tn(probs_low[g], d_att[rows[g]]))
        d_value = jnp.concatenate(parts, axis=0)
        d_value_pre = (d_value * (value_log + value - value * value_log)).astype(jnp.bfloat16)
        dv_ref[:, span] = d_value_pre
        term = (
            matmul_nt(d_gate, one_ref[m, :, wide : 2 * wide])
            + matmul_nt(d_act[:, thin], one_ref[m, :, 2 * wide : 2 * wide + narrow])
            + matmul_nt(dupd_ref[:, thin], one_ref[m, :, 2 * wide + narrow : base])
        )
        d_xp = term if d_xp is None else d_xp + term
        term = matmul_nt(d_value_pre, one_ref[m, :, 0:wide])
        d_xn = term if d_xn is None else d_xn + term
    dxn_ref[...] = d_xn.astype(jnp.bfloat16)
    d_query, d_keys = [], []
    for g in range(groups):
        d_scores = probs[g] * (d_probs[g] - jnp.sum(probs[g] * d_probs[g], axis=1, keepdims=True))
        low = d_scores.astype(jnp.bfloat16)
        d_query.append(matmul(low, keys[rows[g]]) * head_scale)
        d_keys.append(matmul_tn(low, query[rows[g]]) * head_scale)
    d_query = jnp.concatenate(d_query, axis=0)
    d_keys = jnp.concatenate(d_keys, axis=0)

    @pl.when(pl.program_id(0) == 0)
    def _():
        sums_ref[...] = jnp.zeros_like(sums_ref)

    sums_ref[0:1, :] += jnp.sum(d_query * shared, axis=0, keepdims=True)
    sums_ref[1:2, :] += jnp.sum(d_query, axis=0, keepdims=True)
    sums_ref[2:3, :] += jnp.sum(d_keys * shared, axis=0, keepdims=True)
    d_shared = (d_query * qgain_ref[...] + d_keys * kgain_ref[...]) * (
        logistic + shared - shared * logistic
    )
    d_shared = d_shared.astype(jnp.bfloat16)
    dshared_ref[...] = d_shared
    d_xp = d_xp + matmul_nt(d_shared, shared_ref[...])
    mix = mix_ref[...]
    mix_log = sigmoid(mix)
    mix_value = mix * mix_log
    dmix_ref[...] = d_xp * (mix_log + mix_value - mix_value * mix_log)


def mixer_weights_kernel(
    xn_ref, xp_ref, hid_ref, dact_all_ref, dv_ref, dg_ref, dact_ref, dupd_ref, dshared_ref,
    one_ref, shared_ref, xnt, xpt,
):
    wide, narrow = dv_ref.shape[1], dact_ref.shape[1]

    @pl.when(pl.program_id(0) == 0)
    def _():
        xnt[...] = xn_ref[...].T
        xpt[...] = xp_ref[...].T
        shared_ref[...] = matmul(xpt[...], dshared_ref[...]).astype(jnp.bfloat16)

    one_ref[0, :, 0:wide] = matmul(xnt[...], dv_ref[...]).astype(jnp.bfloat16)
    one_ref[0, :, wide : 2 * wide] = matmul(xpt[...], dg_ref[...]).astype(jnp.bfloat16)
    one_ref[0, :, 2 * wide : 2 * wide + narrow] = matmul(xpt[...], dact_ref[...]).astype(jnp.bfloat16)
    base = 2 * (wide + narrow)
    one_ref[0, :, 2 * wide + narrow : base] = matmul(xpt[...], dupd_ref[...]).astype(jnp.bfloat16)
    out = matmul_tn(hid_ref[...], dact_all_ref[...]).astype(jnp.bfloat16)
    one_ref[0, 0:wide, base:] = out[:, : D // 2]
    one_ref[0, wide:, base:] = out[:, D // 2 :]


def ffn_weights_kernel(ffn_ref, grad_ref, upper_ref, dup_ref, two_ref, fft):
    units = dup_ref.shape[1]

    @pl.when(pl.program_id(0) == 0)
    def _():
        fft[...] = ffn_ref[...].T

    two_ref[0, :, 0:units] = matmul(fft[...], dup_ref[...]).astype(jnp.bfloat16)
    two_ref[0, :, units:] = matmul_tn(upper_ref[...], grad_ref[...]).astype(jnp.bfloat16)


def held(*shape):
    return pl.BlockSpec(shape, lambda i: (0,) * len(shape), pipeline_mode=pl.Buffered(1))


def rows_block(width):
    return pl.BlockSpec((ROWS_C, width), lambda i: (i, 0))


BIG = pltpu.CompilerParams(vmem_limit_bytes=60 << 20)


def cost(flops, bytes_accessed):
    return pl.CostEstimate(flops=int(flops), transcendentals=0, bytes_accessed=int(bytes_accessed))


def ffn(middle, grad, x, act, upd, two, gain):
    count = x.shape[0]
    units = two.shape[0] * (two.shape[2] - D)
    low = jnp.bfloat16
    return pl.pallas_call(
        ffn_kernel,
        grid=(count // ROWS_C,),
        in_specs=[rows_block(D)] * 5 + [held(*two.shape), held(1, D)],
        out_specs=[rows_block(D)] * 2 + [rows_block(units)] * 2 + [rows_block(D)] * 3 + [whole(1, D)],
        out_shape=[sds((count, D), low)] * 2
        + [sds((count, units), low)] * 2
        + [sds((count, D), low)] * 3
        + [sds((1, D))],
        compiler_params=BIG,
        cost_estimate=cost(4 * count * two.size, 60 << 20),
        name="ffn",
    )(middle, grad, x, act, upd, two, gain)


def mixer_backward(
    dp, mp, d_act, d_upd, vpre, gpre, att, spre, mix, one, shared, qgain, qbias, kgain, pack, layer
):
    count = d_act.shape[0]
    units = vpre.shape[1]
    z = shared.shape[1]
    low = jnp.bfloat16

    def part(width):
        return pl.BlockSpec((ROWS_E, width), lambda i: (i, 0))

    return pl.pallas_call(
        functools.partial(backward_kernel, dp, mp),
        grid=(count // ROWS_E,),
        in_specs=[HBM, HBM]
        + [part(D)] * 2
        + [part(units)] * 3
        + [part(z), part(D)]
        + [held(*one.shape), held(*shared.shape)]
        + [held(1, z)] * 3,
        out_specs=[part(units)] * 2 + [part(z), part(D), part(D), whole(8, z)] + [HBM] * 2,
        out_shape=[sds((count, units), low)] * 2
        + [sds((count, z), low), sds((count, D)), sds((count, D), low), sds((8, z))]
        + [sds((mp, 2, pack.shape[1] >> SPLIT, pack.shape[2] // 2), low), sds((count * mp, D // mp), low)],
        scratch_shapes=swap_scratch(mp, count, D // mp)
        + reduce_scratch(dp, mp, pack.shape[1], pack.shape[2], 0, SPLIT)
        + [pltpu.SemaphoreType.DMA((mp, 2))],
        compiler_params=pltpu.CompilerParams(
            collective_id=3, has_side_effects=True, vmem_limit_bytes=61 << 20
        ),
        name="mixer_backward",
    )(pack, layer, d_act, d_upd, vpre, gpre, att, spre, mix, one, shared, qgain, qbias, kgain)


def mixer_weights(mp, xn, xp, hidden, d_act, d_value, d_gate, d_upd, d_shared):
    count = xn.shape[0]
    wide, narrow, z = d_value.shape[1] // mp, D // mp, d_shared.shape[1]
    low = jnp.bfloat16

    def part(width):
        return pl.BlockSpec((count, width), lambda i: (0, i))

    return pl.pallas_call(
        mixer_weights_kernel,
        grid=(mp,),
        in_specs=[held(count, D), held(count, D), part(wide), held(count, D)]
        + [part(wide), part(wide), part(narrow), part(narrow), held(count, z)],
        out_specs=[
            pl.BlockSpec((1, D, 2 * (wide + narrow) + D // 2), lambda i: (i, 0, 0)),
            whole(D, z),
        ],
        out_shape=[sds((mp, D, 2 * (wide + narrow) + D // 2), low), sds((D, z), low)],
        scratch_shapes=[pltpu.VMEM((D, count), low), pltpu.VMEM((D, count), low)],
        compiler_params=BIG,
        cost_estimate=cost(2 * count * D * mp * (3 * wide + 2 * narrow), 40 << 20),
        name="mixer_weights",
    )(xn, xp, hidden, d_act, d_value, d_gate, d_act, d_upd, d_shared)


def ffn_weights(mp, ffn_in, grad, upper, d_up):
    count = ffn_in.shape[0]
    units = upper.shape[1] // mp
    low = jnp.bfloat16

    def part(width):
        return pl.BlockSpec((count, width), lambda i: (0, i))

    return pl.pallas_call(
        ffn_weights_kernel,
        grid=(mp,),
        in_specs=[held(count, D), held(count, D), part(units), part(units)],
        out_specs=pl.BlockSpec((1, D, units + D), lambda i: (i, 0, 0)),
        out_shape=sds((mp, D, units + D), low),
        scratch_shapes=[pltpu.VMEM((D, count), low)],
        compiler_params=BIG,
        cost_estimate=cost(4 * count * D * mp * units, 40 << 20),
        name="ffn_weights",
    )(ffn_in, grad, upper, d_up)


MESH = pl.DeviceIdType.MESH


def rank_of(index, order):
    total = 0
    for place, bit in enumerate(order):
        total = total + lax.rem(lax.div(index, 1 << bit), 2) * (1 << place)
    return total


def flip(index, bit):
    low = lax.rem(lax.div(index, 1 << bit), 2)
    return index + (1 - 2 * low) * (1 << bit)


def orders_of(dp):
    bits = dp.bit_length() - 1
    inner = list(range(1, bits))
    return (inner + [0], inner[::-1] + [0])


def greet(dp, mp):
    me = lax.axis_index("dp")
    part = lax.axis_index("mp")
    bits = dp.bit_length() - 1
    barrier = pltpu.get_barrier_semaphore()
    for step in range(1, mp):
        pl.semaphore_signal(
            barrier, inc=1, device_id={"mp": lax.rem(part + step, mp)}, device_id_type=MESH
        )
    for bit in range(bits):
        pl.semaphore_signal(barrier, inc=1, device_id={"dp": flip(me, bit)}, device_id_type=MESH)
    pl.semaphore_wait(barrier, mp - 1 + bits)


def arrived(ref, sem):
    pltpu.make_async_copy(ref, ref, sem).wait()


def remote(src, dst, send_sem, recv_sem, axis, to):
    return pltpu.make_async_remote_copy(
        src_ref=src, dst_ref=dst, send_sem=send_sem, recv_sem=recv_sem,
        device_id={axis: to}, device_id_type=MESH,
    )


def span_of(index, size):
    return pl.ds(pl.multiple_of(index * size, size), size)


class Swap:
    def __init__(self, mp, src, dst, sems, back=False):
        self.mp, self.src, self.dst, self.back = mp, src, dst, back
        self.hold, self.send, self.recv, self.own = sems
        self.part = lax.axis_index("mp")
        if back:
            self.rows, self.width = src.shape[0], dst.shape[1]
        else:
            self.rows, self.width = dst.shape[0], src.shape[1]

    def piece(self, index):
        if self.back:
            return self.src.at[:, span_of(index, self.width)]
        return self.src.at[span_of(index, self.rows), :]

    def place(self, index):
        if self.back:
            return self.dst.at[span_of(index, self.rows), :]
        return self.dst.at[:, span_of(index, self.width)]

    def load(self):
        return pltpu.make_async_copy(self.piece(self.part), self.hold, self.own.at[0])

    def store(self):
        return pltpu.make_async_copy(self.hold, self.place(self.part), self.own.at[1])

    def copies(self):
        for step in range(1, self.mp):
            to = lax.rem(self.part + step, self.mp)
            yield remote(
                self.piece(to), self.place(self.part),
                self.send.at[step], self.recv.at[self.part], "mp", to,
            )

    def start(self):
        self.load().start()
        for copy in self.copies():
            copy.start()

    def turn(self):
        self.load().wait()
        self.store().start()

    def receive(self):
        self.store().wait()
        for step in range(1, self.mp):
            source = lax.rem(self.part + step, self.mp)
            arrived(self.place(source), self.recv.at[source])

    def close(self):
        for copy in self.copies():
            copy.wait_send()


class Gather:
    def __init__(self, dp, mp, srcs, dst, sems):
        self.dp, self.mp, self.srcs, self.dst = dp, mp, srcs, dst
        self.hold, self.line_send, self.pass_send, self.line_recv, self.send, self.recv, self.own = sems
        self.me, self.part = lax.axis_index("dp"), lax.axis_index("mp")
        self.bits = dp.bit_length() - 1
        self.orders = orders_of(dp)

    def region(self, ref, half, index, held):
        total = ref.shape[0] // 2
        share = total // self.dp
        first = lax.div(rank_of(index, self.orders[half]), 1 << held) * (share << held)
        return ref.at[pl.ds(pl.multiple_of(half * total + first, share), share << held), :]

    def spans(self):
        first = 0
        for ref in self.srcs:
            folded = ref.shape[0] < self.dst.shape[1]
            width = ref.shape[1] // 2 if folded else ref.shape[1]
            yield ref, slice(first, first + width), width, folded
            first += width

    def loads(self):
        there = self.dst.at[self.part] if self.hold is None else self.hold
        total = self.dst.shape[1] // 2
        for place, (ref, columns, width, folded) in enumerate(self.spans()):
            if not folded:
                yield pltpu.make_async_copy(ref, there.at[:, columns], self.own.at[place])
                continue
            for half in range(2):
                yield pltpu.make_async_copy(
                    ref.at[:, half * width : (half + 1) * width],
                    there.at[half * total : (half + 1) * total, columns],
                    self.own.at[place + half],
                )

    def store(self):
        return pltpu.make_async_copy(self.hold, self.dst.at[self.part], self.own.at[7])

    def turn(self):
        for copy in self.loads():
            copy.wait()
        if self.hold is not None:
            self.store().start()

    def first(self, up):
        to = self.part + 1 if up else self.part - 1
        total = self.dst.shape[1] // 2
        share = total // self.dp
        for half in range(2):
            first = pl.multiple_of(rank_of(self.me, self.orders[half]) * share, share)
            whole_rows = pl.ds(pl.multiple_of(half * total + first, share), share)
            for place, (ref, columns, width, folded) in enumerate(self.spans()):
                if folded:
                    piece = ref.at[pl.ds(first, share), half * width : (half + 1) * width]
                else:
                    piece = ref.at[whole_rows, :]
                yield remote(
                    piece, self.dst.at[self.part].at[whole_rows, columns],
                    self.line_send.at[place, int(up), half], self.line_recv.at[self.part, half],
                    "mp", to,
                )

    def passed(self, source):
        to = jnp.where(source < self.part, self.part + 1, self.part - 1)
        for half in range(2):
            held = self.region(self.dst.at[source], half, self.me, 0)
            yield remote(
                held, held, self.pass_send.at[source, half], self.line_recv.at[source, half], "mp", to
            )

    def passes(self, source):
        return jnp.logical_or(
            jnp.logical_and(source < self.part, self.part < self.mp - 1),
            jnp.logical_and(source > self.part, self.part > 0),
        )

    def doubled(self, source, stage):
        for half in range(2):
            held = self.region(self.dst.at[source], half, self.me, stage)
            yield remote(
                held, held, self.send.at[stage, source, half], self.recv.at[stage, source, half],
                "dp", flip(self.me, self.orders[half][stage]),
            )

    def source(self, step):
        mp, part = self.mp, self.part
        near = [lax.rem(part + 1, 2) + part - lax.rem(part, 2)]
        low = lax.div(part, mp // 2) == 0
        far = [jnp.where(low, mp // 2 + i, mp // 2 - 1 - i) for i in range(mp // 2)]
        return (near + far)[step]

    def start(self):
        for up in (True, False):

            @pl.when(self.part < self.mp - 1 if up else self.part > 0)
            def _(up=up):
                for copy in self.first(up):
                    copy.start()

        for copy in self.loads():
            copy.start()

    def advance(self, step, stage):
        source = self.source(step)
        for half in range(2):
            if stage == 0:
                came = self.region(self.dst.at[source], half, self.me, 0)
                arrived(came, self.line_recv.at[source, half])
            else:
                other = flip(self.me, self.orders[half][stage - 1])
                came = self.region(self.dst.at[source], half, other, stage - 1)
                arrived(came, self.recv.at[stage - 1, source, half])
        if stage == 0:

            @pl.when(self.passes(source))
            def _():
                for copy in self.passed(source):
                    copy.start()

        if stage < self.bits:
            for copy in self.doubled(source, stage):
                copy.start()

    def waves(self):
        return self.mp - 1 + self.bits

    def wave(self, number):
        for stage in range(self.bits, -1, -1):
            if 0 <= number - stage < self.mp - 1:
                self.advance(number - stage, stage)

    def close(self):
        if self.hold is not None:
            self.store().wait()
        for up in (True, False):

            @pl.when(self.part < self.mp - 1 if up else self.part > 0)
            def _(up=up):
                for copy in self.first(up):
                    copy.wait_send()

        for step in range(self.mp - 1):
            source = self.source(step)

            @pl.when(self.passes(source))
            def _(source=source):
                for copy in self.passed(source):
                    copy.wait_send()

            for stage in range(self.bits):
                for copy in self.doubled(source, stage):
                    copy.wait_send()


def swap_scratch(mp, rows, width, dtype=jnp.bfloat16):
    dma = pltpu.SemaphoreType.DMA
    return [pltpu.VMEM((rows, width), dtype), dma((mp,)), dma((mp,)), dma((2,))]


def gather_scratch(dp, mp, pack):
    dma = pltpu.SemaphoreType.DMA
    bits = dp.bit_length() - 1
    return [
        pltpu.VMEM(pack.shape, pack.dtype), dma((5, 2, 2)), dma((mp, 2)), dma((mp, 2)),
        dma((bits, mp, 2)), dma((bits, mp, 2)), dma((8,)),
    ]


HBM = pl.BlockSpec(memory_space=pl.ANY)


def forward_kernel(
    dp, mp, span,
    small_ref, v_ref, g_ref, m_ref, u_ref, o_ref, tok_ref, shared_ref, qgain_ref, qbias_ref, kgain_ref,
    up_ref, down_ref, cot_ref,
    xn_ref, xp_ref, mix_ref, starts_ref, keep_ref, weight_ref, gains_ref,
    vpre_ref, gpre_ref, att_ref, hid_ref, act_ref, upd_ref, mid_ref, spre_ref,
    one_out, x_out, full_ref, grad_ref,
    one_ref, x_all, small_all, xn_all, rows, outs, ends, starts, state_ref,
    carry_send, carry_recv, out_sem, *sems,
):
    index = pl.program_id(0)
    steps = pl.num_programs(0) // 2
    part = lax.axis_index("mp")
    swap = Swap(mp, cot_ref, grad_ref, sems[0:4])
    plan = Gather(dp, mp, (up_ref, down_ref), full_ref, sems[4:11])
    tokens = Swap(mp, tok_ref, x_all, sems[11:15])
    tiny = Swap(mp, small_ref, small_all, sems[15:19], back=True)
    firsts = (v_ref, g_ref, m_ref, u_ref, o_ref)
    opening = Gather(dp, mp, firsts, one_ref, (None,) + tuple(sems[19:25]))
    gives = lax.rem(part + 1, span) != 0
    takes = lax.rem(part, span) != 0
    gain_ref, omega_ref = gains_ref.at[0:1, :], gains_ref.at[1:2, :]

    def carry():
        return remote(ends, starts, carry_send.at[0], carry_recv.at[0], "mp", part + 1)

    def one_copy():
        return pltpu.make_async_copy(one_ref, one_out, out_sem.at[0])

    def x_copy():
        return pltpu.make_async_copy(x_all, x_out, out_sem.at[1])

    @pl.when(index == 0)
    def _():
        greet(dp, mp)
        tiny.start()
        opening.start()
        tiny.turn()
        opening.turn()
        for number in range(opening.waves()):
            opening.wave(number)
            if number == 0:
                tokens.start()
            if number == 2:
                plan.start()
            if number == 4:
                swap.start()
        tokens.turn()
        tiny.receive()
        lines = small_all.shape[0] // mp
        width = small_all.shape[1]
        gains_ref[...] = jnp.zeros_like(gains_ref)
        for m in range(mp):
            block = small_all[m * lines : (m + 1) * lines, :]
            delta, alpha, beta, eta = (block[NDIM * i : NDIM * (i + 1), :] for i in range(4))
            rate = jax.nn.sigmoid(delta)
            keep = 1.0 - rate * jax.nn.sigmoid(alpha)
            weight = rate * beta * eta
            for piece in range(width // LANES):
                there = pl.ds(m * (width // LANES) + piece, NDIM, stride=SUB)
                keep_ref[there, :] = keep[:, piece * LANES : (piece + 1) * LANES]
                weight_ref[there, :] = weight[:, piece * LANES : (piece + 1) * LANES]
            gains_ref[0:3, m * width : (m + 1) * width] = block[4 * NDIM : 4 * NDIM + 3, :]
        tokens.receive()
        one_copy().start()
        x_copy().start()
        ends[...] = jnp.zeros_like(ends)

    @pl.when(index < steps)
    def _():
        keep = [keep_ref[j * SUB : (j + 1) * SUB, :] for j in range(NDIM)]
        for piece in range(ROWS_C // TB):
            here = slice(piece * TB, (piece + 1) * TB)
            x = x_all[
                pl.ds(pl.multiple_of(index * ROWS_C + piece * TB, TB), TB), :
            ].astype(jnp.float32)
            mean = jnp.mean(x, axis=1, keepdims=True)
            power = jnp.mean(x * x, axis=1, keepdims=True)
            scale = lax.rsqrt(power - mean * mean + EPS)
            xn = ((x - mean) * scale * gain_ref[...]).astype(jnp.bfloat16)
            xn_ref[here, :] = xn
            xn_all[pl.ds(pl.multiple_of(index * ROWS_C + piece * TB, TB), TB), :] = xn
            to_rows(rows, xn.astype(jnp.float32))

            def step(t, carried):
                state, slope = carried
                now = row(rows, t)
                slope = tuple(keep[j] * slope[j] + state[j] for j in range(NDIM))
                state = tuple(keep[j] * state[j] + now for j in range(NDIM))
                return (state, slope)

            state = tuple(ends[j] for j in range(NDIM))
            slope = tuple(ends[NDIM + j] for j in range(NDIM))
            state, slope = lax.fori_loop(0, TB, step, (state, slope), unroll=4)
            for j in range(NDIM):
                ends[j] = state[j]
                ends[NDIM + j] = slope[j]

    @pl.when(index == steps - 1)
    def _():
        @pl.when(gives)
        def _():
            carry().start()

        plan.turn()

    @pl.when(index == steps)
    def _():
        @pl.when(jnp.logical_not(takes))
        def _():
            starts[...] = jnp.zeros_like(starts)

        @pl.when(takes)
        def _():
            arrived(starts, carry_recv.at[0])

        @pl.when(gives)
        def _():
            carry().wait_send()

        for j in range(NDIM):
            state_ref[j] = starts[j]
        starts_ref[...] = starts[...]

    @pl.when(index >= steps)
    def _():
        for piece in range(ROWS_C // TB):
            here = slice(piece * TB, (piece + 1) * TB)
            xn = xn_all[
                pl.ds(pl.multiple_of((index - steps) * ROWS_C + piece * TB, TB), TB), :
            ].astype(jnp.float32)
            to_rows(rows, xn)
            keep = [keep_ref[j * SUB : (j + 1) * SUB, :] for j in range(NDIM)]

            def step(t, state):
                now = row(rows, t)
                state = tuple(keep[j] * state[j] + now for j in range(NDIM))
                terms = [weight_ref[j * SUB : (j + 1) * SUB, :] * state[j] for j in range(NDIM)]
                while len(terms) > 1:
                    terms = [a + b for a, b in zip(terms[::2], terms[1::2])]
                outs[pl.ds(pl.multiple_of(t * SUB, SUB), SUB), :] = terms[0]
                return state

            state = lax.fori_loop(0, TB, step, tuple(state_ref[j] for j in range(NDIM)), unroll=4)
            for j in range(NDIM):
                state_ref[j] = state[j]
            mix = from_rows(outs) + omega_ref[...] * xn
            mix_ref[here, :] = mix
            xp_ref[here, :] = (mix * sigmoid(mix)).astype(jnp.bfloat16)

        there = pl.ds(pl.multiple_of((index - steps) * ROWS_C, ROWS_C), ROWS_C)
        mixer_forward_kernel(
            xn_all.at[there, :], xp_ref, x_all.at[there, :], one_ref, shared_ref, qgain_ref, qbias_ref, kgain_ref,
            vpre_ref, gpre_ref, att_ref, hid_ref, act_ref, upd_ref, mid_ref, spre_ref,
        )

    for number in range(plan.waves()):

        @pl.when(index == jnp.minimum(number + 2, 2 * steps - 1))
        def _(number=number):
            plan.wave(number)

    @pl.when(index == 2 * steps - 1)
    def _():
        swap.turn()
        swap.receive()
        for item in (swap, plan, tokens, tiny, opening):
            item.close()
        one_copy().wait()
        x_copy().wait()


def forward(dp, mp, span, units, small, firsts, tokens, shared, vectors, packs, cotangent):
    count = tokens.shape[0] // mp
    steps = count // ROWS_C
    z = shared.shape[1]
    low = jnp.bfloat16
    early = pl.BlockSpec((ROWS_C, D), lambda i: (jnp.minimum(i, steps - 1), 0))

    def late(width):
        return pl.BlockSpec((ROWS_C, width), lambda i: (jnp.maximum(i - steps, 0), 0))

    dma = pltpu.SemaphoreType.DMA
    lines, width = small.shape[0], small.shape[1] // mp
    first = sds((D, sum(item.size for item in firsts) // D), low)
    pack = sds((D, sum(item.size for item in packs) // D), low)
    return pl.pallas_call(
        functools.partial(forward_kernel, dp, mp, span),
        grid=(2 * steps,),
        in_specs=[HBM] * 7 + [held(*shared.shape)] + [held(1, z)] * 3 + [HBM] * 3,
        out_specs=[early, late(D), late(D), whole(*STATES)]
        + [whole(NDIM * SUB, LANES)] * 2
        + [whole(8, D)]
        + [late(units)] * 4
        + [late(D)] * 3
        + [late(z)]
        + [HBM] * 4,
        out_shape=[sds((count, D), low), sds((count, D), low), sds((count, D)), sds(STATES)]
        + [sds((NDIM * SUB, LANES))] * 2
        + [sds((8, D))]
        + [sds((count, units), low)] * 4
        + [sds((count, D), low)] * 2
        + [sds((count, D)), sds((count, z))]
        + [sds((mp,) + first.shape, low), sds((count, D), low)]
        + [sds((mp,) + pack.shape, low), sds((count, D), low)],
        scratch_shapes=[
            pltpu.VMEM((mp,) + first.shape, low), pltpu.VMEM((count, D), low),
            pltpu.VMEM((mp * lines, width), jnp.float32), pltpu.VMEM((count, D), low), ROWS, ROWS,
            pltpu.VMEM(STATES, jnp.float32), pltpu.VMEM(STATES, jnp.float32),
            pltpu.VMEM(STATE, jnp.float32), dma((1,)), dma((1,)), dma((2,)),
        ]
        + swap_scratch(mp, count, cotangent.shape[1])
        + gather_scratch(dp, mp, pack)
        + swap_scratch(mp, count, tokens.shape[1])
        + swap_scratch(mp, lines, width, small.dtype)
        + gather_scratch(dp, mp, first)[1:],
        compiler_params=pltpu.CompilerParams(
            collective_id=1, has_side_effects=True, vmem_limit_bytes=61 << 20
        ),
        name="forward",
    )(small, *firsts, tokens, shared, *vectors, *packs, cotangent)


def add_rows(acc, first, other, count):
    chunk = min(count, 32)

    def step(index, _):
        there = pl.ds(pl.multiple_of(first + index * chunk, chunk), chunk)
        here = pl.ds(pl.multiple_of(index * chunk, chunk), chunk)
        total = acc[there, :].astype(jnp.float32) + other[here, :].astype(jnp.float32)
        acc[there, :] = total.astype(jnp.bfloat16)
        return 0

    lax.fori_loop(0, count // chunk, step, 0)


class Across:
    def __init__(self, dp, mp, mine, out, refs, sums=None):
        self.dp, self.mp, self.mine, self.out, self.sums = dp, mp, mine, out, sums
        (
            self.lines, self.last, self.line_send, self.line_recv,
            self.last_send, self.last_recv, self.ring_send, self.ring_recv, self.own,
        ) = refs
        self.me, self.part = lax.axis_index("dp"), lax.axis_index("mp")
        self.bits = dp.bit_length() - 1
        self.orders = orders_of(dp)
        if sums is None:
            self.share = out.shape[0] // dp
            self.width = out.shape[1] // 2
        else:
            self.share, self.width = sums.shape[1], sums.shape[2]

    def shard(self, i):
        near, far = flip(self.part, 0), flip(self.part, 1)
        return (flip(far, 0), far, near, self.part)[i]

    def kept(self, half, src=None):
        src = self.mine(self.mp - 1, half) if src is None else src
        dst = self.rows_at(half, self.me, 0) if self.sums is None else self.sums.at[half]
        return pltpu.make_async_copy(src, dst, self.own.at[half])

    def across(self, i, half):
        if i % 2 == 0:
            return remote(
                self.mine(i, half), self.lines.at[self.shard(i), half],
                self.line_send.at[i // 2, half], self.line_recv.at[self.shard(i), half],
                "mp", flip(self.part, 0),
            )
        return remote(
            self.mine(i, half), self.last.at[half],
            self.last_send.at[half], self.last_recv.at[half], "mp", flip(self.part, 1),
        )

    def ring(self, half, stage):
        rows = self.rows_at(half, self.me, stage)
        return remote(
            rows, rows, self.ring_send.at[stage, half], self.ring_recv.at[stage, half],
            "dp", flip(self.me, self.orders[half][stage]),
        )

    def rows_at(self, half, index, stage):
        rank = rank_of(index, self.orders[half])
        first = lax.div(rank, 1 << stage) * (self.share << stage)
        return self.out.at[
            pl.ds(pl.multiple_of(first, self.share), self.share << stage),
            half * self.width : (half + 1) * self.width,
        ]

    def fold(self, i):
        for half in range(2):
            mine = self.mine(i, half)
            if i % 2:
                came = self.lines.at[self.shard(i), half]
                arrived(came, self.line_recv.at[self.shard(i), half])
                add_rows(mine, 0, came, self.share)
            if i < self.mp - 1:
                self.across(i, half).start()
            else:
                came = self.last.at[half]
                arrived(came, self.last_recv.at[half])
                add_rows(mine, 0, came, self.share)
                self.kept(half).start()

    def spread(self, stage):
        for half in range(2):
            if stage == 0:
                arrived(self.rows_at(half, self.me, 0), self.own.at[half])
            else:
                other = flip(self.me, self.orders[half][stage - 1])
                arrived(self.rows_at(half, other, stage - 1), self.ring_recv.at[stage - 1, half])
            if stage < self.bits:
                self.ring(half, stage).start()

    def close(self, summed=True):
        for half in range(2):
            for i in range(self.mp - 1):
                if summed:
                    self.across(i, half).wait_send()
            if self.sums is not None:
                self.kept(half).wait()
                continue
            for stage in range(self.bits):
                self.ring(half, stage).wait_send()


class Reduce:
    def __init__(self, dp, mp, src, share, width, stage, load, recvs, send, recv, first, stop):
        self.dp, self.mp, self.src, self.stage, self.load = dp, mp, src, stage, load
        self.share, self.width, self.first, self.stop = share, width, first, stop
        self.recvs, self.send, self.recv = recvs, send, recv
        self.acc = recvs[0] if first == 0 else stage
        self.base = max(first, 1)
        self.tail = self.sums = self.sums_sem = None
        self.me, self.part = lax.axis_index("dp"), lax.axis_index("mp")
        self.bits = dp.bit_length() - 1
        self.orders = orders_of(dp)

    def shard(self, i):
        near, far = flip(self.part, 0), flip(self.part, 1)
        return (flip(far, 0), far, near, self.part)[i]

    def rank(self, half, index):
        return rank_of(index, self.orders[half])

    def top(self, half, index):
        count = self.share << (self.bits - 1)
        return span_of(lax.div(self.rank(half, index), 1 << (self.bits - 1)), count)

    def offset(self, half, index, stage):
        low = lax.rem(self.rank(half, index), 1 << (self.bits - self.base))
        left = self.bits - 1 - stage
        return pl.multiple_of(lax.div(low, 1 << left) * (self.share << left), self.share)

    def columns(self, half):
        return slice(half * self.width, (half + 1) * self.width)

    def rows(self, i, half, index, stage):
        first = self.offset(half, index, stage)
        count = self.share << (self.bits - 1 - stage)
        return self.acc.at[self.shard(i), half].at[pl.ds(first, count), :]

    def give(self, i, half, stage):
        m = self.shard(i)
        place = stage - self.first
        other = flip(self.me, self.orders[half][self.bits - 1 - stage])
        if stage == 0:
            rows = self.src.at[m, self.top(half, other), self.columns(half)]
        else:
            rows = self.rows(i, half, other, stage)
        return remote(
            rows, self.recvs[place].at[m, half],
            self.send.at[place, i, half], self.recv.at[place, m, half], "dp", other,
        )

    def mine(self, i, half):
        return self.rows(i, half, self.me, self.bits - 1)

    def saved(self, i, half):
        return pltpu.make_async_copy(
            self.rows(i, half, self.me, self.stop - 1),
            self.sums.at[self.shard(i), half],
            self.sums_sem.at[i, half],
        )

    def begin(self, i):
        for half in range(2):
            self.give(i, half, self.first).start()
            if self.first == 0:
                pltpu.make_async_copy(
                    self.src.at[self.shard(i), self.top(half, self.me), self.columns(half)],
                    self.stage.at[i, half], self.load.at[i, half],
                ).start()

    def fold(self, i, stage):
        m = self.shard(i)
        place = stage - self.first
        count = self.share << (self.bits - 1 - stage)
        for half in range(2):
            acc = self.acc.at[m, half]
            came = self.recvs[place].at[m, half]
            arrived(came, self.recv.at[place, m, half])
            if stage == 0:
                own = self.stage.at[i, half]
                arrived(own, self.load.at[i, half])
                add_rows(acc, 0, own, count)
            else:
                add_rows(acc, self.offset(half, self.me, stage), came, count)
            if stage < self.stop - 1:
                self.give(i, half, stage + 1).start()
            elif self.sums is not None:
                self.saved(i, half).start()
        if stage == self.bits - 1:
            self.tail.fold(i)

    def waves(self):
        return self.mp + LAG * (self.stop - 1) + 1

    def wave(self, number):
        for stage in range(self.stop):
            i = number - 1 - LAG * stage
            if 0 <= i < self.mp:
                self.fold(i, stage)
        if number == 0:
            for i in range(self.mp):
                self.begin(i)

    def close(self):
        for half in range(2):
            for i in range(self.mp):
                for stage in range(self.first, self.stop):
                    self.give(i, half, stage).wait_send()
                if self.sums is not None:
                    self.saved(i, half).wait()
        if self.tail is not None:
            self.tail.close()


def across_scratch(dp, mp, total, width):
    low = jnp.bfloat16
    dma = pltpu.SemaphoreType.DMA
    bits = dp.bit_length() - 1
    return [
        pltpu.VMEM((mp, 2, total // dp, width // 2), low), pltpu.VMEM((2, total // dp, width // 2), low),
        dma((2, 2)), dma((mp, 2)), dma((2,)), dma((2,)), dma((bits, 2)), dma((bits, 2)), dma((2,)),
    ]


def reduce_scratch(dp, mp, total, width, first, stop):
    low = jnp.bfloat16
    dma = pltpu.SemaphoreType.DMA
    half = width // 2
    held = total // 2 if first == 0 else total >> first
    stages = [pltpu.VMEM((mp, 2, held, half), low), dma((mp, 2))]
    stages += [pltpu.VMEM((mp, 2, total >> (i + 1), half), low) for i in range(first, stop)]
    return stages + [dma((stop - first, mp, 2)), dma((stop - first, mp, 2))]


def reduce_plan(dp, mp, src, total, width, refs, first, stop):
    count = stop - first
    plan = Reduce(
        dp, mp, src, total // dp, width // 2, refs[0], refs[1], refs[2 : 2 + count],
        refs[2 + count], refs[3 + count], first, stop,
    )
    return plan, refs[4 + count :]


class Tiny:
    def __init__(self, dp, mp, piece, line, ring, came, sems, waits):
        self.dp, self.mp, self.piece, self.waits = dp, mp, piece, waits
        self.line, self.ring, self.came = line, ring, came
        self.send, self.recv, self.ring_send, self.ring_recv = sems
        self.me, self.part = lax.axis_index("dp"), lax.axis_index("mp")
        self.bits = dp.bit_length() - 1

    def push(self, copy):
        copy.start()
        self.waits.append(copy.wait_send)

    def start(self):
        for step in range(1, self.mp):
            to = lax.rem(self.part + step, self.mp)
            self.push(
                remote(
                    self.piece(to), self.line.at[self.part],
                    self.send.at[step], self.recv.at[self.part], "mp", to,
                )
            )

    def fold(self, stage):
        if stage == 0:
            total = self.piece(self.part)[...].astype(jnp.float32)
            for step in range(1, self.mp):
                source = lax.rem(self.part + step, self.mp)
                arrived(self.line.at[source], self.recv.at[source])
                total = total + self.line[source].astype(jnp.float32)
        else:
            arrived(self.came.at[stage - 1], self.ring_recv.at[stage - 1])
            total = self.ring[stage - 1] + self.came[stage - 1]
        self.ring[stage] = total
        if stage < self.bits:
            self.push(
                remote(
                    self.ring.at[stage], self.came.at[stage],
                    self.ring_send.at[stage], self.ring_recv.at[stage],
                    "dp", flip(self.me, stage),
                )
            )


def tiny_sems(dp, mp):
    dma = pltpu.SemaphoreType.DMA
    bits = dp.bit_length() - 1
    return [dma((mp,)), dma((mp,)), dma((bits,)), dma((bits,))]


FEATURES = 40


def closing_kernel(
    dp, mp, span,
    one_ref, two_ref, grad_ref, xn_ref, x_ref, normed_ref, direct_ref, shared_ref, vector_ref,
    keep_ref, weight_ref, gain_ref, omega_ref, ffn_ref, starts_ref,
    one_out, two_out, token_out, feat_out, shared_out, vector_out,
    *refs,
):
    bits = dp.bit_length() - 1
    me, part = lax.axis_index("dp"), lax.axis_index("mp")
    waits = []
    taken = 0
    _, total, width = one_ref.shape
    pack, refs = reduce_plan(dp, mp, one_ref, total, width, refs, 0, bits)
    pack.tail = Across(dp, mp, pack.mine, one_out, refs[:9])
    other, refs = reduce_plan(dp, mp, None, total, width, refs[9:], SPLIT, bits)
    other.tail = Across(dp, mp, other.mine, two_out, refs[:9])
    refs = refs[9:]

    def take(count):
        nonlocal taken
        taken += count
        return refs[taken - count : taken]

    grad, xn, x, normed_part, direct, tokens, rows, outs, states, ahead, sums, feat = take(12)
    shared, shared_line, shared_ring, shared_came, shared_low = take(5)
    feat_line, feat_ring, feat_came = take(3)
    vector, vector_line, vector_ring, vector_came = take(4)
    (in_sem,) = take(1)
    carry_send, carry_recv = take(2)
    spread_send, spread_recv, spread_own = take(3)
    token = Swap(mp, tokens, token_out, take(4), back=True)
    quarter = shared.shape[0] // mp
    columns = feat.shape[1] // mp
    tiny_shared = Tiny(
        dp, mp, lambda m: shared.at[span_of(m, quarter), :],
        shared_line, shared_ring, shared_came, take(4), waits,
    )
    tiny_vector = Tiny(
        dp, mp, lambda m: vector, vector_line, vector_ring, vector_came, take(4), waits
    )
    tiny_feat = Tiny(
        dp, mp, lambda m: feat.at[:, span_of(m, columns)],
        feat_line, feat_ring, feat_came, take(4), waits,
    )
    loads = [
        pltpu.make_async_copy(src, dst, in_sem.at[i])
        for i, (src, dst) in enumerate(
            (
                (grad_ref, grad), (xn_ref, xn), (x_ref, x), (normed_ref, normed_part),
                (direct_ref, direct), (shared_ref, shared), (vector_ref, vector),
            )
        )
    ]
    count = grad.shape[0]
    blocks = count // TB
    keep = lambda dims: [keep_ref[j] for j in dims]
    every = range(NDIM)
    gives = lax.rem(part, span) != 0
    takes = lax.rem(part + 1, span) != 0

    def carry():
        return remote(outs.at[0 : NDIM * SUB, :], ahead, carry_send.at[0], carry_recv.at[0], "mp", part - 1)

    def slot_of(j):
        return slice(j * SUB, (j + 1) * SUB)

    def adjoint():
        loads[0].wait()
        kept = keep(every)

        def block_step(number, state):
            first = pl.multiple_of((blocks - 1 - number) * TB, TB)
            to_rows(rows, grad[pl.ds(first, TB), :])

            def step(t, state):
                now = row(rows, TB - 1 - t)
                return tuple(kept[j] * state[j] + now for j in every)

            return lax.fori_loop(0, TB, step, state, unroll=4)

        zero = jnp.zeros((SUB, LANES), jnp.float32)
        state = lax.fori_loop(0, blocks, block_step, tuple(zero for _ in every))
        for j in every:
            outs[slot_of(j), :] = state[j]

        @pl.when(gives)
        def _():
            carry().start()

        for j in range(2 * NDIM):
            states[j] = starts_ref[j]
        sums[...] = jnp.zeros_like(sums)
        feat[...] = jnp.zeros_like(feat)
        feat[34:35, :] = ffn_ref[...]
        loads[1].wait()

    def params(low, high):
        half = NDIM // 2

        def block_step(number, _):
            first = pl.multiple_of(number * TB, TB)
            now_xn = xn[pl.ds(first, TB), :].astype(jnp.float32)
            now_grad = grad[pl.ds(first, TB), :]
            to_rows(rows, now_xn)
            for piece in range(SUB):
                turned[pl.ds(piece, TB, stride=SUB), :] = now_grad[:, piece * LANES : (piece + 1) * LANES]
            feat[32:33, :] += jnp.sum(now_grad * now_xn, axis=0, keepdims=True)
            for start in (0, half):
                dims = range(start, start + half)
                kept = keep(dims)

                def step(t, carried):
                    state, slope, weight_sum, keep_sum = carried
                    now = row(rows, t)
                    grad_now = row(turned, t)
                    slope = tuple(kept[j] * slope[j] + state[j] for j in range(half))
                    state = tuple(kept[j] * state[j] + now for j in range(half))
                    weight_sum = tuple(weight_sum[j] + grad_now * state[j] for j in range(half))
                    keep_sum = tuple(keep_sum[j] + grad_now * slope[j] for j in range(half))
                    return (state, slope, weight_sum, keep_sum)

                carried = (
                    tuple(states[j] for j in dims),
                    tuple(states[NDIM + j] for j in dims),
                    tuple(sums[slot_of(j), :] for j in dims),
                    tuple(sums[slot_of(NDIM + j), :] for j in dims),
                )
                state, slope, weight_sum, keep_sum = lax.fori_loop(0, TB, step, carried, unroll=4)
                for place, j in enumerate(dims):
                    states[j] = state[place]
                    states[NDIM + j] = slope[place]
                    sums[slot_of(j), :] = weight_sum[place]
                    sums[slot_of(NDIM + j), :] = keep_sum[place]
            return 0

        lax.fori_loop(low, high, block_step, 0)

    def meet():
        @pl.when(gives)
        def _():
            carry().wait_send()

        @pl.when(jnp.logical_not(takes))
        def _():
            ahead[...] = jnp.zeros_like(ahead)

        @pl.when(takes)
        def _():
            arrived(ahead, carry_recv.at[0])

        for copy in loads[2:5]:
            copy.wait()

    def token_rows(low, high):
        kept = keep(every)

        def block_step(number, state):
            there = pl.ds(pl.multiple_of((blocks - 1 - number) * TB, TB), TB)
            now_grad = grad[there, :]
            to_rows(rows, now_grad)

            def step(t, state):
                place = TB - 1 - t
                now = row(rows, place)
                state = tuple(kept[j] * state[j] + now for j in every)
                terms = [weight_ref[j] * state[j] for j in every]
                while len(terms) > 1:
                    terms = [a + b for a, b in zip(terms[::2], terms[1::2])]
                outs[pl.ds(pl.multiple_of(place * SUB, SUB), SUB), :] = terms[0]
                return state

            state = lax.fori_loop(0, TB, step, state, unroll=4)
            d_xn = from_rows(outs) + now_grad * omega_ref[...]
            d_xn = d_xn + normed_part[there, :].astype(jnp.float32)
            now_x = x[there, :].astype(jnp.float32)
            mean = jnp.mean(now_x, axis=1, keepdims=True)
            power = jnp.mean(now_x * now_x, axis=1, keepdims=True)
            scale = lax.rsqrt(power - mean * mean + EPS)
            normed = (now_x - mean) * scale
            feat[33:34, :] += jnp.sum(d_xn * normed, axis=0, keepdims=True)
            scaled = d_xn * gain_ref[...]
            first = jnp.mean(scaled, axis=1, keepdims=True)
            second = jnp.mean(scaled * normed, axis=1, keepdims=True)
            back = scale * (scaled - first - normed * second)
            tokens[there, :] = (direct[there, :].astype(jnp.float32) + back).astype(jnp.bfloat16)
            return state

        state = tuple(ahead[slot_of(j), :] for j in every)
        state = lax.fori_loop(low, high, block_step, state)
        for j in every:
            ahead[slot_of(j), :] = state[j]

    def gathered():
        for piece in range(SUB):
            feat[0 : 2 * NDIM, piece * LANES : (piece + 1) * LANES] = sums[
                pl.ds(piece, 2 * NDIM, stride=SUB), :
            ]
        token.start()
        tiny_feat.start()

    def shared_back():
        low = shared_ring[bits].astype(jnp.bfloat16)
        shared_low[...] = low
        there = shared_out.at[span_of(part, quarter), :]
        pltpu.make_async_copy(shared_low, there, spread_own.at[0]).start()
        for step in range(1, mp):
            to = lax.rem(part + step, mp)
            copy = remote(shared_low, there, spread_send.at[step], spread_recv.at[part], "mp", to)
            copy.start()
            waits.append(copy.wait_send)

    (turned,) = take(1)

    greet(dp, mp)
    for copy in loads:
        copy.start()
    def parts():
        return pltpu.make_async_copy(two_ref, other.stage, other.load.at[0, 0])

    def sums_ready():
        parts().wait()
        for i in range(mp):
            other.begin(i)

    def tiny_ready():
        loads[5].wait()
        loads[6].wait()
        tiny_shared.start()
        tiny_vector.start()

    def vector_ready():
        shared_back()
        vector_out[...] = vector_ring[bits]

    def feat_ready():
        feat_out[...] = feat_ring[bits]

    parts().start()
    for i in range(mp):
        pack.begin(i)
    pace = max(blocks // 4, 1)
    late = [
        lambda i=i, stage=stage: other.fold(i, stage)
        for stage in range(SPLIT, bits)
        for i in range(mp)
    ]
    work = [sums_ready, adjoint, lambda: pack.fold(0, 0), lambda: params(0, pace)]
    work += [lambda: pack.fold(1, 0), late[0], tiny_ready, lambda: params(pace, 2 * pace)]
    work += [lambda: pack.fold(2, 0), lambda: pack.fold(3, 0), late[1], lambda: params(2 * pace, 3 * pace)]
    work += [late[2], lambda: pack.fold(0, 1), lambda: params(3 * pace, blocks)]
    work += [meet, lambda: pack.fold(1, 1), lambda: token_rows(0, blocks // 2)]
    work += [lambda: pack.fold(2, 1), lambda: token_rows(blocks // 2, blocks), gathered]
    work += [lambda: pack.fold(3, 1)] + late[3:] + [lambda: other.tail.spread(0)]
    for stage in range(2, bits):
        for i in range(mp):
            work.append(lambda i=i, stage=stage: pack.fold(i, stage))
            if stage == 2 and i < 3:
                work.append(lambda i=i: other.tail.spread(1 + i))
            if stage == 2 and i <= bits:
                work.append(lambda i=i: tiny_shared.fold(i))
                work.append(lambda i=i: tiny_vector.fold(i))
    for i in range(mp, bits + 1):
        work.append(lambda i=i: other.tail.spread(i))
        work.append(lambda i=i: tiny_shared.fold(i))
        work.append(lambda i=i: tiny_vector.fold(i))
    work.append(vector_ready)
    for step in range(bits + 1):
        work.append(lambda step=step: pack.tail.spread(step))
        work.append(lambda step=step: tiny_feat.fold(step))
    work.append(feat_ready)
    for item in work:
        item()
    arrived(shared_low, spread_own.at[0])
    for step in range(1, mp):
        source = lax.rem(part + step, mp)
        arrived(shared_out.at[span_of(source, quarter), :], spread_recv.at[source])
    token.turn()
    token.receive()
    token.close()
    pack.close()
    other.close()
    for wait in waits:
        wait()


def closing(dp, mp, span, one, two, inputs, shared, vector, params, starts):
    low, full = jnp.bfloat16, jnp.float32
    bits = dp.bit_length() - 1
    dma = pltpu.SemaphoreType.DMA
    count = inputs[0].shape[0]
    _, total, width = one.shape
    z = shared.shape[1]
    quarter, columns = D // mp, D // mp

    def vmem(*shape, dtype=full):
        return pltpu.VMEM(shape, dtype)

    scratch = reduce_scratch(dp, mp, total, width, 0, bits) + across_scratch(dp, mp, total, width)
    scratch += reduce_scratch(dp, mp, total, width, SPLIT, bits) + across_scratch(dp, mp, total, width)
    scratch += [vmem(count, D)] + [vmem(count, D, dtype=low)] * 5
    scratch += [ROWS, ROWS, pltpu.VMEM(STATES, full), vmem(NDIM * SUB, LANES)]
    scratch += [vmem(2 * NDIM * SUB, LANES), vmem(FEATURES, D)]
    scratch += [
        vmem(D, z, dtype=low), vmem(mp, quarter, z, dtype=low), vmem(bits + 1, quarter, z),
        vmem(bits, quarter, z), vmem(quarter, z, dtype=low),
    ]
    scratch += [vmem(mp, FEATURES, columns), vmem(bits + 1, FEATURES, columns), vmem(bits, FEATURES, columns)]
    scratch += [vmem(8, z), vmem(mp, 8, z), vmem(bits + 1, 8, z), vmem(bits, 8, z)]
    scratch += [dma((7,)), dma((1,)), dma((1,)), dma((mp,)), dma((mp,)), dma((1,))]
    scratch += swap_scratch(mp, count, D // mp) + tiny_sems(dp, mp) * 3
    scratch += [ROWS]
    near = pl.BlockSpec(memory_space=pltpu.VMEM)
    return pl.pallas_call(
        functools.partial(closing_kernel, dp, mp, span),
        in_specs=[HBM] * 9 + [near] * 6,
        out_specs=[HBM] * 3 + [near, HBM, near],
        out_shape=[
            sds((total, width), low), sds((total, width), low), sds((count * mp, D // mp), low),
            sds((FEATURES, columns)), sds((D, z), low), sds((8, z)),
        ],
        scratch_shapes=scratch,
        compiler_params=pltpu.CompilerParams(
            collective_id=2, has_side_effects=True, vmem_limit_bytes=61 << 20
        ),
        name="closing",
    )(one, two, *inputs, shared, vector, *params, starts)


def local(
    dp,
    mp,
    tokens,
    cotangent,
    norm_gain,
    ema_delta,
    ema_alpha,
    ema_beta,
    ema_eta,
    ema_omega,
    shared_proj,
    query_gain,
    query_bias,
    key_gain,
    value_proj,
    gate_proj,
    mixer_proj,
    update_proj,
    output_proj,
    ffn_gain,
    up_proj,
    down_proj,
):
    width = tokens.shape[1]
    count = tokens.shape[0] // mp
    span = LEN // count
    small = jnp.concatenate(
        [
            ema_delta, ema_alpha, ema_beta, ema_eta,
            norm_gain[:, None], ema_omega[:, None], ffn_gain[:, None],
        ],
        axis=1,
    ).T
    lines = small.shape[0]
    small = jnp.pad(small, ((0, -lines % 8), (0, 0)))
    firsts = (value_proj, gate_proj, mixer_proj, update_proj, output_proj)
    vectors = (query_gain[None], query_bias[None], key_gain[None])
    wide, narrow = value_proj.shape[1], mixer_proj.shape[1]
    (
        xn, xp, mix_pre, starts, keep, weight, gains,
        vpre, gpre, att, hidden, act_pre, upd_pre, middle, spre, one, x_low, two, grad_out,
    ) = forward(
        dp, mp, span, mp * wide, jnp.tile(small, (1, mp)), firsts, tokens, shared_proj, vectors,
        (up_proj, down_proj), cotangent,
    )
    keep, weight = keep.reshape(STATE), weight.reshape(STATE)
    gain, omega, gain_two = gains[0:1], gains[1:2], gains[2:3]
    layer_rows, ffn_in, upper, d_up, d_act, d_upd, d_inputs, ffn_part = ffn(
        middle, grad_out, x_low, act_pre, upd_pre, two, gain_two
    )
    two_grad = ffn_weights(mp, ffn_in, grad_out, upper, d_up)
    (
        d_value, d_gate, d_shared, d_mix_pre, normed_part, vector_sums, two_sums, layer_out,
    ) = mixer_backward(
        dp, mp, d_act, d_upd, vpre, gpre, att, spre, mix_pre, one, shared_proj, *vectors,
        two_grad, layer_rows,
    )
    one_grad, shared_part = mixer_weights(
        mp, xn, xp, hidden, d_act, d_value, d_gate, d_upd, d_shared
    )

    one_grad, two_grad, token_grad, feature, shared_grad, vector_sums = closing(
        dp, mp, span, one_grad, two_sums,
        (d_mix_pre, xn, x_low, normed_part, d_inputs), shared_part, vector_sums,
        (keep, weight, gain, omega, ffn_part), starts,
    )
    up_grad = two_grad[:, : up_proj.shape[1]].astype(jnp.float32)
    down_grad = two_grad[:, up_proj.shape[1] :].astype(jnp.float32)
    base = 2 * (wide + narrow)
    value_grad = one_grad[:, :wide].astype(jnp.float32)
    gate_grad = one_grad[:, wide : 2 * wide].astype(jnp.float32)
    mixer_grad = one_grad[:, 2 * wide : 2 * wide + narrow].astype(jnp.float32)
    update_grad = one_grad[:, 2 * wide + narrow : base].astype(jnp.float32)
    output_grad = jnp.concatenate(
        [one_grad[:wide, base:], one_grad[wide:, base:]], axis=1
    ).astype(jnp.float32)

    shared_grad = shared_grad.astype(jnp.float32)
    query_grad, bias_grad, key_grad = vector_sums[0], vector_sums[1], vector_sums[2]
    delta, alpha, beta, eta = (
        item.T for item in (ema_delta, ema_alpha, ema_beta, ema_eta)
    )
    rate = jax.nn.sigmoid(delta)
    damp = jax.nn.sigmoid(alpha)
    weight_sum = feature[:NDIM]
    keep_sum = feature[NDIM : 2 * NDIM] * (rate * beta * eta)
    d_rate = weight_sum * beta * eta - keep_sum * damp
    delta_grad = (d_rate * rate * (1.0 - rate)).T
    alpha_grad = (-keep_sum * rate * damp * (1.0 - damp)).T
    beta_grad = (weight_sum * rate * eta).T
    eta_grad = (weight_sum * rate * beta).T
    omega_grad, gain_grad, ffn_grad = feature[2 * NDIM], feature[2 * NDIM + 1], feature[2 * NDIM + 2]
    return (
        layer_out, token_grad, gain_grad, delta_grad, alpha_grad, beta_grad, eta_grad, omega_grad,
        shared_grad, query_grad, bias_grad, key_grad, value_grad, gate_grad, mixer_grad,
        update_grad, output_grad, ffn_grad, up_grad, down_grad,
    )


def solution(mesh):
    dp, mp = mesh.shape["dp"], mesh.shape["mp"]
    params = (
        P("mp"), P("mp", None), P("mp", None), P("mp", None), P("mp", None), P("mp"),
        P(), P(), P(), P(),
        P(None, "mp"), P(None, "mp"), P(None, "mp"), P(None, "mp"), P("mp", None),
        P("mp"), P(None, "mp"), P("mp", None),
    )
    specs = (P("dp", "mp"), P("dp", "mp")) + params
    return jax.shard_map(
        functools.partial(local, dp, mp), mesh=mesh, in_specs=specs, out_specs=specs, check_vma=False
    )
```
